32 devices in a mesh: dp: 4 (over x, core), head: 4 (over z), expert: 2 (over y).
Axes of the slice: x: 2, y: 2, z: 4, core: 2. Of those that a mesh axis runs over, the one named last changes fastest.
Arguments:
- tokens: bfloat16 [4, 64, 4096], P('dp', ('head', 'expert')), may hold values from -6 to 6
- cotangent: bfloat16 [4, 64, 4096], P('dp', ('head', 'expert')), may hold values from -1.5 to 1.5
- queries: bfloat16 [4, 64, 32, 128], P('dp', 'expert', 'head'), may hold values from -32 to 32
- key_vectors: bfloat16 [4, 64, 32, 128], P('dp', 'expert', 'head'), may hold values from -32 to 32
- value_routes: int32 [4, 32, 64, 1], P('dp', 'head'), may hold values from 0 to 3; in each aligned block of 8 rows (0 to 7, 8 to 15, ..., all dimensions but the last counted through in order) at most 3 rows name the same one
- output_routes: int32 [4, 32, 64, 1], P('dp', 'head'), may hold values from 0 to 3; in each aligned block of 8 rows (0 to 7, 8 to 15, ..., all dimensions but the last counted through in order) at most 3 rows name the same one
- value_experts: bfloat16 [128, 4096, 128], P(('head', 'expert')), may hold values from -0.09375 to 0.09375
- output_experts: bfloat16 [128, 4096, 128], P(('head', 'expert')), may hold values from -0.09375 to 0.09375
Outputs:
- token_grads: bfloat16 [4, 64, 4096], P('dp', ('head', 'expert'))
- query_grads: bfloat16 [4, 64, 32, 128], P('dp', 'expert', 'head')
- key_grads: bfloat16 [4, 64, 32, 128], P('dp', 'expert', 'head')
- value_grads: bfloat16 [128, 4096, 128], P(('head', 'expert'), 'dp')
- output_grads: bfloat16 [128, 4096, 128], P(('head', 'expert'), 'dp')
The draws below stay inside these ranges and needn't reach their ends.
Inputs may be any that keep to these rules, and one draw needn't show every extreme that they name: value_routes[b, h, t, 0] is the value expert of head h for token t. In each aligned block of 8 tokens of one sequence and head, no expert is chosen more than 3 times, and in every draw some block has exactly 3 for one expert. output_routes[b, h, t, 0] is the output expert of head h for token t. In each aligned block of 8 tokens of one sequence and head, no expert is chosen more than 3 times, and in every draw some block has exactly 3 for one expert.
All inputs are finite; a program needn't handle non-finite values.
Results may differ from the reference program's by a relative error of at most 0.028.
Values may be sent and summed in bfloat16 or wider, within the bound.
A program may use at most 128 MiB of HBM per device.

```python
import math
import jax
import jax.numpy as jnp
import numpy as np
from jax import lax

D = 4096
H = 32
HD = 128
E = 4
TOK_DEV = 8
CAP = 3
SEQ = 64
B = 4


def attention_draw(key):
    folded = jax.random.fold_in(key, 4409)
    subkeys = jax.random.split(folded, 4)
    full_shape = (B, SEQ, H, HD)
    query_raw = jnp.clip(jax.random.normal(subkeys[0], full_shape, jnp.float32), -4.0, 4.0)
    key_raw = jnp.clip(jax.random.normal(subkeys[1], full_shape, jnp.float32), -4.0, 4.0)
    query_scale = jnp.exp(jax.random.uniform(subkeys[2], (B, SEQ, H, 1), jnp.float32, math.log(0.15), math.log(1.5)))
    key_scale = jnp.exp(jax.random.uniform(subkeys[3], (B, SEQ, H, 1), jnp.float32, math.log(0.3), math.log(3.0)))
    query_field = query_raw * query_scale
    key_field = key_raw * key_scale
    return (jnp.clip(query_field, -32.0, 32.0), jnp.clip(key_field, -32.0, 32.0))


def draw_queries(key, part):
    return attention_draw(key)[0].astype(jnp.bfloat16)


def draw_key_vectors(key, part):
    return attention_draw(key)[1].astype(jnp.bfloat16)


def block_scale(own_key, dims, cuts, least, high):
    def one(axis_at, parts):
        steps = jax.random.uniform(jax.random.fold_in(jax.random.fold_in(own_key, 6), axis_at), (parts,), jnp.float32, least / len(cuts), high / len(cuts))
        return jnp.repeat(jnp.exp(steps), dims[axis_at] // parts).reshape((-1,) + (1,) * (len(dims) - axis_at - 1))

    level = one(*cuts[0])
    for cut in cuts[1:]:
        level = level * one(*cut)
    return level


def routed_block(own_key, own, number, rows, count, top, most, skew):
    order = jax.random.permutation(own_key, count)
    crowded, common = shares(count, rows * top, most, skew, True), shares(count, rows * top, most, skew, False)
    places = jnp.arange(count)

    def named(lengths, turn):
        used = int((lengths > 0).sum())
        fixed = max(1, used // 4)
        shifted = fixed + (places - fixed + turn * (used - fixed)) % max(1, count - fixed)
        return jnp.zeros((count,), jnp.int32).at[order[jnp.where(places < fixed, places, shifted)]].set(jnp.asarray(lengths, jnp.int32))

    lengths = jnp.where(number % 4 == 0, named(crowded, number // 4), named(common, number - number // 4 - 1))
    mixed = jax.random.permutation(jax.random.fold_in(own, 3), count)
    giver, sink = mixed[0:count // 2 * 2:2], mixed[1:count // 2 * 2:2]
    room = jnp.minimum(lengths[giver] - 1, most - lengths[sink]) // 2
    room = jnp.where((giver == order[0]) | (sink == order[0]) | (lengths[sink] == 0), 0, jnp.maximum(room, 0))
    shifted = jax.random.randint(jax.random.fold_in(own, 4), (count // 2,), 0, 1 << 20) % (room + 1)
    lengths = lengths.at[giver].add(-shifted).at[sink].add(shifted)
    labels = jnp.searchsorted(jnp.cumsum(lengths), jnp.arange(rows * top), side="right").astype(jnp.int32)
    grid = labels.reshape(top, rows).T
    grid = grid[jax.random.permutation(jax.random.fold_in(own, 1), rows)]
    turn = jax.random.randint(jax.random.fold_in(own, 2), (rows, 1), 0, top)
    return jnp.take_along_axis(grid, (jnp.arange(top)[None, :] + turn) % top, axis=1)


def shares(number_of, total, limit, skew, full):
    portions = [(1 << 20) // math.isqrt(rank ** skew) + 1 for rank in range(1, number_of + 1)]
    largest = limit if full else min(limit, max(-(-total // number_of), total * portions[0] // sum(portions)))
    least = 1 if total - largest >= number_of - 1 else 0
    given, spare = [largest] + [least] * (number_of - 1), total - largest - least * (number_of - 1)
    while spare > 0:
        candidates = [i for i in range(1, number_of) if given[i] < largest] or [i for i in range(1, number_of) if given[i] < limit]
        whole, budget = sum([portions[i] for i in candidates]), spare
        for i in candidates:
            extra = min(limit - given[i], max(1, budget * portions[i] // whole), spare)
            given[i] = given[i] + extra
            spare = spare - extra
    return np.array(given)


def centred(stream_key, shape, width, bound, pieces=(), held_as=jnp.bfloat16):
    gain = block_scale(stream_key, shape, pieces, -0.22, 0.18) if pieces else 1.0
    result = jax.random.normal(stream_key, shape, jnp.float32) * width * gain
    return jnp.minimum(jnp.maximum(result, -bound), bound).astype(held_as)


def setup_inputs(seed: int = 0) -> dict:
    seeds = jax.random.split(jax.random.key(seed), 9)
    tokens = centred(seeds[0], (B, SEQ, D), 1.0, 6.0, ((0, 4), (1, 8)))
    cotangent = centred(seeds[1], (B, SEQ, D), 0.25, 1.5, ((0, 4), (1, 8)))
    queries = draw_queries(jax.random.fold_in(seeds[8], 71), 0)
    key_vectors = draw_key_vectors(jax.random.fold_in(seeds[8], 71), 0)
    value_routes_keys = jax.random.split(jax.random.fold_in(seeds[4], 1), B * H * SEQ // TOK_DEV)
    value_routes_turns = jax.random.permutation(jax.random.fold_in(seeds[4], 3), B * H * SEQ // TOK_DEV)
    value_routes = jax.vmap(lambda own, number: routed_block(jax.random.fold_in(seeds[4], 2), own, number, TOK_DEV, E, 1, CAP, 2))(value_routes_keys, value_routes_turns).reshape((B, H, SEQ, 1))
    output_routes_keys = jax.random.split(jax.random.fold_in(seeds[5], 1), B * H * SEQ // TOK_DEV)
    output_routes_turns = jax.random.permutation(jax.random.fold_in(seeds[5], 3), B * H * SEQ // TOK_DEV)
    output_routes = jax.vmap(lambda own, number: routed_block(jax.random.fold_in(seeds[5], 2), own, number, TOK_DEV, E, 1, CAP, 2))(output_routes_keys, output_routes_turns).reshape((B, H, SEQ, 1))
    value_experts = centred(seeds[6], (H * E, D, HD), D ** -0.5, 0.09375, ((0, 8),))
    output_experts = centred(seeds[7], (H * E, D, HD), D ** -0.5, 0.09375, ((0, 8),))
    return dict(tokens=tokens, cotangent=cotangent, queries=queries, key_vectors=key_vectors, value_routes=value_routes, output_routes=output_routes, value_experts=value_experts, output_experts=output_experts)


def reference(tokens, cotangent, queries, key_vectors, value_routes, output_routes, value_experts, output_experts):
    score_scale = HD ** (-0.5)
    value_weight = value_experts.astype(jnp.float32).reshape(H, E, D, HD)
    output_weight = output_experts.astype(jnp.float32).reshape(H, E, D, HD)
    expert_ids = jnp.arange(E, dtype=jnp.int32)
    positions = jnp.arange(SEQ, dtype=jnp.int32)
    causal = positions[None, :] <= positions[:, None]

    def sequence_step(running, inputs):
        value_sum, output_sum = running
        token_seq, cotangent_seq, query_seq, key_seq, value_seq_routes, output_seq_routes = inputs
        value_pick = (value_seq_routes[:, :, 0, None] == expert_ids).astype(jnp.float32)
        output_pick = (output_seq_routes[:, :, 0, None] == expert_ids).astype(jnp.float32)
        token_float = token_seq.astype(jnp.float32)
        cotangent_float = cotangent_seq.astype(jnp.float32)
        every_value = jnp.einsum('td,hedc->thec', token_float, value_weight)
        values = jnp.einsum('thec,hte->thc', every_value, value_pick).astype(jnp.bfloat16)
        every_upstream = jnp.einsum('td,hedc->thec', cotangent_float, output_weight)
        upstream = jnp.einsum('thec,hte->thc', every_upstream, output_pick).astype(jnp.bfloat16)
        query_float = query_seq.astype(jnp.float32)
        key_float = key_seq.astype(jnp.float32)
        scores = jnp.einsum('ihc,jhc->hij', query_float, key_float) * score_scale
        row_top = jnp.max(jnp.where(causal, scores, -jnp.inf), axis=-1, keepdims=True)
        weights = jnp.where(causal, jnp.exp(scores - row_top), 0.0)
        probs = weights / jnp.sum(weights, axis=-1, keepdims=True)
        prob_half = lax.optimization_barrier(probs.astype(jnp.bfloat16)).astype(jnp.float32)
        value_float = values.astype(jnp.float32)
        upstream_float = upstream.astype(jnp.float32)
        outputs = jnp.einsum('hij,jhc->ihc', prob_half, value_float).astype(jnp.bfloat16)
        output_float = outputs.astype(jnp.float32)
        row_delta = jnp.sum(output_float * upstream_float, axis=-1)
        prob_grads = jnp.einsum('ihc,jhc->hij', upstream_float, value_float)
        score_grads = probs * (prob_grads - row_delta.T[:, :, None])
        score_half = lax.optimization_barrier(score_grads.astype(jnp.bfloat16)).astype(jnp.float32)
        query_grads = (jnp.einsum('hij,jhc->ihc', score_half, key_float) * score_scale).astype(jnp.bfloat16)
        key_grads = (jnp.einsum('hij,ihc->jhc', score_half, query_float) * score_scale).astype(jnp.bfloat16)
        value_half = jnp.einsum('hij,ihc->jhc', prob_half, upstream_float).astype(jnp.bfloat16)
        value_half_float = value_half.astype(jnp.float32)
        value_masked = jnp.transpose(value_pick, (1, 0, 2))[..., None] * value_half_float[:, :, None, :]
        value_term = jnp.einsum('td,thec->hedc', token_float, value_masked).astype(jnp.bfloat16)
        output_masked = jnp.transpose(output_pick, (1, 0, 2))[..., None] * output_float[:, :, None, :]
        output_term = jnp.einsum('td,thec->hedc', cotangent_float, output_masked).astype(jnp.bfloat16)
        value_sum = value_sum + lax.optimization_barrier(value_term).astype(jnp.float32)
        output_sum = output_sum + lax.optimization_barrier(output_term).astype(jnp.float32)

        def head_step(running_sum, head_pos):
            masked = value_pick[head_pos][:, :, None] * value_half_float[:, head_pos][:, None, :]
            head_term = jnp.einsum('tec,edc->td', masked, value_weight[head_pos]).astype(jnp.bfloat16)
            return (running_sum + lax.optimization_barrier(head_term).astype(jnp.float32), None)
        token_total, _ = lax.scan(head_step, jnp.zeros((SEQ, D), jnp.float32), jnp.arange(H, dtype=jnp.int32))
        return ((value_sum, output_sum), (token_total.astype(jnp.bfloat16), query_grads, key_grads))
    zeros = jnp.zeros((H, E, D, HD), jnp.float32)
    sums, stacked = lax.scan(sequence_step, (zeros, zeros), (tokens, cotangent, queries, key_vectors, value_routes, output_routes))
    value_grads = sums[0].reshape(H * E, D, HD).astype(jnp.bfloat16)
    output_grads = sums[1].reshape(H * E, D, HD).astype(jnp.bfloat16)
    return (stacked[0], stacked[1], stacked[2], value_grads, output_grads)
```

```python
import functools

import jax
import jax.numpy as jnp
from jax import lax
from jax.experimental import pallas as pl
from jax.experimental.pallas import tpu as pltpu
from jax.sharding import PartitionSpec as P

E = 4
CAP = 3


def slot_rank(routes):
    places = jnp.arange(routes.shape[-1], dtype=jnp.int32)
    same = routes[..., :, None] == routes[..., None, :]
    return jnp.sum(jnp.logical_and(same, places[None, :] < places[:, None]).astype(jnp.int32), axis=-1)


def slot_table(routes):
    rank_of = slot_rank(routes)
    expert_hit = routes[..., None, None, :] == jnp.arange(E, dtype=jnp.int32)[:, None, None]
    place_hit = rank_of[..., None, None, :] == jnp.arange(CAP, dtype=jnp.int32)[:, None]
    return jnp.logical_and(expert_hit, place_hit).astype(jnp.bfloat16)


def local(
    tokens,
    cotangent,
    queries,
    key_vectors,
    value_routes,
    output_routes,
    value_experts,
    output_experts,
):
    head_count = lax.axis_size("head")
    expert_count = lax.axis_size("expert")
    sources = head_count * expert_count
    expert_index = lax.axis_index("expert")
    tok_rows = tokens.shape[1]
    model_width = tokens.shape[2]
    query_rows = queries.shape[1]
    groups = queries.shape[2]
    head_dim = queries.shape[3]
    seq_len = value_routes.shape[2]
    pairs_dev = value_experts.shape[0]
    slot_count = sources * CAP
    score_scale = head_dim ** (-0.5)
    value_local = value_routes[0, :, :, 0]
    output_local = output_routes[0, :, :, 0]

    def own_block(route_part):
        shaped = route_part.reshape(groups, head_count, expert_count, tok_rows)
        return lax.dynamic_index_in_dim(shaped, expert_index, 2, keepdims=False)

    own_pair = jnp.stack([own_block(value_local), own_block(output_local)])
    own_routes = lax.all_to_all(own_pair, "head", split_axis=2, concat_axis=1, tiled=True).reshape(
        2, groups * head_count, tok_rows
    )
    value_table = slot_table(own_routes[0]).reshape(
        head_count, expert_count, pairs_dev, CAP, tok_rows
    )

    def pair_rows(route_part, gathered):
        slot_map = slot_table(route_part.reshape(groups, sources, tok_rows))
        slot_map = jnp.moveaxis(slot_map, 2, 1).reshape(groups * E, sources, CAP, tok_rows)
        slot_map = lax.dynamic_slice_in_dim(slot_map, expert_index * pairs_dev, pairs_dev, 0)
        picked = jnp.einsum(
            "psmt,stw->psmw",
            slot_map,
            gathered.reshape(sources, tok_rows, model_width),
            preferred_element_type=jnp.float32,
        )
        return picked.astype(jnp.bfloat16).reshape(pairs_dev, slot_count, model_width)

    whole_tokens, whole_cotangent = (
        lax.all_gather(tokens[0], ("head", "expert"), axis=0, tiled=True),
        lax.all_gather(cotangent[0], ("head", "expert"), axis=0, tiled=True),
    )
    token_slots = pair_rows(value_local, whole_tokens)
    cotangent_slots = pair_rows(output_local, whole_cotangent)
    value_slots = jnp.einsum(
        "prw,pwk->prk", token_slots, value_experts, preferred_element_type=jnp.float32
    ).astype(jnp.bfloat16)
    upstream_slots = jnp.einsum(
        "prw,pwk->prk", cotangent_slots, output_experts, preferred_element_type=jnp.float32
    ).astype(jnp.bfloat16)
    query_start = expert_index * query_rows
    group_values, group_upstream, all_keys = (
        lax.all_gather(value_slots, "expert", axis=0, tiled=True),
        lax.all_gather(upstream_slots, "expert", axis=0, tiled=True),
        lax.all_gather(key_vectors[0], "expert", axis=0, tiled=True),
    )
    token_source = jnp.arange(seq_len, dtype=jnp.int32) // tok_rows
    head_base = jnp.arange(groups, dtype=jnp.int32)[:, None] * E
    value_rank = slot_rank(value_local.reshape(groups, sources, tok_rows)).reshape(groups, seq_len)
    value_index = (head_base + value_local) * slot_count + token_source * CAP + value_rank
    value_rows = group_values.reshape(-1, head_dim)[value_index]
    output_rank = slot_rank(output_local.reshape(groups, sources, tok_rows)).reshape(
        groups, seq_len
    )
    block_routes = lax.dynamic_slice_in_dim(output_local, query_start, query_rows, 1)
    block_rank = lax.dynamic_slice_in_dim(output_rank, query_start, query_rows, 1)
    block_source = lax.dynamic_slice_in_dim(token_source, query_start, query_rows, 0)
    upstream_index = (head_base + block_routes) * slot_count + block_source * CAP + block_rank
    upstream_rows = group_upstream.reshape(-1, head_dim)[upstream_index]
    query_own = queries[0]
    scores = (
        jnp.einsum("ihc,jhc->hij", query_own, all_keys, preferred_element_type=jnp.float32)
        * score_scale
    )
    query_pos = query_start + jnp.arange(query_rows, dtype=jnp.int32)
    causal = jnp.arange(seq_len, dtype=jnp.int32)[None, :] <= query_pos[:, None]
    row_top = jnp.max(jnp.where(causal, scores, -jnp.inf), axis=-1, keepdims=True)
    weights = jnp.where(causal, jnp.exp(scores - row_top), 0.0)
    probs_full = weights / jnp.sum(weights, axis=-1, keepdims=True)
    prob_half = probs_full.astype(jnp.bfloat16)
    outputs = jnp.einsum(
        "hij,hjc->hic", prob_half, value_rows, preferred_element_type=jnp.float32
    ).astype(jnp.bfloat16)
    row_delta = jnp.sum(outputs.astype(jnp.float32) * upstream_rows.astype(jnp.float32), axis=-1)
    prob_grads = jnp.einsum(
        "hic,hjc->hij", upstream_rows, value_rows, preferred_element_type=jnp.float32
    )
    score_grads = (probs_full * (prob_grads - row_delta[:, :, None])).astype(jnp.bfloat16)
    query_grads = (
        jnp.einsum("hij,jhc->ihc", score_grads, all_keys, preferred_element_type=jnp.float32)
        * score_scale
    ).astype(jnp.bfloat16)
    key_part = (
        jnp.einsum("hij,ihc->jhc", score_grads, query_own, preferred_element_type=jnp.float32)
        * score_scale
    )
    value_part = jnp.einsum(
        "hij,hic->jhc", prob_half, upstream_rows, preferred_element_type=jnp.float32
    )
    key_sum, value_sum = (
        lax.psum_scatter(key_part, "expert", scatter_dimension=0, tiled=True),
        lax.psum_scatter(value_part, "expert", scatter_dimension=0, tiled=True),
    )
    value_half = value_sum.astype(jnp.bfloat16)
    block_value_routes = lax.dynamic_slice_in_dim(value_local, query_start, query_rows, 1).reshape(
        groups, head_count, tok_rows
    )
    value_place = slot_table(block_value_routes)
    output_place = slot_table(block_routes.reshape(groups, head_count, tok_rows))
    value_send = jnp.einsum(
        "hsemt,sthc->hesmc",
        value_place,
        value_half.reshape(head_count, tok_rows, groups, head_dim),
        preferred_element_type=jnp.float32,
    )
    value_send = value_send.astype(jnp.bfloat16).reshape(groups * E, head_count * CAP, head_dim)
    output_send = jnp.einsum(
        "hsemt,hstc->hesmc",
        output_place,
        outputs.reshape(groups, head_count, tok_rows, head_dim),
        preferred_element_type=jnp.float32,
    )
    output_send = output_send.astype(jnp.bfloat16).reshape(groups * E, head_count * CAP, head_dim)
    output_slots, grad_slots = (
        lax.all_to_all(output_send, "expert", split_axis=0, concat_axis=1, tiled=True),
        lax.all_to_all(value_send, "expert", split_axis=0, concat_axis=1, tiled=True),
    )
    value_term = jnp.einsum(
        "prw,prk->pwk", token_slots, grad_slots, preferred_element_type=jnp.float32
    )
    output_term = jnp.einsum(
        "prw,prk->pwk", cotangent_slots, output_slots, preferred_element_type=jnp.float32
    )
    value_grads, output_grads = (
        lax.psum_scatter(
            value_term.astype(jnp.bfloat16), "dp", scatter_dimension=1, tiled=True
        ).astype(jnp.float32),
        lax.psum_scatter(
            output_term.astype(jnp.bfloat16), "dp", scatter_dimension=1, tiled=True
        ).astype(jnp.float32),
    )
    token_terms = jnp.einsum(
        "prk,pwk->prw", grad_slots, value_experts, preferred_element_type=jnp.float32
    ).astype(jnp.bfloat16)
    returned = lax.all_to_all(
        token_terms.reshape(pairs_dev, sources, CAP, model_width),
        ("head", "expert"),
        split_axis=1,
        concat_axis=0,
        tiled=True,
    )
    returned = returned.reshape(head_count, expert_count, pairs_dev, CAP, model_width)
    token_grads = jnp.einsum(
        "gjpmt,gjpmw->tw", value_table, returned, preferred_element_type=jnp.float32
    )
    return (
        token_grads.astype(jnp.bfloat16)[None],
        query_grads[None],
        key_sum.astype(jnp.bfloat16)[None],
        value_grads.astype(jnp.bfloat16),
        output_grads.astype(jnp.bfloat16),
    )


def fused_kernel(
    sizes,
    tok,
    cot,
    q_in,
    k_in,
    value_routes_in,
    output_routes_in,
    value_hbm,
    output_hbm,
    tok_out,
    qg_out,
    kg_out,
    vg_out,
    og_out,
    rows,
    flat,
    flat_t,
    heads_raw,
    by_heads,
    routes,
    route_columns,
    weight,
    heads_in,
    part,
    part_in,
    factor,
    masked,
    score_keep,
    prob_keep,
    upstream_keep,
    back,
    back_in,
    term,
    term_in,
    sem_weight,
    sem_own,
    sem_rows,
    sem_routes,
    sem_line,
    sem_side,
    sem_heads,
    sem_part,
    sem_factor,
    sem_back,
    sem_term,
):
    dn, gn, jn, own_heads, query_rows, tok_rows, width, head_dim = sizes
    sources = gn * jn
    seq_len = sources * tok_rows
    scale = head_dim ** (-0.5)
    d, g, j = lax.axis_index("dp"), lax.axis_index("head"), lax.axis_index("expert")
    block = g * jn + j
    f32, bf16 = jnp.float32, jnp.bfloat16

    def at(dd, gg, jj):
        return {"dp": lax.rem(d + dd, dn), "head": lax.rem(g + gg, gn), "expert": lax.rem(j + jj, jn)}

    others = [
        (dd, gg, jj)
        for dd in range(dn)
        for gg in range(gn)
        for jj in range(jn)
        if (dd, gg, jj) != (0, 0, 0)
    ]
    sent = []

    def send(src, dst, sems, slot, where):
        copy = pltpu.make_async_remote_copy(
            src_ref=src,
            dst_ref=dst,
            send_sem=sems.at[(0,) + slot],
            recv_sem=sems.at[(1,) + slot],
            device_id=at(*where),
            device_id_type=pl.DeviceIdType.MESH,
        )
        copy.start()
        sent.append(copy)
        return copy

    def columns(index):
        return pl.ds(pl.multiple_of(index * width, 128), width)

    weights_on_way = [
        pltpu.make_async_copy(hbm.at[:, columns(d), :], weight.at[i], sem_weight.at[i])
        for i, hbm in enumerate((value_hbm, output_hbm))
    ]
    own = [
        pltpu.make_async_copy(tok.at[:, columns(d)], rows.at[block, 0, d], sem_own.at[0]),
        pltpu.make_async_copy(cot.at[:, columns(d)], rows.at[block, 1, d], sem_own.at[1]),
        pltpu.make_async_copy(
            value_routes_in.at[pl.ds(j * own_heads, own_heads)],
            routes.at[d, pl.ds(0, own_heads)],
            sem_own.at[2],
        ),
        pltpu.make_async_copy(
            output_routes_in.at[pl.ds(j * own_heads, own_heads)],
            routes.at[d, pl.ds(own_heads, own_heads)],
            sem_own.at[3],
        ),
        pltpu.make_async_copy(q_in, heads_raw.at[0], sem_own.at[4]),
        pltpu.make_async_copy(k_in, heads_raw.at[1], sem_own.at[5]),
    ]
    for copy in own:
        copy.start()

    barrier = pltpu.get_barrier_semaphore()
    for where in others:
        pl.semaphore_signal(
            barrier, inc=1, device_id=at(*where), device_id_type=pl.DeviceIdType.MESH
        )
    pl.semaphore_wait(barrier, len(others))

    first, late, line, side = [[], []], [], [[], []], [[], []]
    for i in (1, 0):
        for dd in range(1, dn):
            target = columns(lax.rem(d + dd, dn))
            source = (tok, cot)[i]
            first[i].append(
                send(source.at[:, target], rows.at[block, i, d], sem_rows, (dd, i), (dd, 0, 0))
            )
    for copy in weights_on_way:
        copy.start()
    for copy in own:
        copy.wait()
    late = [
        send(routes.at[d], routes.at[d], sem_routes, (dd,), (dd, 0, 0)) for dd in range(1, dn)
    ]
    for i in (1, 0):
        for copy in first[i]:
            copy.wait_recv()
        here = rows.at[block, i]
        for gg in range(1, gn):
            line[i].append(send(here, here, sem_line, (gg, i), (0, gg, 0)))
        for jj in range(1, jn):
            side[i].append(send(here, here, sem_side, (0, jj, i), (0, 0, jj)))
    for i in range(2):
        turned = jnp.transpose(heads_raw[i].astype(f32), (1, 0, 2)).astype(bf16)
        for jj in range(jn):
            by_heads[i, jj] = turned[jj * own_heads : (jj + 1) * own_heads]
        heads_in[i, j] = by_heads[i, j]
    swapped = []
    for jj in range(1, jn):
        peer = lax.rem(j + jj, jn)
        for i in range(2):
            swapped.append(
                send(by_heads.at[i, peer], heads_in.at[i, j], sem_heads, (i, jj), (0, 0, jj))
            )

    def forward(i):
        for gg in range(1, gn):
            line[i][gg - 1].wait_recv()
            came = rows.at[lax.rem(g + gn - gg, gn) * jn + j, i]
            for jj in range(1, jn):
                side[i].append(send(came, came, sem_side, (gg, jj, i), (0, 0, jj)))

    def flatten(i):
        for copy in side[i]:
            copy.wait_recv()
        for b in range(dn):
            piece = jnp.concatenate([rows[s, i, b].astype(f32) for s in range(sources)], axis=0)
            flat[i, b * seq_len : (b + 1) * seq_len, :] = piece.astype(bf16)

    def column(i, h, b):
        c = i * own_heads + h
        return jnp.broadcast_to(route_columns[b, :seq_len, c : c + 1], (seq_len, head_dim))

    def turn_routes(b):
        lines = jnp.concatenate([routes[b, c] for c in range(2 * own_heads)], axis=0)
        spare = route_columns.shape[1] - seq_len
        if spare:
            lines = jnp.concatenate([lines, jnp.zeros((2 * own_heads, spare), jnp.int32)], axis=1)
        route_columns[b] = lines.T

    def project(i):
        weights_on_way[i].wait()
        for h in range(own_heads):
            picked = [jnp.zeros((seq_len, head_dim), f32) for _ in range(dn)]
            for e in range(0, E, 2):
                p = h * E + e
                both = jnp.concatenate([weight[i, p], weight[i, p + 1]], axis=1)
                every = jnp.dot(flat[i], both, preferred_element_type=f32)
                for b in range(dn):
                    own_rows = every[b * seq_len : (b + 1) * seq_len]
                    route = column(i, h, b)
                    picked[b] = jnp.where(route == e, own_rows[:, :head_dim], picked[b])
                    picked[b] = jnp.where(route == e + 1, own_rows[:, head_dim:], picked[b])
            for b in range(dn):
                part[b, i, h] = picked[b].astype(bf16)
        return [
            send(
                part.at[lax.rem(d + dd, dn), i], part_in.at[dd, i], sem_part, (dd, i), (dd, 0, 0)
            )
            for dd in range(1, dn)
        ]

    forward(1)
    flatten(1)
    for copy in late:
        copy.wait_recv()
    for b in range(dn):
        turn_routes(b)
    upstream_on_way = project(1)
    forward(0)

    query_pos = lax.broadcasted_iota(jnp.int32, (seq_len, seq_len), 0)
    key_pos = lax.broadcasted_iota(jnp.int32, (seq_len, seq_len), 1)
    causal = key_pos <= query_pos

    def joined(i, h):
        return jnp.concatenate([heads_in[i, jj, h] for jj in range(jn)], axis=0)

    def total(i, h):
        whole = part[d, i, h].astype(f32)
        for dd in range(1, dn):
            whole = whole + part_in[dd, i, h].astype(f32)
        return whole.astype(bf16)

    def across(a, b):
        return lax.dot_general(a, b, (((1,), (1,)), ((), ())), preferred_element_type=f32)

    def over_rows(a, b):
        return lax.dot_general(a, b, (((0,), (0,)), ((), ())), preferred_element_type=f32)

    def mask(i):
        for h in range(own_heads):
            for b in range(dn):
                source = factor[b, i, h].astype(f32)
                route = column(i, h, b)
                for e in range(E):
                    p = h * E + e
                    masked[
                        i,
                        p // 2,
                        b * seq_len : (b + 1) * seq_len,
                        (p % 2) * head_dim : (p % 2 + 1) * head_dim,
                    ] = jnp.where(route == e, source, 0.0).astype(bf16)

    def spread(i):
        return [
            send(factor.at[d, i], factor.at[d, i], sem_factor, (dd, i), (dd, 0, 0))
            for dd in range(1, dn)
        ]

    for copy in swapped:
        copy.wait_recv()
    for h in range(own_heads):
        query, key = joined(0, h), joined(1, h)
        scores = across(query, key) * scale
        top = jnp.max(jnp.where(causal, scores, -jnp.inf), axis=-1, keepdims=True)
        soft = jnp.where(causal, jnp.exp(scores - top), 0.0)
        prob_keep[h] = soft / jnp.sum(soft, axis=-1, keepdims=True)
    for copy in upstream_on_way:
        copy.wait_recv()
    for h in range(own_heads):
        upstream_keep[h] = total(1, h)
        factor[d, 0, h] = over_rows(prob_keep[h].astype(bf16), upstream_keep[h]).astype(bf16)
    value_spread = spread(0)
    flatten(0)
    values_on_way = project(0)
    for copy in value_spread:
        copy.wait_recv()
    mask(0)
    couples = own_heads * E // 2
    step = min(width, 256)
    for n in range(0, width, step):
        added = jnp.zeros((dn * seq_len, step), f32)
        for c in range(couples):
            both = jnp.concatenate(
                [weight[0, 2 * c, n : n + step, :], weight[0, 2 * c + 1, n : n + step, :]], axis=1
            )
            added = added + across(masked[0, c], both)
        for r in range(dn * sources):
            term[r, :, n : n + step] = added[r * tok_rows : (r + 1) * tok_rows].astype(bf16)
    terms = []
    for slot, (dd, gg, jj) in enumerate(others):
        target = (
            lax.rem(d + dd, dn) * sources + lax.rem(g + gg, gn) * jn + lax.rem(j + jj, jn)
        )
        terms.append(
            send(term.at[target], term_in.at[d * sources + block], sem_term, (slot,), (dd, gg, jj))
        )
    term_in[d * sources + block] = term[d * sources + block]

    for copy in values_on_way:
        copy.wait_recv()
    for h in range(own_heads):
        value, upstream, probs = total(0, h), upstream_keep[h], prob_keep[h]
        output = jnp.dot(probs.astype(bf16), value, preferred_element_type=f32).astype(bf16)
        factor[d, 1, h] = output
        delta = jnp.sum(output.astype(f32) * upstream.astype(f32), axis=-1, keepdims=True)
        score_keep[h] = (probs * (across(upstream, value) - delta)).astype(bf16)
    output_spread = spread(1)
    for h in range(own_heads):
        query, key, score = joined(0, h), joined(1, h), score_keep[h]
        query_grad = (jnp.dot(score, key, preferred_element_type=f32) * scale).astype(bf16)
        key_grad = (over_rows(score, query) * scale).astype(bf16)
        for jj in range(jn):
            back[jj, 0, h] = query_grad[jj * query_rows : (jj + 1) * query_rows]
            back[jj, 1, h] = key_grad[jj * query_rows : (jj + 1) * query_rows]
    returned = [
        send(back.at[lax.rem(j + jj, jn)], back_in.at[j], sem_back, (jj,), (0, 0, jj))
        for jj in range(1, jn)
    ]

    def gradients(i, out):
        flat_t[i] = flat[i].T
        for c in range(couples):
            whole = jnp.dot(flat_t[i], masked[i, c], preferred_element_type=f32)
            out[2 * c] = whole[:, :head_dim].astype(bf16)
            out[2 * c + 1] = whole[:, head_dim:].astype(bf16)

    gradients(0, vg_out)
    for copy in output_spread:
        copy.wait_recv()
    mask(1)
    gradients(1, og_out)

    back_in[j] = back[j]
    for copy in returned:
        copy.wait_recv()
    for jj in range(jn):
        qg_out[jj] = back_in[jj, 0]
        kg_out[jj] = back_in[jj, 1]
    for copy in terms:
        copy.wait_recv()
    for b in range(dn):
        total_rows = term_in[b * sources].astype(f32)
        for s in range(1, sources):
            total_rows = total_rows + term_in[b * sources + s].astype(f32)
        tok_out[:, b * width : (b + 1) * width] = total_rows.astype(bf16)
    for copy in sent:
        copy.wait_send()


def finish_kernel(
    tok_in, qg_in, kg_in, vg_in, og_in, tok_out, qg_out, kg_out, vg_out, og_out, turned, sems
):
    pieces = sems.shape[1]
    size = vg_in.shape[0] // (pieces - 1)
    copies = [pltpu.make_async_copy(tok_in, tok_out, sems.at[0, pieces - 1])]
    for i, (source, out) in enumerate(((vg_in, vg_out), (og_in, og_out))):
        for n in range(pieces - 1):
            part = pl.ds(n * size, size)
            copies.append(pltpu.make_async_copy(source.at[part], out.at[part], sems.at[i, n]))
    for copy in copies:
        copy.start()
    late = []
    for i, (source, out) in enumerate(((qg_in, qg_out), (kg_in, kg_out))):
        turned[i] = jnp.transpose(source[...].astype(jnp.float32), (1, 0, 2)).astype(out.dtype)
        late.append(pltpu.make_async_copy(turned.at[i], out, sems.at[2, i]))
        late[i].start()
    for copy in copies + late:
        copy.wait()


def fused(
    tokens,
    cotangent,
    queries,
    key_vectors,
    value_routes,
    output_routes,
    value_experts,
    output_experts,
):
    dn, gn, jn = lax.axis_size("dp"), lax.axis_size("head"), lax.axis_size("expert")
    _, tok_rows, model_width = tokens.shape
    width = model_width // dn
    _, query_rows, groups, head_dim = queries.shape
    seq_len = value_routes.shape[2]
    pairs_dev = value_experts.shape[0]
    own_heads = groups // jn
    sources = gn * jn
    bf16 = jnp.bfloat16

    value_lines = value_routes.reshape(groups, 1, seq_len)
    output_lines = output_routes.reshape(groups, 1, seq_len)

    vmem = pl.BlockSpec(memory_space=pltpu.VMEM)
    hbm = pl.BlockSpec(memory_space=pl.ANY)
    dma = pltpu.SemaphoreType.DMA
    head_block = (jn, own_heads, query_rows, head_dim)
    grad_shape = jax.ShapeDtypeStruct((pairs_dev, width, head_dim), bf16)
    tok_grads, query_grads, key_grads, value_grads, output_grads = pl.pallas_call(
        functools.partial(
            fused_kernel, (dn, gn, jn, own_heads, query_rows, tok_rows, width, head_dim)
        ),
        name="fused",
        out_shape=(
            pltpu.VMEM((tok_rows, model_width), bf16),
            pltpu.VMEM(head_block, bf16),
            pltpu.VMEM(head_block, bf16),
            pltpu.VMEM(grad_shape.shape, bf16),
            pltpu.VMEM(grad_shape.shape, bf16),
        ),
        in_specs=[hbm] * 8,
        out_specs=(vmem,) * 5,
        scratch_shapes=[
            pltpu.VMEM((sources, 2, dn, tok_rows, width), bf16),
            pltpu.VMEM((2, dn * seq_len, width), bf16),
            pltpu.VMEM((2, width, dn * seq_len), bf16),
            pltpu.VMEM((2, query_rows, groups, head_dim), bf16),
            pltpu.VMEM((2, jn, own_heads, query_rows, head_dim), bf16),
            pltpu.VMEM((dn, 2 * own_heads, 1, seq_len), jnp.int32),
            pltpu.VMEM((dn, -(-seq_len // 128) * 128, 2 * own_heads), jnp.int32),
            pltpu.VMEM((2, pairs_dev, width, head_dim), bf16),
            pltpu.VMEM((2, jn, own_heads, query_rows, head_dim), bf16),
            pltpu.VMEM((dn, 2, own_heads, seq_len, head_dim), bf16),
            pltpu.VMEM((dn, 2, own_heads, seq_len, head_dim), bf16),
            pltpu.VMEM((dn, 2, own_heads, seq_len, head_dim), bf16),
            pltpu.VMEM((2, pairs_dev // 2, dn * seq_len, 2 * head_dim), bf16),
            pltpu.VMEM((own_heads, seq_len, seq_len), bf16),
            pltpu.VMEM((own_heads, seq_len, seq_len), jnp.float32),
            pltpu.VMEM((own_heads, seq_len, head_dim), bf16),
            pltpu.VMEM((jn, 2, own_heads, query_rows, head_dim), bf16),
            pltpu.VMEM((jn, 2, own_heads, query_rows, head_dim), bf16),
            pltpu.VMEM((dn * sources, tok_rows, width), bf16),
            pltpu.VMEM((dn * sources, tok_rows, width), bf16),
            dma((2,)),
            dma((6,)),
            dma((2, dn, 2)),
            dma((2, dn)),
            dma((2, gn, 2)),
            dma((2, gn, jn, 2)),
            dma((2, 2, jn)),
            dma((2, dn, 2)),
            dma((2, dn, 2)),
            dma((2, jn)),
            dma((2, dn * sources)),
        ],
        compiler_params=pltpu.CompilerParams(
            collective_id=0, has_side_effects=True, vmem_limit_bytes=40 * 1024 * 1024
        ),
    )(
        *(
            pltpu.with_memory_space_constraint(x, pltpu.HBM)
            for x in (
                tokens[0],
                cotangent[0],
                queries[0],
                key_vectors[0],
                value_lines,
                output_lines,
            )
        ),
        value_experts,
        output_experts,
    )

    by_head = (groups, query_rows, head_dim)
    row_shape = jax.ShapeDtypeStruct((query_rows, groups, head_dim), bf16)
    tok_grads, query_grads, key_grads, value_grads, output_grads = pl.pallas_call(
        finish_kernel,
        name="finish",
        out_shape=(
            jax.ShapeDtypeStruct((tok_rows, model_width), bf16),
            row_shape,
            row_shape,
            grad_shape,
            grad_shape,
        ),
        in_specs=[vmem] * 5,
        out_specs=(hbm,) * 5,
        scratch_shapes=[
            pltpu.VMEM((2, query_rows, groups, head_dim), bf16),
            dma((3, E + 1)),
        ],
        compiler_params=pltpu.CompilerParams(vmem_limit_bytes=8 * 1024 * 1024),
    )(
        tok_grads,
        query_grads.reshape(by_head),
        key_grads.reshape(by_head),
        value_grads,
        output_grads,
    )
    return tok_grads[None], query_grads[None], key_grads[None], value_grads, output_grads


def chosen(*args):
    groups, pairs_dev = args[2].shape[2], args[6].shape[0]
    dp_count, expert_count = lax.axis_size("dp"), lax.axis_size("expert")
    whole_heads = groups % expert_count == 0 and pairs_dev == groups // expert_count * E
    if whole_heads and args[0].shape[2] % (dp_count * 256) == 0 and args[2].shape[1] <= 64:
        return fused(*args)
    return local(*args)


def solution(mesh):
    return jax.shard_map(
        chosen,
        mesh=mesh,
        in_specs=(
            P("dp", ("head", "expert"), None),
            P("dp", ("head", "expert"), None),
            P("dp", "expert", "head", None),
            P("dp", "expert", "head", None),
            P("dp", "head", None, None),
            P("dp", "head", None, None),
            P(("head", "expert"), None, None),
            P(("head", "expert"), None, None),
        ),
        out_specs=(
            P("dp", ("head", "expert"), None),
            P("dp", "expert", "head", None),
            P("dp", "expert", "head", None),
            P(("head", "expert"), "dp", None),
            P(("head", "expert"), "dp", None),
        ),
        check_vma=False,
    )
```

```python
import functools

import jax
import jax.numpy as jnp
from jax import lax
from jax.experimental import pallas as pl
from jax.experimental.pallas import tpu as pltpu
from jax.sharding import PartitionSpec as P

E = 4
CAP = 3


def slot_rank(routes):
    places = jnp.arange(routes.shape[-1], dtype=jnp.int32)
    same = routes[..., :, None] == routes[..., None, :]
    return jnp.sum(jnp.logical_and(same, places[None, :] < places[:, None]).astype(jnp.int32), axis=-1)


def slot_table(routes):
    rank_of = slot_rank(routes)
    expert_hit = routes[..., None, None, :] == jnp.arange(E, dtype=jnp.int32)[:, None, None]
    place_hit = rank_of[..., None, None, :] == jnp.arange(CAP, dtype=jnp.int32)[:, None]
    return jnp.logical_and(expert_hit, place_hit).astype(jnp.bfloat16)


def local(
    tokens,
    cotangent,
    queries,
    key_vectors,
    value_routes,
    output_routes,
    value_experts,
    output_experts,
):
    head_count = lax.axis_size("head")
    expert_count = lax.axis_size("expert")
    sources = head_count * expert_count
    expert_index = lax.axis_index("expert")
    tok_rows = tokens.shape[1]
    model_width = tokens.shape[2]
    query_rows = queries.shape[1]
    groups = queries.shape[2]
    head_dim = queries.shape[3]
    seq_len = value_routes.shape[2]
    pairs_dev = value_experts.shape[0]
    slot_count = sources * CAP
    score_scale = head_dim ** (-0.5)
    value_local = value_routes[0, :, :, 0]
    output_local = output_routes[0, :, :, 0]

    def own_block(route_part):
        shaped = route_part.reshape(groups, head_count, expert_count, tok_rows)
        return lax.dynamic_index_in_dim(shaped, expert_index, 2, keepdims=False)

    own_pair = jnp.stack([own_block(value_local), own_block(output_local)])
    own_routes = lax.all_to_all(own_pair, "head", split_axis=2, concat_axis=1, tiled=True).reshape(
        2, groups * head_count, tok_rows
    )
    value_table = slot_table(own_routes[0]).reshape(
        head_count, expert_count, pairs_dev, CAP, tok_rows
    )

    def pair_rows(route_part, gathered):
        slot_map = slot_table(route_part.reshape(groups, sources, tok_rows))
        slot_map = jnp.moveaxis(slot_map, 2, 1).reshape(groups * E, sources, CAP, tok_rows)
        slot_map = lax.dynamic_slice_in_dim(slot_map, expert_index * pairs_dev, pairs_dev, 0)
        picked = jnp.einsum(
            "psmt,stw->psmw",
            slot_map,
            gathered.reshape(sources, tok_rows, model_width),
            preferred_element_type=jnp.float32,
        )
        return picked.astype(jnp.bfloat16).reshape(pairs_dev, slot_count, model_width)

    whole_tokens, whole_cotangent = (
        lax.all_gather(tokens[0], ("head", "expert"), axis=0, tiled=True),
        lax.all_gather(cotangent[0], ("head", "expert"), axis=0, tiled=True),
    )
    token_slots = pair_rows(value_local, whole_tokens)
    cotangent_slots = pair_rows(output_local, whole_cotangent)
    value_slots = jnp.einsum(
        "prw,pwk->prk", token_slots, value_experts, preferred_element_type=jnp.float32
    ).astype(jnp.bfloat16)
    upstream_slots = jnp.einsum(
        "prw,pwk->prk", cotangent_slots, output_experts, preferred_element_type=jnp.float32
    ).astype(jnp.bfloat16)
    query_start = expert_index * query_rows
    group_values, group_upstream, all_keys = (
        lax.all_gather(value_slots, "expert", axis=0, tiled=True),
        lax.all_gather(upstream_slots, "expert", axis=0, tiled=True),
        lax.all_gather(key_vectors[0], "expert", axis=0, tiled=True),
    )
    token_source = jnp.arange(seq_len, dtype=jnp.int32) // tok_rows
    head_base = jnp.arange(groups, dtype=jnp.int32)[:, None] * E
    value_rank = slot_rank(value_local.reshape(groups, sources, tok_rows)).reshape(groups, seq_len)
    value_index = (head_base + value_local) * slot_count + token_source * CAP + value_rank
    value_rows = group_values.reshape(-1, head_dim)[value_index]
    output_rank = slot_rank(output_local.reshape(groups, sources, tok_rows)).reshape(
        groups, seq_len
    )
    block_routes = lax.dynamic_slice_in_dim(output_local, query_start, query_rows, 1)
    block_rank = lax.dynamic_slice_in_dim(output_rank, query_start, query_rows, 1)
    block_source = lax.dynamic_slice_in_dim(token_source, query_start, query_rows, 0)
    upstream_index = (head_base + block_routes) * slot_count + block_source * CAP + block_rank
    upstream_rows = group_upstream.reshape(-1, head_dim)[upstream_index]
    query_own = queries[0]
    scores = (
        jnp.einsum("ihc,jhc->hij", query_own, all_keys, preferred_element_type=jnp.float32)
        * score_scale
    )
    query_pos = query_start + jnp.arange(query_rows, dtype=jnp.int32)
    causal = jnp.arange(seq_len, dtype=jnp.int32)[None, :] <= query_pos[:, None]
    row_top = jnp.max(jnp.where(causal, scores, -jnp.inf), axis=-1, keepdims=True)
    weights = jnp.where(causal, jnp.exp(scores - row_top), 0.0)
    probs_full = weights / jnp.sum(weights, axis=-1, keepdims=True)
    prob_half = probs_full.astype(jnp.bfloat16)
    outputs = jnp.einsum(
        "hij,hjc->hic", prob_half, value_rows, preferred_element_type=jnp.float32
    ).astype(jnp.bfloat16)
    row_delta = jnp.sum(outputs.astype(jnp.float32) * upstream_rows.astype(jnp.float32), axis=-1)
    prob_grads = jnp.einsum(
        "hic,hjc->hij", upstream_rows, value_rows, preferred_element_type=jnp.float32
    )
    score_grads = (probs_full * (prob_grads - row_delta[:, :, None])).astype(jnp.bfloat16)
    query_grads = (
        jnp.einsum("hij,jhc->ihc", score_grads, all_keys, preferred_element_type=jnp.float32)
        * score_scale
    ).astype(jnp.bfloat16)
    key_part = (
        jnp.einsum("hij,ihc->jhc", score_grads, query_own, preferred_element_type=jnp.float32)
        * score_scale
    )
    value_part = jnp.einsum(
        "hij,hic->jhc", prob_half, upstream_rows, preferred_element_type=jnp.float32
    )
    key_sum, value_sum = (
        lax.psum_scatter(key_part, "expert", scatter_dimension=0, tiled=True),
        lax.psum_scatter(value_part, "expert", scatter_dimension=0, tiled=True),
    )
    value_half = value_sum.astype(jnp.bfloat16)
    block_value_routes = lax.dynamic_slice_in_dim(value_local, query_start, query_rows, 1).reshape(
        groups, head_count, tok_rows
    )
    value_place = slot_table(block_value_routes)
    output_place = slot_table(block_routes.reshape(groups, head_count, tok_rows))
    value_send = jnp.einsum(
        "hsemt,sthc->hesmc",
        value_place,
        value_half.reshape(head_count, tok_rows, groups, head_dim),
        preferred_element_type=jnp.float32,
    )
    value_send = value_send.astype(jnp.bfloat16).reshape(groups * E, head_count * CAP, head_dim)
    output_send = jnp.einsum(
        "hsemt,hstc->hesmc",
        output_place,
        outputs.reshape(groups, head_count, tok_rows, head_dim),
        preferred_element_type=jnp.float32,
    )
    output_send = output_send.astype(jnp.bfloat16).reshape(groups * E, head_count * CAP, head_dim)
    output_slots, grad_slots = (
        lax.all_to_all(output_send, "expert", split_axis=0, concat_axis=1, tiled=True),
        lax.all_to_all(value_send, "expert", split_axis=0, concat_axis=1, tiled=True),
    )
    value_term = jnp.einsum(
        "prw,prk->pwk", token_slots, grad_slots, preferred_element_type=jnp.float32
    )
    output_term = jnp.einsum(
        "prw,prk->pwk", cotangent_slots, output_slots, preferred_element_type=jnp.float32
    )
    value_grads, output_grads = (
        lax.psum_scatter(
            value_term.astype(jnp.bfloat16), "dp", scatter_dimension=1, tiled=True
        ).astype(jnp.float32),
        lax.psum_scatter(
            output_term.astype(jnp.bfloat16), "dp", scatter_dimension=1, tiled=True
        ).astype(jnp.float32),
    )
    token_terms = jnp.einsum(
        "prk,pwk->prw", grad_slots, value_experts, preferred_element_type=jnp.float32
    ).astype(jnp.bfloat16)
    returned = lax.all_to_all(
        token_terms.reshape(pairs_dev, sources, CAP, model_width),
        ("head", "expert"),
        split_axis=1,
        concat_axis=0,
        tiled=True,
    )
    returned = returned.reshape(head_count, expert_count, pairs_dev, CAP, model_width)
    token_grads = jnp.einsum(
        "gjpmt,gjpmw->tw", value_table, returned, preferred_element_type=jnp.float32
    )
    return (
        token_grads.astype(jnp.bfloat16)[None],
        query_grads[None],
        key_sum.astype(jnp.bfloat16)[None],
        value_grads.astype(jnp.bfloat16),
        output_grads.astype(jnp.bfloat16),
    )


def fused_kernel(
    sizes,
    tok,
    cot,
    q_in,
    k_in,
    value_routes_in,
    output_routes_in,
    value_hbm,
    output_hbm,
    tok_out,
    qg_out,
    kg_out,
    vg_out,
    og_out,
    rows,
    flat,
    flat_t,
    heads_raw,
    by_heads,
    routes,
    route_columns,
    weight,
    heads_in,
    part,
    part_in,
    factor,
    masked,
    score_keep,
    prob_keep,
    upstream_keep,
    back,
    back_in,
    term,
    term_side,
    term_sum,
    term_in,
    own_rows,
    sem_weight,
    sem_own,
    sem_piece,
    sem_block,
    sem_routes,
    sem_side,
    sem_heads,
    sem_part,
    sem_factor,
    sem_back,
    sem_half,
    sem_term,
):
    dn, gn, jn, own_heads, query_rows, tok_rows, width, head_dim = sizes
    sources = gn * jn
    seq_len = sources * tok_rows
    scale = head_dim ** (-0.5)
    d, g, j = lax.axis_index("dp"), lax.axis_index("head"), lax.axis_index("expert")
    block = g * jn + j
    f32, bf16 = jnp.float32, jnp.bfloat16

    def at(dd, gg, jj):
        return {"dp": lax.rem(d + dd, dn), "head": lax.rem(g + gg, gn), "expert": lax.rem(j + jj, jn)}

    others = [(dd, gg) for gg in range(gn) for dd in range(dn) if (dd, gg) != (0, 0)]
    sent = []

    def send(src, dst, sems, slot, where):
        copy = pltpu.make_async_remote_copy(
            src_ref=src,
            dst_ref=dst,
            send_sem=sems.at[(0,) + slot],
            recv_sem=sems.at[(1,) + slot],
            device_id=at(*where),
            device_id_type=pl.DeviceIdType.MESH,
        )
        copy.start()
        sent.append(copy)
        return copy

    def columns(index):
        return pl.ds(pl.multiple_of(index * width, 128), width)

    weights_on_way = [
        pltpu.make_async_copy(hbm.at[:, columns(d), :], weight.at[i], sem_weight.at[i])
        for i, hbm in enumerate((value_hbm, output_hbm))
    ]
    own = [
        pltpu.make_async_copy(tok, own_rows.at[0], sem_own.at[0]),
        pltpu.make_async_copy(cot, own_rows.at[1], sem_own.at[1]),
        pltpu.make_async_copy(tok.at[:, columns(d)], rows.at[block, 0, d], sem_own.at[2]),
        pltpu.make_async_copy(cot.at[:, columns(d)], rows.at[block, 1, d], sem_own.at[3]),
        pltpu.make_async_copy(
            value_routes_in.at[pl.ds(j * own_heads, own_heads)],
            routes.at[d, pl.ds(0, own_heads)],
            sem_own.at[4],
        ),
        pltpu.make_async_copy(
            output_routes_in.at[pl.ds(j * own_heads, own_heads)],
            routes.at[d, pl.ds(own_heads, own_heads)],
            sem_own.at[5],
        ),
        pltpu.make_async_copy(q_in, heads_raw.at[0], sem_own.at[6]),
        pltpu.make_async_copy(k_in, heads_raw.at[1], sem_own.at[7]),
    ]
    for copy in own:
        copy.start()

    barrier = pltpu.get_barrier_semaphore()

    def greet(where):
        pl.semaphore_signal(
            barrier, inc=1, device_id=at(*where), device_id_type=pl.DeviceIdType.MESH
        )

    for dd, gg in others:
        greet((dd, gg, 0))
    for jj in range(1, jn):
        greet((0, 0, jj))
    for copy in own:
        copy.wait()
    pl.semaphore_wait(barrier, len(others) + jn - 1)

    def share(i):
        for dd, gg in others:
            copy = pltpu.make_async_remote_copy(
                src_ref=own_rows.at[i, :, columns(lax.rem(d + dd, dn))],
                dst_ref=rows.at[block, i, d],
                send_sem=sem_piece.at[dd, gg, i],
                recv_sem=sem_block.at[g, i],
                device_id=at(dd, gg, 0),
                device_id_type=pl.DeviceIdType.MESH,
            )
            copy.start()
            sent.append(copy)

    def side(source, jj, i):
        block_rows = rows.at[source * jn + j, i]
        return pltpu.make_async_remote_copy(
            src_ref=block_rows,
            dst_ref=block_rows,
            send_sem=sem_side.at[0, source, jj, i],
            recv_sem=sem_side.at[1, source, jj, i],
            device_id=at(0, 0, jj),
            device_id_type=pl.DeviceIdType.MESH,
        )

    def relay(i, nearest):
        for k in range(gn):
            order = sorted(range(gn), key=lambda t: (abs(t - k), t))

            @pl.when(g == k)
            def _(k=k, order=order):
                for source in order[nearest]:
                    count = dn - 1 if source == k else dn
                    if count:
                        came = rows.at[source * jn + j, i, pl.ds(0, count)]
                        pltpu.make_async_remote_copy(
                            src_ref=came,
                            dst_ref=came,
                            send_sem=sem_piece.at[0, 0, i],
                            recv_sem=sem_block.at[source, i],
                            device_id=at(0, 0, 0),
                            device_id_type=pl.DeviceIdType.MESH,
                        ).wait_recv()
                    for jj in range(1, jn):
                        side(source, jj, i).start()

    near, far = slice(0, gn // 2), slice(gn // 2, gn)
    share(1)
    late = [
        send(routes.at[d], routes.at[d], sem_routes, (dd,), (dd, 0, 0)) for dd in range(1, dn)
    ]
    for i in range(2):
        turned = jnp.transpose(heads_raw[i].astype(f32), (1, 0, 2)).astype(bf16)
        for jj in range(jn):
            by_heads[i, jj] = turned[jj * own_heads : (jj + 1) * own_heads]
        heads_in[i, j] = by_heads[i, j]
    swapped = []
    for jj in range(1, jn):
        peer = lax.rem(j + jj, jn)
        for i in range(2):
            swapped.append(
                send(by_heads.at[i, peer], heads_in.at[i, j], sem_heads, (i, jj), (0, 0, jj))
            )

    for copy in weights_on_way:
        copy.start()
    relay(1, near)
    share(0)
    relay(1, far)

    def flatten(i):
        for source in range(gn):
            for jj in range(1, jn):
                side(source, jj, i).wait_recv()
        for b in range(dn):
            piece = jnp.concatenate([rows[s, i, b].astype(f32) for s in range(sources)], axis=0)
            flat[i, b * seq_len : (b + 1) * seq_len, :] = piece.astype(bf16)

    def column(i, h, b):
        c = i * own_heads + h
        return jnp.broadcast_to(route_columns[b, :seq_len, c : c + 1], (seq_len, head_dim))

    def turn_routes(b):
        lines = jnp.concatenate([routes[b, c] for c in range(2 * own_heads)], axis=0)
        spare = route_columns.shape[1] - seq_len
        if spare:
            lines = jnp.concatenate([lines, jnp.zeros((2 * own_heads, spare), jnp.int32)], axis=1)
        route_columns[b] = lines.T

    def project(i):
        weights_on_way[i].wait()
        for h in range(own_heads):
            picked = [jnp.zeros((seq_len, head_dim), f32) for _ in range(dn)]
            for e in range(0, E, 2):
                p = h * E + e
                both = jnp.concatenate([weight[i, p], weight[i, p + 1]], axis=1)
                every = jnp.dot(flat[i], both, preferred_element_type=f32)
                for b in range(dn):
                    own_rows = every[b * seq_len : (b + 1) * seq_len]
                    route = column(i, h, b)
                    picked[b] = jnp.where(route == e, own_rows[:, :head_dim], picked[b])
                    picked[b] = jnp.where(route == e + 1, own_rows[:, head_dim:], picked[b])
            for b in range(dn):
                part[b, i, h] = picked[b].astype(bf16)
        return [
            send(
                part.at[lax.rem(d + dd, dn), i], part_in.at[dd, i], sem_part, (dd, i), (dd, 0, 0)
            )
            for dd in range(1, dn)
        ]

    query_pos = lax.broadcasted_iota(jnp.int32, (seq_len, seq_len), 0)
    key_pos = lax.broadcasted_iota(jnp.int32, (seq_len, seq_len), 1)
    causal = key_pos <= query_pos

    def joined(i, h):
        return jnp.concatenate([heads_in[i, jj, h] for jj in range(jn)], axis=0)

    def total(i, h):
        whole = part[d, i, h].astype(f32)
        for dd in range(1, dn):
            whole = whole + part_in[dd, i, h].astype(f32)
        return whole.astype(bf16)

    def across(a, b):
        return lax.dot_general(a, b, (((1,), (1,)), ((), ())), preferred_element_type=f32)

    def over_rows(a, b):
        return lax.dot_general(a, b, (((0,), (0,)), ((), ())), preferred_element_type=f32)

    def mask(i):
        for h in range(own_heads):
            for b in range(dn):
                source = factor[b, i, h].astype(f32)
                route = column(i, h, b)
                for e in range(E):
                    p = h * E + e
                    masked[
                        i,
                        p // 2,
                        b * seq_len : (b + 1) * seq_len,
                        (p % 2) * head_dim : (p % 2 + 1) * head_dim,
                    ] = jnp.where(route == e, source, 0.0).astype(bf16)

    def spread(i):
        return [
            send(factor.at[d, i], factor.at[d, i], sem_factor, (dd, i), (dd, 0, 0))
            for dd in range(1, dn)
        ]

    for copy in swapped:
        copy.wait_recv()
    for h in range(own_heads):
        query, key = joined(0, h), joined(1, h)
        scores = across(query, key) * scale
        top = jnp.max(jnp.where(causal, scores, -jnp.inf), axis=-1, keepdims=True)
        soft = jnp.where(causal, jnp.exp(scores - top), 0.0)
        prob_keep[h] = soft / jnp.sum(soft, axis=-1, keepdims=True)
    for copy in late:
        copy.wait_recv()
    for b in range(dn):
        turn_routes(b)
    relay(0, near)
    flatten(1)
    upstream_on_way = project(1)
    relay(0, far)
    for copy in upstream_on_way:
        copy.wait_recv()
    for h in range(own_heads):
        upstream_keep[h] = total(1, h)
        factor[d, 0, h] = over_rows(prob_keep[h].astype(bf16), upstream_keep[h]).astype(bf16)
    value_spread = spread(0)
    flatten(0)
    values_on_way = project(0)
    for copy in value_spread:
        copy.wait_recv()
    mask(0)
    couples = own_heads * E // 2
    step = min(width, 256)
    for n in range(0, width, step):
        added = jnp.zeros((dn * seq_len, step), f32)
        for c in range(couples):
            both = jnp.concatenate(
                [weight[0, 2 * c, n : n + step, :], weight[0, 2 * c + 1, n : n + step, :]], axis=1
            )
            added = added + across(masked[0, c], both)
        for b in range(dn):
            for r in range(sources):
                first = (b * sources + r) * tok_rows
                term[r % jn, r // jn, b, :, n : n + step] = added[first : first + tok_rows].astype(
                    bf16
                )
    halves = {}
    onward = list(range(1, gn)) + [0]
    for gg in onward:
        target = lax.rem(g + gg, gn)
        for jj in range(1, jn):
            peer = lax.rem(j + jj, jn)
            halves[gg, jj] = send(
                term.at[peer, target], term_side.at[jj, gg], sem_half, (gg, jj), (0, 0, jj)
            )

    for copy in values_on_way:
        copy.wait_recv()
    for h in range(own_heads):
        value, upstream, probs = total(0, h), upstream_keep[h], prob_keep[h]
        output = jnp.dot(probs.astype(bf16), value, preferred_element_type=f32).astype(bf16)
        factor[d, 1, h] = output
        delta = jnp.sum(output.astype(f32) * upstream.astype(f32), axis=-1, keepdims=True)
        score_keep[h] = (probs * (across(upstream, value) - delta)).astype(bf16)
    output_spread = spread(1)
    for h in range(own_heads):
        query, key, score = joined(0, h), joined(1, h), score_keep[h]
        query_grad = (jnp.dot(score, key, preferred_element_type=f32) * scale).astype(bf16)
        key_grad = (over_rows(score, query) * scale).astype(bf16)
        for jj in range(jn):
            back[jj, 0, h] = query_grad[jj * query_rows : (jj + 1) * query_rows]
            back[jj, 1, h] = key_grad[jj * query_rows : (jj + 1) * query_rows]
    returned = [
        send(back.at[lax.rem(j + jj, jn)], back_in.at[j], sem_back, (jj,), (0, 0, jj))
        for jj in range(1, jn)
    ]

    def gradients(i, out):
        flat_t[i] = flat[i].T
        for c in range(couples):
            whole = jnp.dot(flat_t[i], masked[i, c], preferred_element_type=f32)
            out[2 * c] = whole[:, :head_dim].astype(bf16)
            out[2 * c + 1] = whole[:, head_dim:].astype(bf16)

    gradients(0, vg_out)
    terms = []
    for gg in onward:
        target = lax.rem(g + gg, gn)
        whole = term[j, target].astype(f32)
        for jj in range(1, jn):
            halves[gg, jj].wait_recv()
            whole = whole + term_side[jj, gg].astype(f32)
        term_sum[gg] = whole.astype(bf16)
        for dd in range(dn):
            if (dd, gg) == (0, 0):
                term_in[g, d] = term_sum[gg, d]
            else:
                terms.append(
                    send(
                        term_sum.at[gg, lax.rem(d + dd, dn)],
                        term_in.at[g, d],
                        sem_term,
                        (dd, gg),
                        (dd, gg, 0),
                    )
                )
    for copy in output_spread:
        copy.wait_recv()
    mask(1)
    gradients(1, og_out)

    back_in[j] = back[j]
    for copy in returned:
        copy.wait_recv()
    for jj in range(jn):
        qg_out[jj] = back_in[jj, 0]
        kg_out[jj] = back_in[jj, 1]
    for copy in terms:
        copy.wait_recv()
    for b in range(dn):
        total_rows = term_in[0, b].astype(f32)
        for s in range(1, gn):
            total_rows = total_rows + term_in[s, b].astype(f32)
        tok_out[:, b * width : (b + 1) * width] = total_rows.astype(bf16)
    for copy in sent:
        copy.wait_send()
    for source in range(gn):
        for jj in range(1, jn):
            for i in range(2):
                side(source, jj, i).wait_send()


def finish_kernel(
    tok_in, qg_in, kg_in, vg_in, og_in, tok_out, qg_out, kg_out, vg_out, og_out, turned, sems
):
    pieces = sems.shape[1]
    size = vg_in.shape[0] // (pieces - 1)
    copies = [pltpu.make_async_copy(tok_in, tok_out, sems.at[0, pieces - 1])]
    for i, (source, out) in enumerate(((vg_in, vg_out), (og_in, og_out))):
        for n in range(pieces - 1):
            part = pl.ds(n * size, size)
            copies.append(pltpu.make_async_copy(source.at[part], out.at[part], sems.at[i, n]))
    for copy in copies:
        copy.start()
    late = []
    for i, (source, out) in enumerate(((qg_in, qg_out), (kg_in, kg_out))):
        turned[i] = jnp.transpose(source[...].astype(jnp.float32), (1, 0, 2)).astype(out.dtype)
        late.append(pltpu.make_async_copy(turned.at[i], out, sems.at[2, i]))
        late[i].start()
    for copy in copies + late:
        copy.wait()


def fused(
    tokens,
    cotangent,
    queries,
    key_vectors,
    value_routes,
    output_routes,
    value_experts,
    output_experts,
):
    dn, gn, jn = lax.axis_size("dp"), lax.axis_size("head"), lax.axis_size("expert")
    _, tok_rows, model_width = tokens.shape
    width = model_width // dn
    _, query_rows, groups, head_dim = queries.shape
    seq_len = value_routes.shape[2]
    pairs_dev = value_experts.shape[0]
    own_heads = groups // jn
    sources = gn * jn
    bf16 = jnp.bfloat16

    value_lines = value_routes.reshape(groups, 1, seq_len)
    output_lines = output_routes.reshape(groups, 1, seq_len)

    vmem = pl.BlockSpec(memory_space=pltpu.VMEM)
    hbm = pl.BlockSpec(memory_space=pl.ANY)
    dma = pltpu.SemaphoreType.DMA
    head_block = (jn, own_heads, query_rows, head_dim)
    grad_shape = jax.ShapeDtypeStruct((pairs_dev, width, head_dim), bf16)
    tok_grads, query_grads, key_grads, value_grads, output_grads = pl.pallas_call(
        functools.partial(
            fused_kernel, (dn, gn, jn, own_heads, query_rows, tok_rows, width, head_dim)
        ),
        name="fused",
        out_shape=(
            pltpu.VMEM((tok_rows, model_width), bf16),
            pltpu.VMEM(head_block, bf16),
            pltpu.VMEM(head_block, bf16),
            pltpu.VMEM(grad_shape.shape, bf16),
            pltpu.VMEM(grad_shape.shape, bf16),
        ),
        in_specs=[hbm] * 8,
        out_specs=(vmem,) * 5,
        scratch_shapes=[
            pltpu.VMEM((sources, 2, dn, tok_rows, width), bf16),
            pltpu.VMEM((2, dn * seq_len, width), bf16),
            pltpu.VMEM((2, width, dn * seq_len), bf16),
            pltpu.VMEM((2, query_rows, groups, head_dim), bf16),
            pltpu.VMEM((2, jn, own_heads, query_rows, head_dim), bf16),
            pltpu.VMEM((dn, 2 * own_heads, 1, seq_len), jnp.int32),
            pltpu.VMEM((dn, -(-seq_len // 128) * 128, 2 * own_heads), jnp.int32),
            pltpu.VMEM((2, pairs_dev, width, head_dim), bf16),
            pltpu.VMEM((2, jn, own_heads, query_rows, head_dim), bf16),
            pltpu.VMEM((dn, 2, own_heads, seq_len, head_dim), bf16),
            pltpu.VMEM((dn, 2, own_heads, seq_len, head_dim), bf16),
            pltpu.VMEM((dn, 2, own_heads, seq_len, head_dim), bf16),
            pltpu.VMEM((2, pairs_dev // 2, dn * seq_len, 2 * head_dim), bf16),
            pltpu.VMEM((own_heads, seq_len, seq_len), bf16),
            pltpu.VMEM((own_heads, seq_len, seq_len), jnp.float32),
            pltpu.VMEM((own_heads, seq_len, head_dim), bf16),
            pltpu.VMEM((jn, 2, own_heads, query_rows, head_dim), bf16),
            pltpu.VMEM((jn, 2, own_heads, query_rows, head_dim), bf16),
            pltpu.VMEM((jn, gn, dn, tok_rows, width), bf16),
            pltpu.VMEM((jn, gn, dn, tok_rows, width), bf16),
            pltpu.VMEM((gn, dn, tok_rows, width), bf16),
            pltpu.VMEM((gn, dn, tok_rows, width), bf16),
            pltpu.VMEM((2, tok_rows, model_width), bf16),
            dma((2,)),
            dma((8,)),
            dma((dn, gn, 2)),
            dma((gn, 2)),
            dma((2, dn)),
            dma((2, gn, jn, 2)),
            dma((2, 2, jn)),
            dma((2, dn, 2)),
            dma((2, dn, 2)),
            dma((2, jn)),
            dma((2, gn, jn)),
            dma((2, dn, gn)),
        ],
        compiler_params=pltpu.CompilerParams(
            collective_id=0, has_side_effects=True, vmem_limit_bytes=40 * 1024 * 1024
        ),
    )(
        *(
            pltpu.with_memory_space_constraint(x, pltpu.HBM)
            for x in (
                tokens[0],
                cotangent[0],
                queries[0],
                key_vectors[0],
                value_lines,
                output_lines,
            )
        ),
        value_experts,
        output_experts,
    )

    by_head = (groups, query_rows, head_dim)
    row_shape = jax.ShapeDtypeStruct((query_rows, groups, head_dim), bf16)
    tok_grads, query_grads, key_grads, value_grads, output_grads = pl.pallas_call(
        finish_kernel,
        name="finish",
        out_shape=(
            jax.ShapeDtypeStruct((tok_rows, model_width), bf16),
            row_shape,
            row_shape,
            grad_shape,
            grad_shape,
        ),
        in_specs=[vmem] * 5,
        out_specs=(hbm,) * 5,
        scratch_shapes=[
            pltpu.VMEM((2, query_rows, groups, head_dim), bf16),
            dma((3, E + 1)),
        ],
        compiler_params=pltpu.CompilerParams(vmem_limit_bytes=8 * 1024 * 1024),
    )(
        tok_grads,
        query_grads.reshape(by_head),
        key_grads.reshape(by_head),
        value_grads,
        output_grads,
    )
    return tok_grads[None], query_grads[None], key_grads[None], value_grads, output_grads


def chosen(*args):
    groups, pairs_dev = args[2].shape[2], args[6].shape[0]
    dp_count, expert_count = lax.axis_size("dp"), lax.axis_size("expert")
    whole_heads = groups % expert_count == 0 and pairs_dev == groups // expert_count * E
    small = args[4].shape[2] <= 128
    if whole_heads and small and args[0].shape[2] % (dp_count * 256) == 0:
        return fused(*args)
    return local(*args)


def solution(mesh):
    return jax.shard_map(
        chosen,
        mesh=mesh,
        in_specs=(
            P("dp", ("head", "expert"), None),
            P("dp", ("head", "expert"), None),
            P("dp", "expert", "head", None),
            P("dp", "expert", "head", None),
            P("dp", "head", None, None),
            P("dp", "head", None, None),
            P(("head", "expert"), None, None),
            P(("head", "expert"), None, None),
        ),
        out_specs=(
            P("dp", ("head", "expert"), None),
            P("dp", "expert", "head", None),
            P("dp", "expert", "head", None),
            P(("head", "expert"), "dp", None),
            P(("head", "expert"), "dp", None),
        ),
        check_vma=False,
    )
```

```python
import functools

import jax
import jax.numpy as jnp
from jax import lax
from jax.experimental import pallas as pl
from jax.experimental.pallas import tpu as pltpu
from jax.sharding import PartitionSpec as P

E = 4
CAP = 3


def slot_rank(routes):
    places = jnp.arange(routes.shape[-1], dtype=jnp.int32)
    same = routes[..., :, None] == routes[..., None, :]
    return jnp.sum(jnp.logical_and(same, places[None, :] < places[:, None]).astype(jnp.int32), axis=-1)


def slot_table(routes):
    rank_of = slot_rank(routes)
    expert_hit = routes[..., None, None, :] == jnp.arange(E, dtype=jnp.int32)[:, None, None]
    place_hit = rank_of[..., None, None, :] == jnp.arange(CAP, dtype=jnp.int32)[:, None]
    return jnp.logical_and(expert_hit, place_hit).astype(jnp.bfloat16)


def local(
    tokens,
    cotangent,
    queries,
    key_vectors,
    value_routes,
    output_routes,
    value_experts,
    output_experts,
):
    head_count = lax.axis_size("head")
    expert_count = lax.axis_size("expert")
    sources = head_count * expert_count
    expert_index = lax.axis_index("expert")
    tok_rows = tokens.shape[1]
    model_width = tokens.shape[2]
    query_rows = queries.shape[1]
    groups = queries.shape[2]
    head_dim = queries.shape[3]
    seq_len = value_routes.shape[2]
    pairs_dev = value_experts.shape[0]
    slot_count = sources * CAP
    score_scale = head_dim ** (-0.5)
    value_local = value_routes[0, :, :, 0]
    output_local = output_routes[0, :, :, 0]

    def own_block(route_part):
        shaped = route_part.reshape(groups, head_count, expert_count, tok_rows)
        return lax.dynamic_index_in_dim(shaped, expert_index, 2, keepdims=False)

    own_pair = jnp.stack([own_block(value_local), own_block(output_local)])
    own_routes = lax.all_to_all(own_pair, "head", split_axis=2, concat_axis=1, tiled=True).reshape(
        2, groups * head_count, tok_rows
    )
    value_table = slot_table(own_routes[0]).reshape(
        head_count, expert_count, pairs_dev, CAP, tok_rows
    )

    def pair_rows(route_part, gathered):
        slot_map = slot_table(route_part.reshape(groups, sources, tok_rows))
        slot_map = jnp.moveaxis(slot_map, 2, 1).reshape(groups * E, sources, CAP, tok_rows)
        slot_map = lax.dynamic_slice_in_dim(slot_map, expert_index * pairs_dev, pairs_dev, 0)
        picked = jnp.einsum(
            "psmt,stw->psmw",
            slot_map,
            gathered.reshape(sources, tok_rows, model_width),
            preferred_element_type=jnp.float32,
        )
        return picked.astype(jnp.bfloat16).reshape(pairs_dev, slot_count, model_width)

    whole_tokens, whole_cotangent = (
        lax.all_gather(tokens[0], ("head", "expert"), axis=0, tiled=True),
        lax.all_gather(cotangent[0], ("head", "expert"), axis=0, tiled=True),
    )
    token_slots = pair_rows(value_local, whole_tokens)
    cotangent_slots = pair_rows(output_local, whole_cotangent)
    value_slots = jnp.einsum(
        "prw,pwk->prk", token_slots, value_experts, preferred_element_type=jnp.float32
    ).astype(jnp.bfloat16)
    upstream_slots = jnp.einsum(
        "prw,pwk->prk", cotangent_slots, output_experts, preferred_element_type=jnp.float32
    ).astype(jnp.bfloat16)
    query_start = expert_index * query_rows
    group_values, group_upstream, all_keys = (
        lax.all_gather(value_slots, "expert", axis=0, tiled=True),
        lax.all_gather(upstream_slots, "expert", axis=0, tiled=True),
        lax.all_gather(key_vectors[0], "expert", axis=0, tiled=True),
    )
    token_source = jnp.arange(seq_len, dtype=jnp.int32) // tok_rows
    head_base = jnp.arange(groups, dtype=jnp.int32)[:, None] * E
    value_rank = slot_rank(value_local.reshape(groups, sources, tok_rows)).reshape(groups, seq_len)
    value_index = (head_base + value_local) * slot_count + token_source * CAP + value_rank
    value_rows = group_values.reshape(-1, head_dim)[value_index]
    output_rank = slot_rank(output_local.reshape(groups, sources, tok_rows)).reshape(
        groups, seq_len
    )
    block_routes = lax.dynamic_slice_in_dim(output_local, query_start, query_rows, 1)
    block_rank = lax.dynamic_slice_in_dim(output_rank, query_start, query_rows, 1)
    block_source = lax.dynamic_slice_in_dim(token_source, query_start, query_rows, 0)
    upstream_index = (head_base + block_routes) * slot_count + block_source * CAP + block_rank
    upstream_rows = group_upstream.reshape(-1, head_dim)[upstream_index]
    query_own = queries[0]
    scores = (
        jnp.einsum("ihc,jhc->hij", query_own, all_keys, preferred_element_type=jnp.float32)
        * score_scale
    )
    query_pos = query_start + jnp.arange(query_rows, dtype=jnp.int32)
    causal = jnp.arange(seq_len, dtype=jnp.int32)[None, :] <= query_pos[:, None]
    row_top = jnp.max(jnp.where(causal, scores, -jnp.inf), axis=-1, keepdims=True)
    weights = jnp.where(causal, jnp.exp(scores - row_top), 0.0)
    probs_full = weights / jnp.sum(weights, axis=-1, keepdims=True)
    prob_half = probs_full.astype(jnp.bfloat16)
    outputs = jnp.einsum(
        "hij,hjc->hic", prob_half, value_rows, preferred_element_type=jnp.float32
    ).astype(jnp.bfloat16)
    row_delta = jnp.sum(outputs.astype(jnp.float32) * upstream_rows.astype(jnp.float32), axis=-1)
    prob_grads = jnp.einsum(
        "hic,hjc->hij", upstream_rows, value_rows, preferred_element_type=jnp.float32
    )
    score_grads = (probs_full * (prob_grads - row_delta[:, :, None])).astype(jnp.bfloat16)
    query_grads = (
        jnp.einsum("hij,jhc->ihc", score_grads, all_keys, preferred_element_type=jnp.float32)
        * score_scale
    ).astype(jnp.bfloat16)
    key_part = (
        jnp.einsum("hij,ihc->jhc", score_grads, query_own, preferred_element_type=jnp.float32)
        * score_scale
    )
    value_part = jnp.einsum(
        "hij,hic->jhc", prob_half, upstream_rows, preferred_element_type=jnp.float32
    )
    key_sum, value_sum = (
        lax.psum_scatter(key_part, "expert", scatter_dimension=0, tiled=True),
        lax.psum_scatter(value_part, "expert", scatter_dimension=0, tiled=True),
    )
    value_half = value_sum.astype(jnp.bfloat16)
    block_value_routes = lax.dynamic_slice_in_dim(value_local, query_start, query_rows, 1).reshape(
        groups, head_count, tok_rows
    )
    value_place = slot_table(block_value_routes)
    output_place = slot_table(block_routes.reshape(groups, head_count, tok_rows))
    value_send = jnp.einsum(
        "hsemt,sthc->hesmc",
        value_place,
        value_half.reshape(head_count, tok_rows, groups, head_dim),
        preferred_element_type=jnp.float32,
    )
    value_send = value_send.astype(jnp.bfloat16).reshape(groups * E, head_count * CAP, head_dim)
    output_send = jnp.einsum(
        "hsemt,hstc->hesmc",
        output_place,
        outputs.reshape(groups, head_count, tok_rows, head_dim),
        preferred_element_type=jnp.float32,
    )
    output_send = output_send.astype(jnp.bfloat16).reshape(groups * E, head_count * CAP, head_dim)
    output_slots, grad_slots = (
        lax.all_to_all(output_send, "expert", split_axis=0, concat_axis=1, tiled=True),
        lax.all_to_all(value_send, "expert", split_axis=0, concat_axis=1, tiled=True),
    )
    value_term = jnp.einsum(
        "prw,prk->pwk", token_slots, grad_slots, preferred_element_type=jnp.float32
    )
    output_term = jnp.einsum(
        "prw,prk->pwk", cotangent_slots, output_slots, preferred_element_type=jnp.float32
    )
    value_grads, output_grads = (
        lax.psum_scatter(
            value_term.astype(jnp.bfloat16), "dp", scatter_dimension=1, tiled=True
        ).astype(jnp.float32),
        lax.psum_scatter(
            output_term.astype(jnp.bfloat16), "dp", scatter_dimension=1, tiled=True
        ).astype(jnp.float32),
    )
    token_terms = jnp.einsum(
        "prk,pwk->prw", grad_slots, value_experts, preferred_element_type=jnp.float32
    ).astype(jnp.bfloat16)
    returned = lax.all_to_all(
        token_terms.reshape(pairs_dev, sources, CAP, model_width),
        ("head", "expert"),
        split_axis=1,
        concat_axis=0,
        tiled=True,
    )
    returned = returned.reshape(head_count, expert_count, pairs_dev, CAP, model_width)
    token_grads = jnp.einsum(
        "gjpmt,gjpmw->tw", value_table, returned, preferred_element_type=jnp.float32
    )
    return (
        token_grads.astype(jnp.bfloat16)[None],
        query_grads[None],
        key_sum.astype(jnp.bfloat16)[None],
        value_grads.astype(jnp.bfloat16),
        output_grads.astype(jnp.bfloat16),
    )


KINDS = ("tok", "cot", "routes", "side", "heads", "part", "factor", "half", "term", "back")


def fused_kernel(
    sizes,
    tok,
    cot,
    q_in,
    k_in,
    value_routes_in,
    output_routes_in,
    value_hbm,
    output_hbm,
    tok_out,
    qg_out,
    kg_out,
    vg_out,
    og_out,
    rows,
    flat,
    flat_t,
    heads_raw,
    by_heads,
    routes,
    route_columns,
    weight,
    heads_in,
    part,
    part_in,
    factor,
    masked,
    score_keep,
    prob_keep,
    upstream_keep,
    back,
    back_in,
    term,
    term_side,
    term_sum,
    term_in,
    own_rows,
    sem_weight,
    sem_own,
    sem_sent,
    sem_block,
    sem_side,
    sem_routes,
    sem_heads,
    sem_part,
    sem_factor,
    sem_back,
    sem_half,
    sem_final,
):
    dn, gn, jn, own_heads, query_rows, tok_rows, width, head_dim = sizes
    sources = gn * jn
    seq_len = sources * tok_rows
    scale = head_dim ** (-0.5)
    group = own_heads // 2 if own_heads % 2 == 0 else own_heads
    d, g, j = lax.axis_index("dp"), lax.axis_index("head"), lax.axis_index("expert")
    block = g * jn + j
    f32, bf16 = jnp.float32, jnp.bfloat16

    def at(dd, gg, jj):
        return {"dp": lax.rem(d + dd, dn), "head": lax.rem(g + gg, gn), "expert": lax.rem(j + jj, jn)}

    others = [(dd, gg) for gg in range(gn) for dd in range(dn) if (dd, gg) != (0, 0)]

    def remote(kind, src, dst, recv_sem, where):
        return pltpu.make_async_remote_copy(
            src_ref=src,
            dst_ref=dst,
            send_sem=sem_sent.at[KINDS.index(kind)],
            recv_sem=recv_sem,
            device_id=where,
            device_id_type=pl.DeviceIdType.MESH,
        )

    def send(*args):
        remote(*args).start()

    def arrived(region, recv_sem):
        remote("tok", region, region, recv_sem, at(0, 0, 0)).wait_recv()

    def left(kind, region):
        remote(kind, region, region, sem_final.at[0], at(0, 0, 0)).wait_send()

    def columns(index):
        return pl.ds(pl.multiple_of(index * width, 128), width)

    weights_on_way = [
        pltpu.make_async_copy(hbm.at[:, columns(d), :], weight.at[i], sem_weight.at[i])
        for i, hbm in enumerate((value_hbm, output_hbm))
    ]
    own = [
        pltpu.make_async_copy(tok, own_rows.at[0], sem_own.at[0]),
        pltpu.make_async_copy(cot, own_rows.at[1], sem_own.at[1]),
        pltpu.make_async_copy(tok.at[:, columns(d)], rows.at[block, 0, d], sem_own.at[2]),
        pltpu.make_async_copy(cot.at[:, columns(d)], rows.at[block, 1, d], sem_own.at[3]),
        pltpu.make_async_copy(
            value_routes_in.at[pl.ds(j * own_heads, own_heads)],
            routes.at[d, pl.ds(0, own_heads)],
            sem_own.at[4],
        ),
        pltpu.make_async_copy(
            output_routes_in.at[pl.ds(j * own_heads, own_heads)],
            routes.at[d, pl.ds(own_heads, own_heads)],
            sem_own.at[5],
        ),
        pltpu.make_async_copy(q_in, heads_raw.at[0], sem_own.at[6]),
        pltpu.make_async_copy(k_in, heads_raw.at[1], sem_own.at[7]),
    ]
    for copy in own:
        copy.start()

    barrier = pltpu.get_barrier_semaphore()

    def greet(where):
        pl.semaphore_signal(
            barrier, inc=1, device_id=at(*where), device_id_type=pl.DeviceIdType.MESH
        )

    for dd, gg in others:
        greet((dd, gg, 0))
    for jj in range(1, jn):
        greet((0, 0, jj))
    for copy in own[:2]:
        copy.wait()
    pl.semaphore_wait(barrier, len(others) + jn - 1)

    def on_line(body):
        for k in range(gn):
            pl.when(g == k)(functools.partial(body, k))

    def nearest(k):
        return sorted(range(gn), key=lambda t: (abs(t - k), t))

    def place(dd, target):
        return {"dp": lax.rem(d + dd, dn), "head": jnp.int32(target), "expert": j}

    def share(i):
        def body(k):
            for target in nearest(k):
                for dd in range(dn):
                    if dd or target != k:
                        send(
                            ("tok", "cot")[i],
                            own_rows.at[i, :, columns(lax.rem(d + dd, dn))],
                            rows.at[block, i, d],
                            sem_block.at[g, i],
                            place(dd, target),
                        )

        on_line(body)

    def relay(i, which):
        def body(k):
            for source in nearest(k)[which]:
                count = dn - 1 if source == k else dn
                here = rows.at[source * jn + j, i]
                if count:
                    arrived(here.at[pl.ds(0, count)], sem_block.at[source, i])
                for jj in range(1, jn):
                    send("side", here, here, sem_side.at[i], at(0, 0, jj))

        on_line(body)

    share(1)
    for copy in own[2:]:
        copy.wait()
    for dd in range(1, dn):
        send("routes", routes.at[d], routes.at[d], sem_routes.at[0], at(dd, 0, 0))
    for i in range(2):
        turned = jnp.transpose(heads_raw[i].astype(f32), (1, 0, 2)).astype(bf16)
        for jj in range(jn):
            by_heads[i, jj] = turned[jj * own_heads : (jj + 1) * own_heads]
        heads_in[i, j] = by_heads[i, j]
    for jj in range(1, jn):
        peer = lax.rem(j + jj, jn)
        for i in range(2):
            send("heads", by_heads.at[i, peer], heads_in.at[i, j], sem_heads.at[0], at(0, 0, jj))
    for copy in weights_on_way:
        copy.start()
    relay(1, slice(0, gn - 1))
    share(0)
    relay(1, slice(gn - 1, gn))

    def flatten(i):
        arrived(rows.at[pl.ds(0, gn * (jn - 1)), i], sem_side.at[i])
        for b in range(dn):
            piece = jnp.concatenate([rows[s, i, b].astype(f32) for s in range(sources)], axis=0)
            flat[i, b * seq_len : (b + 1) * seq_len, :] = piece.astype(bf16)

    def column(i, h, b):
        c = i * own_heads + h
        return jnp.broadcast_to(route_columns[b, :seq_len, c : c + 1], (seq_len, head_dim))

    def turn_routes(b):
        lines = jnp.concatenate([routes[b, c] for c in range(2 * own_heads)], axis=0)
        spare = route_columns.shape[1] - seq_len
        if spare:
            lines = jnp.concatenate([lines, jnp.zeros((2 * own_heads, spare), jnp.int32)], axis=1)
        route_columns[b] = lines.T

    def project(i):
        weights_on_way[i].wait()
        for h in range(own_heads):
            picked = [jnp.zeros((seq_len, head_dim), f32) for _ in range(dn)]
            for e in range(0, E, 2):
                p = h * E + e
                both = jnp.concatenate([weight[i, p], weight[i, p + 1]], axis=1)
                every = jnp.dot(flat[i], both, preferred_element_type=f32)
                for b in range(dn):
                    own_part = every[b * seq_len : (b + 1) * seq_len]
                    route = column(i, h, b)
                    picked[b] = jnp.where(route == e, own_part[:, :head_dim], picked[b])
                    picked[b] = jnp.where(route == e + 1, own_part[:, head_dim:], picked[b])
            for b in range(dn):
                part[b, i, h] = picked[b].astype(bf16)
            if (h + 1) % group == 0:
                heads = pl.ds(h + 1 - group, group)
                for dd in range(1, dn):
                    send(
                        "part",
                        part.at[lax.rem(d + dd, dn), i, heads],
                        part_in.at[dd, i, heads],
                        sem_part.at[i],
                        at(dd, 0, 0),
                    )

    query_pos = lax.broadcasted_iota(jnp.int32, (seq_len, seq_len), 0)
    key_pos = lax.broadcasted_iota(jnp.int32, (seq_len, seq_len), 1)
    causal = key_pos <= query_pos

    def joined(i, h):
        return jnp.concatenate([heads_in[i, jj, h] for jj in range(jn)], axis=0)

    def total(i, h):
        whole = part[d, i, h].astype(f32)
        for dd in range(1, dn):
            whole = whole + part_in[dd, i, h].astype(f32)
        return whole.astype(bf16)

    def across(a, b):
        return lax.dot_general(a, b, (((1,), (1,)), ((), ())), preferred_element_type=f32)

    def over_rows(a, b):
        return lax.dot_general(a, b, (((0,), (0,)), ((), ())), preferred_element_type=f32)

    def mask(i):
        for h in range(own_heads):
            for b in range(dn):
                source = factor[b, i, h].astype(f32)
                route = column(i, h, b)
                for e in range(E):
                    p = h * E + e
                    masked[
                        i,
                        p // 2,
                        b * seq_len : (b + 1) * seq_len,
                        (p % 2) * head_dim : (p % 2 + 1) * head_dim,
                    ] = jnp.where(route == e, source, 0.0).astype(bf16)

    def spread(i):
        for dd in range(1, dn):
            send("factor", factor.at[d, i], factor.at[d, i], sem_factor.at[i], at(dd, 0, 0))

    def others_of(region, i):
        return region.at[pl.ds(0, dn - 1), i]

    arrived(heads_in.at[:, pl.ds(0, jn - 1)], sem_heads.at[0])
    for h in range(own_heads):
        query, key = joined(0, h), joined(1, h)
        scores = across(query, key) * scale
        top = jnp.max(jnp.where(causal, scores, -jnp.inf), axis=-1, keepdims=True)
        soft = jnp.where(causal, jnp.exp(scores - top), 0.0)
        prob_keep[h] = soft / jnp.sum(soft, axis=-1, keepdims=True)
    arrived(routes.at[pl.ds(0, dn - 1)], sem_routes.at[0])
    for b in range(dn):
        turn_routes(b)
    relay(0, slice(0, 1))
    flatten(1)
    project(1)
    relay(0, slice(1, gn))
    arrived(others_of(part_in, 1), sem_part.at[1])
    for h in range(own_heads):
        upstream_keep[h] = total(1, h)
        factor[d, 0, h] = over_rows(prob_keep[h].astype(bf16), upstream_keep[h]).astype(bf16)
    spread(0)
    flatten(0)
    project(0)
    arrived(others_of(factor, 0), sem_factor.at[0])
    mask(0)
    couples = own_heads * E // 2
    step = min(width, 256)
    for n in range(0, width, step):
        added = jnp.zeros((dn * seq_len, step), f32)
        for c in range(couples):
            both = jnp.concatenate(
                [weight[0, 2 * c, n : n + step, :], weight[0, 2 * c + 1, n : n + step, :]], axis=1
            )
            added = added + across(masked[0, c], both)
        for b in range(dn):
            for r in range(sources):
                first = (b * sources + r) * tok_rows
                term[r % jn, r // jn, b, :, n : n + step] = added[first : first + tok_rows].astype(
                    bf16
                )
    for target in range(gn):
        for jj in range(1, jn):
            send(
                "half",
                term.at[lax.rem(j + jj, jn), target],
                term_side.at[jj, target],
                sem_half.at[target],
                at(0, 0, jj),
            )

    arrived(others_of(part_in, 0), sem_part.at[0])
    for h in range(own_heads):
        value, upstream, probs = total(0, h), upstream_keep[h], prob_keep[h]
        output = jnp.dot(probs.astype(bf16), value, preferred_element_type=f32).astype(bf16)
        factor[d, 1, h] = output
        delta = jnp.sum(output.astype(f32) * upstream.astype(f32), axis=-1, keepdims=True)
        score_keep[h] = (probs * (across(upstream, value) - delta)).astype(bf16)
    spread(1)
    for h in range(own_heads):
        query, key, score = joined(0, h), joined(1, h), score_keep[h]
        query_grad = (jnp.dot(score, key, preferred_element_type=f32) * scale).astype(bf16)
        key_grad = (over_rows(score, query) * scale).astype(bf16)
        for jj in range(jn):
            back[jj, 0, h] = query_grad[jj * query_rows : (jj + 1) * query_rows]
            back[jj, 1, h] = key_grad[jj * query_rows : (jj + 1) * query_rows]
    for jj in range(1, jn):
        send("back", back.at[lax.rem(j + jj, jn)], back_in.at[j], sem_back.at[0], at(0, 0, jj))

    def gradients(i, out):
        flat_t[i] = flat[i].T
        for c in range(couples):
            whole = jnp.dot(flat_t[i], masked[i, c], preferred_element_type=f32)
            out[2 * c] = whole[:, :head_dim].astype(bf16)
            out[2 * c + 1] = whole[:, head_dim:].astype(bf16)


    def join_halves(which, k):
        for target in range(gn)[which]:
            arrived(term_side.at[pl.ds(0, jn - 1), target], sem_half.at[target])
            whole = term[j, target].astype(f32)
            for jj in range(1, jn):
                whole = whole + term_side[jj, target].astype(f32)
            term_sum[target] = whole.astype(bf16)
            for dd in range(dn):
                if dd == 0 and target == k:
                    term_in[k * dn + d] = term_sum[k, d]
                else:
                    send(
                        "term",
                        term_sum.at[target, lax.rem(d + dd, dn)],
                        term_in.at[g * dn + d],
                        sem_final.at[0],
                        place(dd, target),
                    )

    on_line(functools.partial(join_halves, slice(0, 1)))
    gradients(0, vg_out)
    on_line(functools.partial(join_halves, slice(1, gn)))
    arrived(others_of(factor, 1), sem_factor.at[1])
    mask(1)
    gradients(1, og_out)

    back_in[j] = back[j]
    arrived(back_in.at[pl.ds(0, jn - 1)], sem_back.at[0])
    for jj in range(jn):
        qg_out[jj] = back_in[jj, 0]
        kg_out[jj] = back_in[jj, 1]
    all_terms = term_in.at[pl.ds(0, len(others))]
    arrived(all_terms, sem_final.at[0])
    for b in range(dn):
        total_rows = term_in[b].astype(f32)
        for s in range(1, gn):
            total_rows = total_rows + term_in[s * dn + b].astype(f32)
        tok_out[:, b * width : (b + 1) * width] = total_rows.astype(bf16)
    for kind in ("tok", "cot", "term"):
        left(kind, all_terms)
    left("routes", routes.at[pl.ds(0, dn - 1)])
    left("side", rows.at[pl.ds(0, gn * (jn - 1))])
    left("heads", heads_in.at[:, pl.ds(0, jn - 1)])
    left("part", part_in.at[pl.ds(0, dn - 1)])
    left("factor", factor.at[pl.ds(0, dn - 1)])
    left("half", term_side.at[pl.ds(0, jn - 1)])
    left("back", back_in.at[pl.ds(0, jn - 1)])


def finish_kernel(
    tok_in, qg_in, kg_in, vg_in, og_in, tok_out, qg_out, kg_out, vg_out, og_out, turned, sems
):
    pieces = E
    size = vg_in.shape[0] // pieces
    whole = [
        pltpu.make_async_copy(source, out, sems.at[i])
        for i, (source, out) in enumerate(((vg_in, vg_out), (og_in, og_out), (tok_in, tok_out)))
    ]
    for i, (source, out) in enumerate(((vg_in, vg_out), (og_in, og_out))):
        for n in range(pieces):
            part = pl.ds(n * size, size)
            pltpu.make_async_copy(source.at[part], out.at[part], sems.at[i]).start()
    whole[2].start()
    for i, (source, out) in enumerate(((qg_in, qg_out), (kg_in, kg_out))):
        turned[i] = jnp.transpose(source[...].astype(jnp.float32), (1, 0, 2)).astype(out.dtype)
        whole.append(pltpu.make_async_copy(turned.at[i], out, sems.at[3 + i]))
        whole[3 + i].start()
    for copy in whole:
        copy.wait()


def fused(
    tokens,
    cotangent,
    queries,
    key_vectors,
    value_routes,
    output_routes,
    value_experts,
    output_experts,
):
    dn, gn, jn = lax.axis_size("dp"), lax.axis_size("head"), lax.axis_size("expert")
    _, tok_rows, model_width = tokens.shape
    width = model_width // dn
    _, query_rows, groups, head_dim = queries.shape
    seq_len = value_routes.shape[2]
    pairs_dev = value_experts.shape[0]
    own_heads = groups // jn
    sources = gn * jn
    bf16 = jnp.bfloat16

    value_lines = value_routes.reshape(groups, 1, seq_len)
    output_lines = output_routes.reshape(groups, 1, seq_len)

    vmem = pl.BlockSpec(memory_space=pltpu.VMEM)
    hbm = pl.BlockSpec(memory_space=pl.ANY)
    dma = pltpu.SemaphoreType.DMA
    head_block = (jn, own_heads, query_rows, head_dim)
    grad_shape = jax.ShapeDtypeStruct((pairs_dev, width, head_dim), bf16)
    tok_grads, query_grads, key_grads, value_grads, output_grads = pl.pallas_call(
        functools.partial(
            fused_kernel, (dn, gn, jn, own_heads, query_rows, tok_rows, width, head_dim)
        ),
        name="fused",
        out_shape=(
            pltpu.VMEM((tok_rows, model_width), bf16),
            pltpu.VMEM(head_block, bf16),
            pltpu.VMEM(head_block, bf16),
            pltpu.VMEM(grad_shape.shape, bf16),
            pltpu.VMEM(grad_shape.shape, bf16),
        ),
        in_specs=[hbm] * 8,
        out_specs=(vmem,) * 5,
        scratch_shapes=[
            pltpu.VMEM((sources, 2, dn, tok_rows, width), bf16),
            pltpu.VMEM((2, dn * seq_len, width), bf16),
            pltpu.VMEM((2, width, dn * seq_len), bf16),
            pltpu.VMEM((2, query_rows, groups, head_dim), bf16),
            pltpu.VMEM((2, jn, own_heads, query_rows, head_dim), bf16),
            pltpu.VMEM((dn, 2 * own_heads, 1, seq_len), jnp.int32),
            pltpu.VMEM((dn, -(-seq_len // 128) * 128, 2 * own_heads), jnp.int32),
            pltpu.VMEM((2, pairs_dev, width, head_dim), bf16),
            pltpu.VMEM((2, jn, own_heads, query_rows, head_dim), bf16),
            pltpu.VMEM((dn, 2, own_heads, seq_len, head_dim), bf16),
            pltpu.VMEM((dn, 2, own_heads, seq_len, head_dim), bf16),
            pltpu.VMEM((dn, 2, own_heads, seq_len, head_dim), bf16),
            pltpu.VMEM((2, pairs_dev // 2, dn * seq_len, 2 * head_dim), bf16),
            pltpu.VMEM((own_heads, seq_len, seq_len), bf16),
            pltpu.VMEM((own_heads, seq_len, seq_len), jnp.float32),
            pltpu.VMEM((own_heads, seq_len, head_dim), bf16),
            pltpu.VMEM((jn, 2, own_heads, query_rows, head_dim), bf16),
            pltpu.VMEM((jn, 2, own_heads, query_rows, head_dim), bf16),
            pltpu.VMEM((jn, gn, dn, tok_rows, width), bf16),
            pltpu.VMEM((jn, gn, dn, tok_rows, width), bf16),
            pltpu.VMEM((gn, dn, tok_rows, width), bf16),
            pltpu.VMEM((gn * dn, tok_rows, width), bf16),
            pltpu.VMEM((2, tok_rows, model_width), bf16),
            dma((2,)),
            dma((8,)),
            dma((len(KINDS),)),
            dma((gn, 2)),
            dma((2,)),
            dma((1,)),
            dma((1,)),
            dma((2,)),
            dma((2,)),
            dma((1,)),
            dma((gn,)),
            dma((1,)),
        ],
        compiler_params=pltpu.CompilerParams(
            collective_id=0, has_side_effects=True, vmem_limit_bytes=40 * 1024 * 1024
        ),
    )(
        *(
            pltpu.with_memory_space_constraint(x, pltpu.HBM)
            for x in (
                tokens[0],
                cotangent[0],
                queries[0],
                key_vectors[0],
                value_lines,
                output_lines,
            )
        ),
        value_experts,
        output_experts,
    )

    by_head = (groups, query_rows, head_dim)
    row_shape = jax.ShapeDtypeStruct((query_rows, groups, head_dim), bf16)
    tok_grads, query_grads, key_grads, value_grads, output_grads = pl.pallas_call(
        finish_kernel,
        name="finish",
        out_shape=(
            jax.ShapeDtypeStruct((tok_rows, model_width), bf16),
            row_shape,
            row_shape,
            grad_shape,
            grad_shape,
        ),
        in_specs=[vmem] * 5,
        out_specs=(hbm,) * 5,
        scratch_shapes=[
            pltpu.VMEM((2, query_rows, groups, head_dim), bf16),
            dma((5,)),
        ],
        compiler_params=pltpu.CompilerParams(vmem_limit_bytes=8 * 1024 * 1024),
    )(
        tok_grads,
        query_grads.reshape(by_head),
        key_grads.reshape(by_head),
        value_grads,
        output_grads,
    )
    return tok_grads[None], query_grads[None], key_grads[None], value_grads, output_grads


def chosen(*args):
    groups, pairs_dev = args[2].shape[2], args[6].shape[0]
    dp_count, expert_count = lax.axis_size("dp"), lax.axis_size("expert")
    whole_heads = groups % expert_count == 0 and pairs_dev == groups // expert_count * E
    small = args[4].shape[2] <= 128
    if whole_heads and small and expert_count > 1 and dp_count > 1 and args[0].shape[2] % (dp_count * 256) == 0:
        return fused(*args)
    return local(*args)


def solution(mesh):
    return jax.shard_map(
        chosen,
        mesh=mesh,
        in_specs=(
            P("dp", ("head", "expert"), None),
            P("dp", ("head", "expert"), None),
            P("dp", "expert", "head", None),
            P("dp", "expert", "head", None),
            P("dp", "head", None, None),
            P("dp", "head", None, None),
            P(("head", "expert"), None, None),
            P(("head", "expert"), None, None),
        ),
        out_specs=(
            P("dp", ("head", "expert"), None),
            P("dp", "expert", "head", None),
            P("dp", "expert", "head", None),
            P(("head", "expert"), "dp", None),
            P(("head", "expert"), "dp", None),
        ),
        check_vma=False,
    )
```

```python
import functools

import jax
import jax.numpy as jnp
from jax import lax
from jax.experimental import pallas as pl
from jax.experimental.pallas import tpu as pltpu
from jax.sharding import PartitionSpec as P

E = 4
CAP = 3


def slot_rank(routes):
    places = jnp.arange(routes.shape[-1], dtype=jnp.int32)
    same = routes[..., :, None] == routes[..., None, :]
    return jnp.sum(jnp.logical_and(same, places[None, :] < places[:, None]).astype(jnp.int32), axis=-1)


def slot_table(routes):
    rank_of = slot_rank(routes)
    expert_hit = routes[..., None, None, :] == jnp.arange(E, dtype=jnp.int32)[:, None, None]
    place_hit = rank_of[..., None, None, :] == jnp.arange(CAP, dtype=jnp.int32)[:, None]
    return jnp.logical_and(expert_hit, place_hit).astype(jnp.bfloat16)


def local(
    tokens,
    cotangent,
    queries,
    key_vectors,
    value_routes,
    output_routes,
    value_experts,
    output_experts,
):
    head_count = lax.axis_size("head")
    expert_count = lax.axis_size("expert")
    sources = head_count * expert_count
    expert_index = lax.axis_index("expert")
    tok_rows = tokens.shape[1]
    model_width = tokens.shape[2]
    query_rows = queries.shape[1]
    groups = queries.shape[2]
    head_dim = queries.shape[3]
    seq_len = value_routes.shape[2]
    pairs_dev = value_experts.shape[0]
    slot_count = sources * CAP
    score_scale = head_dim ** (-0.5)
    value_local = value_routes[0, :, :, 0]
    output_local = output_routes[0, :, :, 0]

    def own_block(route_part):
        shaped = route_part.reshape(groups, head_count, expert_count, tok_rows)
        return lax.dynamic_index_in_dim(shaped, expert_index, 2, keepdims=False)

    own_pair = jnp.stack([own_block(value_local), own_block(output_local)])
    own_routes = lax.all_to_all(own_pair, "head", split_axis=2, concat_axis=1, tiled=True).reshape(
        2, groups * head_count, tok_rows
    )
    value_table = slot_table(own_routes[0]).reshape(
        head_count, expert_count, pairs_dev, CAP, tok_rows
    )

    def pair_rows(route_part, gathered):
        slot_map = slot_table(route_part.reshape(groups, sources, tok_rows))
        slot_map = jnp.moveaxis(slot_map, 2, 1).reshape(groups * E, sources, CAP, tok_rows)
        slot_map = lax.dynamic_slice_in_dim(slot_map, expert_index * pairs_dev, pairs_dev, 0)
        picked = jnp.einsum(
            "psmt,stw->psmw",
            slot_map,
            gathered.reshape(sources, tok_rows, model_width),
            preferred_element_type=jnp.float32,
        )
        return picked.astype(jnp.bfloat16).reshape(pairs_dev, slot_count, model_width)

    whole_tokens, whole_cotangent = (
        lax.all_gather(tokens[0], ("head", "expert"), axis=0, tiled=True),
        lax.all_gather(cotangent[0], ("head", "expert"), axis=0, tiled=True),
    )
    token_slots = pair_rows(value_local, whole_tokens)
    cotangent_slots = pair_rows(output_local, whole_cotangent)
    value_slots = jnp.einsum(
        "prw,pwk->prk", token_slots, value_experts, preferred_element_type=jnp.float32
    ).astype(jnp.bfloat16)
    upstream_slots = jnp.einsum(
        "prw,pwk->prk", cotangent_slots, output_experts, preferred_element_type=jnp.float32
    ).astype(jnp.bfloat16)
    query_start = expert_index * query_rows
    group_values, group_upstream, all_keys = (
        lax.all_gather(value_slots, "expert", axis=0, tiled=True),
        lax.all_gather(upstream_slots, "expert", axis=0, tiled=True),
        lax.all_gather(key_vectors[0], "expert", axis=0, tiled=True),
    )
    token_source = jnp.arange(seq_len, dtype=jnp.int32) // tok_rows
    head_base = jnp.arange(groups, dtype=jnp.int32)[:, None] * E
    value_rank = slot_rank(value_local.reshape(groups, sources, tok_rows)).reshape(groups, seq_len)
    value_index = (head_base + value_local) * slot_count + token_source * CAP + value_rank
    value_rows = group_values.reshape(-1, head_dim)[value_index]
    output_rank = slot_rank(output_local.reshape(groups, sources, tok_rows)).reshape(
        groups, seq_len
    )
    block_routes = lax.dynamic_slice_in_dim(output_local, query_start, query_rows, 1)
    block_rank = lax.dynamic_slice_in_dim(output_rank, query_start, query_rows, 1)
    block_source = lax.dynamic_slice_in_dim(token_source, query_start, query_rows, 0)
    upstream_index = (head_base + block_routes) * slot_count + block_source * CAP + block_rank
    upstream_rows = group_upstream.reshape(-1, head_dim)[upstream_index]
    query_own = queries[0]
    scores = (
        jnp.einsum("ihc,jhc->hij", query_own, all_keys, preferred_element_type=jnp.float32)
        * score_scale
    )
    query_pos = query_start + jnp.arange(query_rows, dtype=jnp.int32)
    causal = jnp.arange(seq_len, dtype=jnp.int32)[None, :] <= query_pos[:, None]
    row_top = jnp.max(jnp.where(causal, scores, -jnp.inf), axis=-1, keepdims=True)
    weights = jnp.where(causal, jnp.exp(scores - row_top), 0.0)
    probs_full = weights / jnp.sum(weights, axis=-1, keepdims=True)
    prob_half = probs_full.astype(jnp.bfloat16)
    outputs = jnp.einsum(
        "hij,hjc->hic", prob_half, value_rows, preferred_element_type=jnp.float32
    ).astype(jnp.bfloat16)
    row_delta = jnp.sum(outputs.astype(jnp.float32) * upstream_rows.astype(jnp.float32), axis=-1)
    prob_grads = jnp.einsum(
        "hic,hjc->hij", upstream_rows, value_rows, preferred_element_type=jnp.float32
    )
    score_grads = (probs_full * (prob_grads - row_delta[:, :, None])).astype(jnp.bfloat16)
    query_grads = (
        jnp.einsum("hij,jhc->ihc", score_grads, all_keys, preferred_element_type=jnp.float32)
        * score_scale
    ).astype(jnp.bfloat16)
    key_part = (
        jnp.einsum("hij,ihc->jhc", score_grads, query_own, preferred_element_type=jnp.float32)
        * score_scale
    )
    value_part = jnp.einsum(
        "hij,hic->jhc", prob_half, upstream_rows, preferred_element_type=jnp.float32
    )
    key_sum, value_sum = (
        lax.psum_scatter(key_part, "expert", scatter_dimension=0, tiled=True),
        lax.psum_scatter(value_part, "expert", scatter_dimension=0, tiled=True),
    )
    value_half = value_sum.astype(jnp.bfloat16)
    block_value_routes = lax.dynamic_slice_in_dim(value_local, query_start, query_rows, 1).reshape(
        groups, head_count, tok_rows
    )
    value_place = slot_table(block_value_routes)
    output_place = slot_table(block_routes.reshape(groups, head_count, tok_rows))
    value_send = jnp.einsum(
        "hsemt,sthc->hesmc",
        value_place,
        value_half.reshape(head_count, tok_rows, groups, head_dim),
        preferred_element_type=jnp.float32,
    )
    value_send = value_send.astype(jnp.bfloat16).reshape(groups * E, head_count * CAP, head_dim)
    output_send = jnp.einsum(
        "hsemt,hstc->hesmc",
        output_place,
        outputs.reshape(groups, head_count, tok_rows, head_dim),
        preferred_element_type=jnp.float32,
    )
    output_send = output_send.astype(jnp.bfloat16).reshape(groups * E, head_count * CAP, head_dim)
    output_slots, grad_slots = (
        lax.all_to_all(output_send, "expert", split_axis=0, concat_axis=1, tiled=True),
        lax.all_to_all(value_send, "expert", split_axis=0, concat_axis=1, tiled=True),
    )
    value_term = jnp.einsum(
        "prw,prk->pwk", token_slots, grad_slots, preferred_element_type=jnp.float32
    )
    output_term = jnp.einsum(
        "prw,prk->pwk", cotangent_slots, output_slots, preferred_element_type=jnp.float32
    )
    value_grads, output_grads = (
        lax.psum_scatter(
            value_term.astype(jnp.bfloat16), "dp", scatter_dimension=1, tiled=True
        ).astype(jnp.float32),
        lax.psum_scatter(
            output_term.astype(jnp.bfloat16), "dp", scatter_dimension=1, tiled=True
        ).astype(jnp.float32),
    )
    token_terms = jnp.einsum(
        "prk,pwk->prw", grad_slots, value_experts, preferred_element_type=jnp.float32
    ).astype(jnp.bfloat16)
    returned = lax.all_to_all(
        token_terms.reshape(pairs_dev, sources, CAP, model_width),
        ("head", "expert"),
        split_axis=1,
        concat_axis=0,
        tiled=True,
    )
    returned = returned.reshape(head_count, expert_count, pairs_dev, CAP, model_width)
    token_grads = jnp.einsum(
        "gjpmt,gjpmw->tw", value_table, returned, preferred_element_type=jnp.float32
    )
    return (
        token_grads.astype(jnp.bfloat16)[None],
        query_grads[None],
        key_sum.astype(jnp.bfloat16)[None],
        value_grads.astype(jnp.bfloat16),
        output_grads.astype(jnp.bfloat16),
    )


def line_plan(gn):
    order = [sorted(range(gn), key=lambda t: (abs(t - k), t)) for k in range(gn)]
    plain = (order, [row[1:] for row in order], [{} for _ in range(gn)])
    if gn != 4:
        return plain, plain
    passed = (
        [[0, 1, 3, 2], [1, 2, 0, 3], [2, 1, 3, 0], [3, 2, 0, 1]],
        [[1, 2, 3], [2, 0], [1, 3], [2, 1, 0]],
        [{}, {2: 0}, {1: 3}, {}],
    )
    return plain, passed


KINDS = (
    "tok",
    "cot",
    "onward",
    "routes",
    "side",
    "heads",
    "part",
    "factor",
    "cols",
    "half",
    "term",
    "back",
)
NEAR = 2


def fused_kernel(
    sizes,
    tok,
    cot,
    q_in,
    k_in,
    value_routes_in,
    output_routes_in,
    value_hbm,
    output_hbm,
    tok_out,
    qg_out,
    kg_out,
    vg_out,
    og_out,
    rows,
    far_rows,
    flat,
    cols,
    flat_t,
    heads_raw,
    by_heads,
    routes,
    route_columns,
    weight,
    heads_in,
    part,
    part_in,
    factor,
    masked,
    score_keep,
    prob_keep,
    upstream_keep,
    back,
    back_in,
    term,
    term_side,
    term_sum,
    term_in,
    own_rows,
    sem_weight,
    sem_own,
    sem_sent,
    sem_block,
    sem_side,
    sem_routes,
    sem_heads,
    sem_part,
    sem_factor,
    sem_cols,
    sem_back,
    sem_half,
    sem_final,
):
    dn, gn, jn, own_heads, query_rows, tok_rows, width, head_dim = sizes
    sources = gn * jn
    cn, xn = NEAR, dn // NEAR
    seq_len = sources * tok_rows
    scale = head_dim ** (-0.5)
    group = own_heads // 2 if own_heads % 2 == 0 else own_heads
    d, g, j = lax.axis_index("dp"), lax.axis_index("head"), lax.axis_index("expert")
    block = g * jn + j
    x, c = d // cn, lax.rem(d, cn)
    f32, bf16 = jnp.float32, jnp.bfloat16

    def at(dd, gg, jj):
        return {"dp": lax.rem(d + dd, dn), "head": lax.rem(g + gg, gn), "expert": lax.rem(j + jj, jn)}

    def near(cc):
        return lax.rem(c + cc, cn)

    others = [(cc, gg) for gg in range(gn) for cc in range(cn) if (cc, gg) != (0, 0)]
    afar = [(xx, cc) for xx in range(1, xn) for cc in range(cn)]

    def across(xx, cc):
        return {"dp": lax.rem(x + xx, xn) * cn + near(cc), "head": g, "expert": j}

    def remote(kind, src, dst, recv_sem, where):
        return pltpu.make_async_remote_copy(
            src_ref=src,
            dst_ref=dst,
            send_sem=sem_sent.at[KINDS.index(kind)],
            recv_sem=recv_sem,
            device_id=where,
            device_id_type=pl.DeviceIdType.MESH,
        )

    def send(*args):
        remote(*args).start()

    def arrived(region, recv_sem):
        remote("tok", region, region, recv_sem, at(0, 0, 0)).wait_recv()

    def left(kind, region):
        remote(kind, region, region, sem_final.at[0], at(0, 0, 0)).wait_send()

    def columns(index):
        return pl.ds(pl.multiple_of(index * width, 128), width)

    weights_on_way = [
        pltpu.make_async_copy(
            hbm.at[:, columns(q * cn + c), :], weight.at[i, :, q], sem_weight.at[i, q]
        )
        for i, hbm in ((1, output_hbm), (0, value_hbm))
        for q in range(xn)
    ]
    own = [
        pltpu.make_async_copy(tok, own_rows.at[0], sem_own.at[0]),
        pltpu.make_async_copy(cot, own_rows.at[1], sem_own.at[1]),
        pltpu.make_async_copy(
            value_routes_in.at[pl.ds(j * own_heads, own_heads)],
            routes.at[d, pl.ds(0, own_heads)],
            sem_own.at[2],
        ),
        pltpu.make_async_copy(
            output_routes_in.at[pl.ds(j * own_heads, own_heads)],
            routes.at[d, pl.ds(own_heads, own_heads)],
            sem_own.at[3],
        ),
        pltpu.make_async_copy(q_in, heads_raw.at[0], sem_own.at[4]),
        pltpu.make_async_copy(k_in, heads_raw.at[1], sem_own.at[5]),
    ]
    own += [
        pltpu.make_async_copy(
            source.at[:, columns(q * cn + c)], rows.at[block, i, c, q], sem_own.at[6 + i * xn + q]
        )
        for i, source in enumerate((tok, cot))
        for q in range(xn)
    ]
    for copy in own:
        copy.start()

    barrier = pltpu.get_barrier_semaphore()

    def greet(where):
        pl.semaphore_signal(
            barrier, inc=1, device_id=where, device_id_type=pl.DeviceIdType.MESH
        )

    for cc, gg in others:
        greet({"dp": x * cn + near(cc), "head": lax.rem(g + gg, gn), "expert": j})
    for xx, cc in afar:
        greet(across(xx, cc))
    for jj in range(1, jn):
        greet(at(0, 0, jj))
    for copy in own[:2]:
        copy.wait()
    pl.semaphore_wait(barrier, len(others) + len(afar) + jn - 1)

    def on_line(body):
        for k in range(gn):
            pl.when(g == k)(functools.partial(body, k))

    plans = line_plan(gn)

    def place(cc, target):
        return {"dp": x * cn + near(cc), "head": jnp.int32(target), "expert": j}

    def share(i):
        def body(k):
            for target in [k] + plans[i][1][k]:
                for cc in range(cn):
                    for q in range(xn):
                        if cc or target != k:
                            send(
                                ("tok", "cot")[i],
                                own_rows.at[i, :, columns(q * cn + near(cc))],
                                rows.at[block, i, c, q],
                                sem_block.at[g, i],
                                place(cc, target),
                            )

        on_line(body)

    def exchange(i, source):
        for xx in range(1, xn):
            send(
                "cols",
                rows.at[source, i, :, lax.rem(x + xx, xn)],
                far_rows.at[source, i, x],
                sem_cols.at[i],
                across(xx, 0),
            )

    def relay(i, which):
        def body(k):
            for source in plans[i][0][k][which]:
                count = cn - 1 if source == k else cn
                here = rows.at[source * jn + j, i]
                if count:
                    arrived(here.at[pl.ds(0, count)], sem_block.at[source, i])
                onward = plans[i][2][k]
                if source in onward:
                    send("onward", here, here, sem_block.at[source, i], place(0, onward[source]))
                for jj in range(1, jn):
                    send("side", here, here, sem_side.at[source, i], at(0, 0, jj))
                exchange(i, source * jn + j)

        on_line(body)

    share(1)
    for copy in own[2:]:
        copy.wait()
    for dd in range(1, dn):
        send("routes", routes.at[d], routes.at[d], sem_routes.at[0], at(dd, 0, 0))
    for i in range(2):
        turned = jnp.transpose(heads_raw[i].astype(f32), (1, 0, 2)).astype(bf16)
        for jj in range(jn):
            by_heads[i, jj] = turned[jj * own_heads : (jj + 1) * own_heads]
        heads_in[i, j] = by_heads[i, j]
    for jj in range(1, jn):
        peer = lax.rem(j + jj, jn)
        for i in range(2):
            send("heads", by_heads.at[i, peer], heads_in.at[i, j], sem_heads.at[0], at(0, 0, jj))
    for copy in weights_on_way:
        copy.start()
    relay(1, slice(0, 2))
    share(0)
    relay(0, slice(0, 1))
    relay(1, slice(2, gn))

    def flatten(i):
        for b in range(cn):
            for q in range(xn):
                piece = jnp.concatenate(
                    [rows[s, i, b, q].astype(f32) for s in range(sources)], axis=0
                )
                flat[i, q, b * seq_len : (b + 1) * seq_len, :] = piece.astype(bf16)

    def own_span(place_x):
        return pl.ds(pl.multiple_of(place_x * cn * seq_len, cn * seq_len), cn * seq_len)

    def from_side(i, which):
        def body(k):
            for source in plans[i][0][k][which]:
                arrived(rows.at[pl.ds(0, jn - 1), i], sem_side.at[source, i])
                for jj in range(1, jn):
                    exchange(i, source * jn + lax.rem(j + jj, jn))

        on_line(body)

    def gather_columns(i):
        arrived(far_rows.at[:, i, pl.ds(0, xn - 1)], sem_cols.at[i])
        cols[i, own_span(x), :] = flat[i, x]
        for xx in range(1, xn):
            other = lax.rem(x + xx, xn)
            pieces = [
                far_rows[s, i, other, b].astype(f32) for b in range(cn) for s in range(sources)
            ]
            cols[i, own_span(other), :] = jnp.concatenate(pieces, axis=0).astype(bf16)
        flat_t[i] = cols[i].T

    def column(i, h, b):
        c = i * own_heads + h
        return jnp.broadcast_to(route_columns[b, :seq_len, c : c + 1], (seq_len, head_dim))

    def turn_routes(b):
        lines = jnp.concatenate([routes[b, c] for c in range(2 * own_heads)], axis=0)
        spare = route_columns.shape[1] - seq_len
        if spare:
            lines = jnp.concatenate([lines, jnp.zeros((2 * own_heads, spare), jnp.int32)], axis=1)
        route_columns[b] = lines.T

    def project(i):
        for h in range(own_heads):
            picked = [jnp.zeros((seq_len, head_dim), f32) for _ in range(cn)]
            for e in range(0, E, 2):
                p = h * E + e
                every = jnp.zeros((cn * seq_len, 2 * head_dim), f32)
                for q in range(xn):
                    both = jnp.concatenate([weight[i, p, q], weight[i, p + 1, q]], axis=1)
                    every = every + jnp.dot(flat[i, q], both, preferred_element_type=f32)
                for b in range(cn):
                    own_part = every[b * seq_len : (b + 1) * seq_len]
                    route = column(i, h, x * cn + b)
                    picked[b] = jnp.where(route == e, own_part[:, :head_dim], picked[b])
                    picked[b] = jnp.where(route == e + 1, own_part[:, head_dim:], picked[b])
            for b in range(cn):
                part[b, i, h] = picked[b].astype(bf16)
            if (h + 1) % group == 0:
                heads = pl.ds(h + 1 - group, group)
                for cc in range(1, cn):
                    send(
                        "part",
                        part.at[near(cc), i, heads],
                        part_in.at[cc, i, heads],
                        sem_part.at[i],
                        place_near(cc),
                    )

    def place_near(cc):
        return {"dp": x * cn + near(cc), "head": g, "expert": j}

    query_pos = lax.broadcasted_iota(jnp.int32, (seq_len, seq_len), 0)
    key_pos = lax.broadcasted_iota(jnp.int32, (seq_len, seq_len), 1)
    causal = key_pos <= query_pos

    def joined(i, h):
        return jnp.concatenate([heads_in[i, jj, h] for jj in range(jn)], axis=0)

    def total(i, h):
        whole = part[c, i, h].astype(f32)
        for cc in range(1, cn):
            whole = whole + part_in[cc, i, h].astype(f32)
        return whole.astype(bf16)

    def across_rows(a, b):
        return lax.dot_general(a, b, (((1,), (1,)), ((), ())), preferred_element_type=f32)

    def over_rows(a, b):
        return lax.dot_general(a, b, (((0,), (0,)), ((), ())), preferred_element_type=f32)

    def mask(i, groups_x):
        for xx in groups_x:
            for h in range(own_heads):
                for cc in range(cn):
                    b = lax.rem(x + xx, xn) * cn + cc
                    source = factor[b, i, h].astype(f32)
                    route = column(i, h, b)
                    line = pl.ds(pl.multiple_of(b * seq_len, seq_len), seq_len)
                    for e in range(E):
                        p = h * E + e
                        masked[
                            i, p // 2, line, (p % 2) * head_dim : (p % 2 + 1) * head_dim
                        ] = jnp.where(route == e, source, 0.0).astype(bf16)

    def spread(i):
        for cc in range(1, cn):
            send("factor", factor.at[d, i], factor.at[d, i], sem_factor.at[i, 0], place_near(cc))
        for xx in range(1, xn):
            send("factor", factor.at[d, i], factor.at[d, i], sem_factor.at[i, 1], across(xx, 0))

    def near_factor(i):
        arrived(factor.at[pl.ds(0, cn - 1), i], sem_factor.at[i, 0])

    def hand_over(i):
        arrived(factor.at[pl.ds(0, xn - 1), i], sem_factor.at[i, 1])
        for xx in range(1, xn):
            came = factor.at[lax.rem(x + xx, xn) * cn + c, i]
            for cc in range(1, cn):
                send("factor", came, came, sem_factor.at[i, 2], place_near(cc))

    def far_factor(i):
        arrived(factor.at[pl.ds(0, (xn - 1) * (cn - 1)), i], sem_factor.at[i, 2])

    arrived(heads_in.at[:, pl.ds(0, jn - 1)], sem_heads.at[0])
    for h in range(own_heads):
        query, key = joined(0, h), joined(1, h)
        scores = across_rows(query, key) * scale
        top = jnp.max(jnp.where(causal, scores, -jnp.inf), axis=-1, keepdims=True)
        soft = jnp.where(causal, jnp.exp(scores - top), 0.0)
        prob_keep[h] = soft / jnp.sum(soft, axis=-1, keepdims=True)
    arrived(routes.at[pl.ds(0, dn - 1)], sem_routes.at[0])
    for b in range(dn):
        turn_routes(b)
    from_side(1, slice(0, gn))
    flatten(1)
    relay(0, slice(1, 2))
    for copy in weights_on_way[:xn]:
        copy.wait()
    project(1)
    relay(0, slice(2, gn))
    arrived(part_in.at[pl.ds(0, cn - 1), 1], sem_part.at[1])
    for h in range(own_heads):
        upstream_keep[h] = total(1, h)
        factor[d, 0, h] = over_rows(prob_keep[h].astype(bf16), upstream_keep[h]).astype(bf16)
    spread(0)
    near_factor(0)
    mask(0, range(0, 1))
    for copy in weights_on_way[xn:]:
        copy.wait()
    couples = own_heads * E // 2
    step = min(width, 256)
    for q in range(xn):
        for n in range(0, width, step):
            added = jnp.zeros((cn * seq_len, step), f32)
            for m in range(couples):
                both = jnp.concatenate(
                    [weight[0, 2 * m, q, n : n + step, :], weight[0, 2 * m + 1, q, n : n + step, :]],
                    axis=1,
                )
                added = added + across_rows(masked[0, m, own_span(x), :], both)
            for b in range(cn):
                for r in range(sources):
                    first = b * seq_len + r * tok_rows
                    term[r % jn, r // jn, b, q, :, n : n + step] = added[
                        first : first + tok_rows
                    ].astype(bf16)
    for target in range(gn):
        for jj in range(1, jn):
            send(
                "half",
                term.at[lax.rem(j + jj, jn), target],
                term_side.at[jj, target],
                sem_half.at[target],
                at(0, 0, jj),
            )

    def join_halves(which, k):
        for target in range(gn)[which]:
            arrived(term_side.at[pl.ds(0, jn - 1), target], sem_half.at[target])
            whole = term[j, target].astype(f32)
            for jj in range(1, jn):
                whole = whole + term_side[jj, target].astype(f32)
            term_sum[target] = whole.astype(bf16)
            for cc in range(cn):
                if cc == 0 and target == k:
                    term_in[k * cn + c] = term_sum[k, c]
                else:
                    send(
                        "term",
                        term_sum.at[target, near(cc)],
                        term_in.at[g * cn + c],
                        sem_final.at[0],
                        place(cc, target),
                    )

    from_side(0, slice(0, gn))
    flatten(0)
    project(0)
    arrived(part_in.at[pl.ds(0, cn - 1), 0], sem_part.at[0])
    for h in range(own_heads):
        value, upstream, probs = total(0, h), upstream_keep[h], prob_keep[h]
        output = jnp.dot(probs.astype(bf16), value, preferred_element_type=f32).astype(bf16)
        factor[d, 1, h] = output
        delta = jnp.sum(output.astype(f32) * upstream.astype(f32), axis=-1, keepdims=True)
        score_keep[h] = (probs * (across_rows(upstream, value) - delta)).astype(bf16)
    spread(1)
    on_line(functools.partial(join_halves, slice(0, 1)))
    for h in range(own_heads):
        query, key, score = joined(0, h), joined(1, h), score_keep[h]
        query_grad = (jnp.dot(score, key, preferred_element_type=f32) * scale).astype(bf16)
        key_grad = (over_rows(score, query) * scale).astype(bf16)
        for jj in range(jn):
            back[jj, 0, h] = query_grad[jj * query_rows : (jj + 1) * query_rows]
            back[jj, 1, h] = key_grad[jj * query_rows : (jj + 1) * query_rows]
    for jj in range(1, jn):
        send("back", back.at[lax.rem(j + jj, jn)], back_in.at[j], sem_back.at[0], at(0, 0, jj))

    def gradients(i, out):
        for m in range(couples):
            whole = jnp.dot(flat_t[i], masked[i, m], preferred_element_type=f32)
            out[2 * m] = whole[:, :head_dim].astype(bf16)
            out[2 * m + 1] = whole[:, head_dim:].astype(bf16)


    hand_over(0)
    on_line(functools.partial(join_halves, slice(1, 2)))
    far_factor(0)
    mask(0, range(1, xn))
    on_line(functools.partial(join_halves, slice(2, gn - 1)))
    gather_columns(0)
    hand_over(1)
    on_line(functools.partial(join_halves, slice(gn - 1, gn)))
    gradients(0, vg_out)
    near_factor(1)
    mask(1, range(0, 1))
    gather_columns(1)
    far_factor(1)
    mask(1, range(1, xn))
    gradients(1, og_out)

    back_in[j] = back[j]
    arrived(back_in.at[pl.ds(0, jn - 1)], sem_back.at[0])
    for jj in range(jn):
        qg_out[jj] = back_in[jj, 0]
        kg_out[jj] = back_in[jj, 1]
    all_terms = term_in.at[pl.ds(0, len(others))]
    arrived(all_terms, sem_final.at[0])
    for b in range(cn):
        for q in range(xn):
            total_rows = term_in[b, q].astype(f32)
            for s in range(1, gn):
                total_rows = total_rows + term_in[s * cn + b, q].astype(f32)
            n = (q * cn + b) * width
            tok_out[:, n : n + width] = total_rows.astype(bf16)
    left("term", all_terms)

    def left_line(k):
        for i, kind in enumerate(("tok", "cot")):
            left(kind, term_in.at[pl.ds(0, cn - 1 + cn * len(plans[i][1][k]))])
        count = sum(len(plan[2][k]) for plan in plans)
        if count:
            left("onward", rows.at[pl.ds(0, count), 0])

    on_line(left_line)
    left("routes", routes.at[pl.ds(0, dn - 1)])
    left("side", rows.at[pl.ds(0, gn * (jn - 1))])
    left("heads", heads_in.at[:, pl.ds(0, jn - 1)])
    left("part", part_in.at[pl.ds(0, cn - 1)])
    left("cols", far_rows.at[:, :, pl.ds(0, xn - 1)])
    left("factor", factor.at[pl.ds(0, dn - 1)])
    left("half", term_side.at[pl.ds(0, jn - 1)])
    left("back", back_in.at[pl.ds(0, jn - 1)])


def finish_kernel(
    tok_in, qg_in, kg_in, vg_in, og_in, tok_out, qg_out, kg_out, vg_out, og_out, turned, sems
):
    pieces = E
    size = vg_in.shape[0] // pieces
    whole = [
        pltpu.make_async_copy(source, out, sems.at[i])
        for i, (source, out) in enumerate(((vg_in, vg_out), (og_in, og_out), (tok_in, tok_out)))
    ]
    for i, (source, out) in enumerate(((vg_in, vg_out), (og_in, og_out))):
        for n in range(pieces):
            part = pl.ds(n * size, size)
            pltpu.make_async_copy(source.at[part], out.at[part], sems.at[i]).start()
    whole[2].start()
    for i, (source, out) in enumerate(((qg_in, qg_out), (kg_in, kg_out))):
        turned[i] = jnp.transpose(source[...].astype(jnp.float32), (1, 0, 2)).astype(out.dtype)
        whole.append(pltpu.make_async_copy(turned.at[i], out, sems.at[3 + i]))
        whole[3 + i].start()
    for copy in whole:
        copy.wait()


def fused(
    tokens,
    cotangent,
    queries,
    key_vectors,
    value_routes,
    output_routes,
    value_experts,
    output_experts,
):
    dn, gn, jn = lax.axis_size("dp"), lax.axis_size("head"), lax.axis_size("expert")
    _, tok_rows, model_width = tokens.shape
    width = model_width // dn
    _, query_rows, groups, head_dim = queries.shape
    seq_len = value_routes.shape[2]
    pairs_dev = value_experts.shape[0]
    own_heads = groups // jn
    sources = gn * jn
    xn = dn // NEAR
    bf16 = jnp.bfloat16

    value_lines = value_routes.reshape(groups, 1, seq_len)
    output_lines = output_routes.reshape(groups, 1, seq_len)

    vmem = pl.BlockSpec(memory_space=pltpu.VMEM)
    hbm = pl.BlockSpec(memory_space=pl.ANY)
    dma = pltpu.SemaphoreType.DMA
    head_block = (jn, own_heads, query_rows, head_dim)
    grad_shape = jax.ShapeDtypeStruct((pairs_dev, width, head_dim), bf16)
    tok_grads, query_grads, key_grads, value_grads, output_grads = pl.pallas_call(
        functools.partial(
            fused_kernel, (dn, gn, jn, own_heads, query_rows, tok_rows, width, head_dim)
        ),
        name="fused",
        out_shape=(
            pltpu.VMEM((tok_rows, model_width), bf16),
            pltpu.VMEM(head_block, bf16),
            pltpu.VMEM(head_block, bf16),
            pltpu.VMEM(grad_shape.shape, bf16),
            pltpu.VMEM(grad_shape.shape, bf16),
        ),
        in_specs=[hbm] * 8,
        out_specs=(vmem,) * 5,
        scratch_shapes=[
            pltpu.VMEM((sources, 2, NEAR, xn, tok_rows, width), bf16),
            pltpu.VMEM((sources, 2, xn, NEAR, tok_rows, width), bf16),
            pltpu.VMEM((2, xn, NEAR * seq_len, width), bf16),
            pltpu.VMEM((2, dn * seq_len, width), bf16),
            pltpu.VMEM((2, width, dn * seq_len), bf16),
            pltpu.VMEM((2, query_rows, groups, head_dim), bf16),
            pltpu.VMEM((2, jn, own_heads, query_rows, head_dim), bf16),
            pltpu.VMEM((dn, 2 * own_heads, 1, seq_len), jnp.int32),
            pltpu.VMEM((dn, -(-seq_len // 128) * 128, 2 * own_heads), jnp.int32),
            pltpu.VMEM((2, pairs_dev, xn, width, head_dim), bf16),
            pltpu.VMEM((2, jn, own_heads, query_rows, head_dim), bf16),
            pltpu.VMEM((NEAR, 2, own_heads, seq_len, head_dim), bf16),
            pltpu.VMEM((NEAR, 2, own_heads, seq_len, head_dim), bf16),
            pltpu.VMEM((dn, 2, own_heads, seq_len, head_dim), bf16),
            pltpu.VMEM((2, pairs_dev // 2, dn * seq_len, 2 * head_dim), bf16),
            pltpu.VMEM((own_heads, seq_len, seq_len), bf16),
            pltpu.VMEM((own_heads, seq_len, seq_len), jnp.float32),
            pltpu.VMEM((own_heads, seq_len, head_dim), bf16),
            pltpu.VMEM((jn, 2, own_heads, query_rows, head_dim), bf16),
            pltpu.VMEM((jn, 2, own_heads, query_rows, head_dim), bf16),
            pltpu.VMEM((jn, gn, NEAR, xn, tok_rows, width), bf16),
            pltpu.VMEM((jn, gn, NEAR, xn, tok_rows, width), bf16),
            pltpu.VMEM((gn, NEAR, xn, tok_rows, width), bf16),
            pltpu.VMEM((gn * NEAR, xn, tok_rows, width), bf16),
            pltpu.VMEM((2, tok_rows, model_width), bf16),
            dma((2, xn)),
            dma((6 + 2 * xn,)),
            dma((len(KINDS),)),
            dma((gn, 2)),
            dma((gn, 2)),
            dma((1,)),
            dma((1,)),
            dma((2,)),
            dma((2, 3)),
            dma((2,)),
            dma((1,)),
            dma((gn,)),
            dma((1,)),
        ],
        compiler_params=pltpu.CompilerParams(
            collective_id=0, has_side_effects=True, vmem_limit_bytes=44 * 1024 * 1024
        ),
    )(
        *(
            pltpu.with_memory_space_constraint(x, pltpu.HBM)
            for x in (
                tokens[0],
                cotangent[0],
                queries[0],
                key_vectors[0],
                value_lines,
                output_lines,
            )
        ),
        value_experts,
        output_experts,
    )

    by_head = (groups, query_rows, head_dim)
    row_shape = jax.ShapeDtypeStruct((query_rows, groups, head_dim), bf16)
    tok_grads, query_grads, key_grads, value_grads, output_grads = pl.pallas_call(
        finish_kernel,
        name="finish",
        out_shape=(
            jax.ShapeDtypeStruct((tok_rows, model_width), bf16),
            row_shape,
            row_shape,
            grad_shape,
            grad_shape,
        ),
        in_specs=[vmem] * 5,
        out_specs=(hbm,) * 5,
        scratch_shapes=[
            pltpu.VMEM((2, query_rows, groups, head_dim), bf16),
            dma((5,)),
        ],
        compiler_params=pltpu.CompilerParams(vmem_limit_bytes=8 * 1024 * 1024),
    )(
        tok_grads,
        query_grads.reshape(by_head),
        key_grads.reshape(by_head),
        value_grads,
        output_grads,
    )
    return tok_grads[None], query_grads[None], key_grads[None], value_grads, output_grads


def chosen(*args):
    groups, pairs_dev = args[2].shape[2], args[6].shape[0]
    dp_count, expert_count = lax.axis_size("dp"), lax.axis_size("expert")
    whole_heads = groups % expert_count == 0 and pairs_dev == groups // expert_count * E
    small = args[4].shape[2] <= 128
    if whole_heads and small and expert_count > 1 and dp_count % NEAR == 0 and dp_count > NEAR and args[0].shape[2] % (dp_count * 256) == 0:
        return fused(*args)
    return local(*args)


def solution(mesh):
    return jax.shard_map(
        chosen,
        mesh=mesh,
        in_specs=(
            P("dp", ("head", "expert"), None),
            P("dp", ("head", "expert"), None),
            P("dp", "expert", "head", None),
            P("dp", "expert", "head", None),
            P("dp", "head", None, None),
            P("dp", "head", None, None),
            P(("head", "expert"), None, None),
            P(("head", "expert"), None, None),
        ),
        out_specs=(
            P("dp", ("head", "expert"), None),
            P("dp", "expert", "head", None),
            P("dp", "expert", "head", None),
            P(("head", "expert"), "dp", None),
            P(("head", "expert"), "dp", None),
        ),
        check_vma=False,
    )
```

```python
import functools

import jax
import jax.numpy as jnp
from jax import lax
from jax.experimental import pallas as pl
from jax.experimental.pallas import tpu as pltpu
from jax.sharding import PartitionSpec as P

E = 4
CAP = 3


def slot_rank(routes):
    places = jnp.arange(routes.shape[-1], dtype=jnp.int32)
    same = routes[..., :, None] == routes[..., None, :]
    return jnp.sum(jnp.logical_and(same, places[None, :] < places[:, None]).astype(jnp.int32), axis=-1)


def slot_table(routes):
    rank_of = slot_rank(routes)
    expert_hit = routes[..., None, None, :] == jnp.arange(E, dtype=jnp.int32)[:, None, None]
    place_hit = rank_of[..., None, None, :] == jnp.arange(CAP, dtype=jnp.int32)[:, None]
    return jnp.logical_and(expert_hit, place_hit).astype(jnp.bfloat16)


def local(
    tokens,
    cotangent,
    queries,
    key_vectors,
    value_routes,
    output_routes,
    value_experts,
    output_experts,
):
    head_count = lax.axis_size("head")
    expert_count = lax.axis_size("expert")
    sources = head_count * expert_count
    expert_index = lax.axis_index("expert")
    tok_rows = tokens.shape[1]
    model_width = tokens.shape[2]
    query_rows = queries.shape[1]
    groups = queries.shape[2]
    head_dim = queries.shape[3]
    seq_len = value_routes.shape[2]
    pairs_dev = value_experts.shape[0]
    slot_count = sources * CAP
    score_scale = head_dim ** (-0.5)
    value_local = value_routes[0, :, :, 0]
    output_local = output_routes[0, :, :, 0]

    def own_block(route_part):
        shaped = route_part.reshape(groups, head_count, expert_count, tok_rows)
        return lax.dynamic_index_in_dim(shaped, expert_index, 2, keepdims=False)

    own_pair = jnp.stack([own_block(value_local), own_block(output_local)])
    own_routes = lax.all_to_all(own_pair, "head", split_axis=2, concat_axis=1, tiled=True).reshape(
        2, groups * head_count, tok_rows
    )
    value_table = slot_table(own_routes[0]).reshape(
        head_count, expert_count, pairs_dev, CAP, tok_rows
    )

    def pair_rows(route_part, gathered):
        slot_map = slot_table(route_part.reshape(groups, sources, tok_rows))
        slot_map = jnp.moveaxis(slot_map, 2, 1).reshape(groups * E, sources, CAP, tok_rows)
        slot_map = lax.dynamic_slice_in_dim(slot_map, expert_index * pairs_dev, pairs_dev, 0)
        picked = jnp.einsum(
            "psmt,stw->psmw",
            slot_map,
            gathered.reshape(sources, tok_rows, model_width),
            preferred_element_type=jnp.float32,
        )
        return picked.astype(jnp.bfloat16).reshape(pairs_dev, slot_count, model_width)

    whole_tokens, whole_cotangent = (
        lax.all_gather(tokens[0], ("head", "expert"), axis=0, tiled=True),
        lax.all_gather(cotangent[0], ("head", "expert"), axis=0, tiled=True),
    )
    token_slots = pair_rows(value_local, whole_tokens)
    cotangent_slots = pair_rows(output_local, whole_cotangent)
    value_slots = jnp.einsum(
        "prw,pwk->prk", token_slots, value_experts, preferred_element_type=jnp.float32
    ).astype(jnp.bfloat16)
    upstream_slots = jnp.einsum(
        "prw,pwk->prk", cotangent_slots, output_experts, preferred_element_type=jnp.float32
    ).astype(jnp.bfloat16)
    query_start = expert_index * query_rows
    group_values, group_upstream, all_keys = (
        lax.all_gather(value_slots, "expert", axis=0, tiled=True),
        lax.all_gather(upstream_slots, "expert", axis=0, tiled=True),
        lax.all_gather(key_vectors[0], "expert", axis=0, tiled=True),
    )
    token_source = jnp.arange(seq_len, dtype=jnp.int32) // tok_rows
    head_base = jnp.arange(groups, dtype=jnp.int32)[:, None] * E
    value_rank = slot_rank(value_local.reshape(groups, sources, tok_rows)).reshape(groups, seq_len)
    value_index = (head_base + value_local) * slot_count + token_source * CAP + value_rank
    value_rows = group_values.reshape(-1, head_dim)[value_index]
    output_rank = slot_rank(output_local.reshape(groups, sources, tok_rows)).reshape(
        groups, seq_len
    )
    block_routes = lax.dynamic_slice_in_dim(output_local, query_start, query_rows, 1)
    block_rank = lax.dynamic_slice_in_dim(output_rank, query_start, query_rows, 1)
    block_source = lax.dynamic_slice_in_dim(token_source, query_start, query_rows, 0)
    upstream_index = (head_base + block_routes) * slot_count + block_source * CAP + block_rank
    upstream_rows = group_upstream.reshape(-1, head_dim)[upstream_index]
    query_own = queries[0]
    scores = (
        jnp.einsum("ihc,jhc->hij", query_own, all_keys, preferred_element_type=jnp.float32)
        * score_scale
    )
    query_pos = query_start + jnp.arange(query_rows, dtype=jnp.int32)
    causal = jnp.arange(seq_len, dtype=jnp.int32)[None, :] <= query_pos[:, None]
    row_top = jnp.max(jnp.where(causal, scores, -jnp.inf), axis=-1, keepdims=True)
    weights = jnp.where(causal, jnp.exp(scores - row_top), 0.0)
    probs_full = weights / jnp.sum(weights, axis=-1, keepdims=True)
    prob_half = probs_full.astype(jnp.bfloat16)
    outputs = jnp.einsum(
        "hij,hjc->hic", prob_half, value_rows, preferred_element_type=jnp.float32
    ).astype(jnp.bfloat16)
    row_delta = jnp.sum(outputs.astype(jnp.float32) * upstream_rows.astype(jnp.float32), axis=-1)
    prob_grads = jnp.einsum(
        "hic,hjc->hij", upstream_rows, value_rows, preferred_element_type=jnp.float32
    )
    score_grads = (probs_full * (prob_grads - row_delta[:, :, None])).astype(jnp.bfloat16)
    query_grads = (
        jnp.einsum("hij,jhc->ihc", score_grads, all_keys, preferred_element_type=jnp.float32)
        * score_scale
    ).astype(jnp.bfloat16)
    key_part = (
        jnp.einsum("hij,ihc->jhc", score_grads, query_own, preferred_element_type=jnp.float32)
        * score_scale
    )
    value_part = jnp.einsum(
        "hij,hic->jhc", prob_half, upstream_rows, preferred_element_type=jnp.float32
    )
    key_sum, value_sum = (
        lax.psum_scatter(key_part, "expert", scatter_dimension=0, tiled=True),
        lax.psum_scatter(value_part, "expert", scatter_dimension=0, tiled=True),
    )
    value_half = value_sum.astype(jnp.bfloat16)
    block_value_routes = lax.dynamic_slice_in_dim(value_local, query_start, query_rows, 1).reshape(
        groups, head_count, tok_rows
    )
    value_place = slot_table(block_value_routes)
    output_place = slot_table(block_routes.reshape(groups, head_count, tok_rows))
    value_send = jnp.einsum(
        "hsemt,sthc->hesmc",
        value_place,
        value_half.reshape(head_count, tok_rows, groups, head_dim),
        preferred_element_type=jnp.float32,
    )
    value_send = value_send.astype(jnp.bfloat16).reshape(groups * E, head_count * CAP, head_dim)
    output_send = jnp.einsum(
        "hsemt,hstc->hesmc",
        output_place,
        outputs.reshape(groups, head_count, tok_rows, head_dim),
        preferred_element_type=jnp.float32,
    )
    output_send = output_send.astype(jnp.bfloat16).reshape(groups * E, head_count * CAP, head_dim)
    output_slots, grad_slots = (
        lax.all_to_all(output_send, "expert", split_axis=0, concat_axis=1, tiled=True),
        lax.all_to_all(value_send, "expert", split_axis=0, concat_axis=1, tiled=True),
    )
    value_term = jnp.einsum(
        "prw,prk->pwk", token_slots, grad_slots, preferred_element_type=jnp.float32
    )
    output_term = jnp.einsum(
        "prw,prk->pwk", cotangent_slots, output_slots, preferred_element_type=jnp.float32
    )
    value_grads, output_grads = (
        lax.psum_scatter(
            value_term.astype(jnp.bfloat16), "dp", scatter_dimension=1, tiled=True
        ).astype(jnp.float32),
        lax.psum_scatter(
            output_term.astype(jnp.bfloat16), "dp", scatter_dimension=1, tiled=True
        ).astype(jnp.float32),
    )
    token_terms = jnp.einsum(
        "prk,pwk->prw", grad_slots, value_experts, preferred_element_type=jnp.float32
    ).astype(jnp.bfloat16)
    returned = lax.all_to_all(
        token_terms.reshape(pairs_dev, sources, CAP, model_width),
        ("head", "expert"),
        split_axis=1,
        concat_axis=0,
        tiled=True,
    )
    returned = returned.reshape(head_count, expert_count, pairs_dev, CAP, model_width)
    token_grads = jnp.einsum(
        "gjpmt,gjpmw->tw", value_table, returned, preferred_element_type=jnp.float32
    )
    return (
        token_grads.astype(jnp.bfloat16)[None],
        query_grads[None],
        key_sum.astype(jnp.bfloat16)[None],
        value_grads.astype(jnp.bfloat16),
        output_grads.astype(jnp.bfloat16),
    )


def line_plan(gn):
    order = [sorted(range(gn), key=lambda t: (abs(t - k), t)) for k in range(gn)]
    plain = (order, [row[1:] for row in order], [{} for _ in range(gn)])
    if gn != 4:
        return plain, plain
    passed = (
        [[0, 1, 3, 2], [1, 2, 0, 3], [2, 1, 3, 0], [3, 2, 0, 1]],
        [[1, 2, 3], [2, 0], [1, 3], [2, 1, 0]],
        [{}, {2: 0}, {1: 3}, {}],
    )
    return plain, passed


KINDS = (
    "tok",
    "cot",
    "onward",
    "routes",
    "side",
    "heads",
    "part",
    "factor",
    "cols",
    "half",
    "term",
    "back",
)
NEAR = 2


def fused_kernel(
    sizes,
    tok,
    cot,
    q_in,
    k_in,
    value_routes_in,
    output_routes_in,
    value_hbm,
    output_hbm,
    tok_out,
    qg_out,
    kg_out,
    vg_out,
    og_out,
    rows,
    far_rows,
    flat,
    cols,
    flat_t,
    heads_raw,
    by_heads,
    routes,
    route_columns,
    weight,
    turned_weight,
    heads_in,
    part,
    part_in,
    factor,
    masked,
    score_keep,
    prob_keep,
    upstream_keep,
    back,
    back_in,
    term,
    term_side,
    term_sum,
    term_in,
    own_rows,
    sem_weight,
    sem_own,
    sem_sent,
    sem_block,
    sem_side,
    sem_routes,
    sem_heads,
    sem_part,
    sem_factor,
    sem_cols,
    sem_back,
    sem_half,
    sem_final,
):
    dn, gn, jn, own_heads, query_rows, tok_rows, width, head_dim = sizes
    sources = gn * jn
    cn, xn = NEAR, dn // NEAR
    seq_len = sources * tok_rows
    scale = head_dim ** (-0.5)
    group = own_heads // 2 if own_heads % 2 == 0 else own_heads
    d, g, j = lax.axis_index("dp"), lax.axis_index("head"), lax.axis_index("expert")
    block = g * jn + j
    x, c = d // cn, lax.rem(d, cn)
    f32, bf16 = jnp.float32, jnp.bfloat16

    def at(dd, gg, jj):
        return {"dp": lax.rem(d + dd, dn), "head": lax.rem(g + gg, gn), "expert": lax.rem(j + jj, jn)}

    def near(cc):
        return lax.rem(c + cc, cn)

    others = [(cc, gg) for gg in range(gn) for cc in range(cn) if (cc, gg) != (0, 0)]
    afar = [(xx, cc) for xx in range(1, xn) for cc in range(cn)]

    def across(xx, cc):
        return {"dp": lax.rem(x + xx, xn) * cn + near(cc), "head": g, "expert": j}

    def remote(kind, src, dst, recv_sem, where):
        return pltpu.make_async_remote_copy(
            src_ref=src,
            dst_ref=dst,
            send_sem=sem_sent.at[KINDS.index(kind)],
            recv_sem=recv_sem,
            device_id=where,
            device_id_type=pl.DeviceIdType.MESH,
        )

    def send(*args):
        remote(*args).start()

    def arrived(region, recv_sem):
        remote("tok", region, region, recv_sem, at(0, 0, 0)).wait_recv()

    def left(kind, region):
        remote(kind, region, region, sem_final.at[0], at(0, 0, 0)).wait_send()

    def columns(index):
        return pl.ds(pl.multiple_of(index * width, 128), width)

    weights_on_way = [
        pltpu.make_async_copy(
            hbm.at[:, columns(q * cn + c), :], weight.at[i, :, q], sem_weight.at[i, q]
        )
        for i, hbm in ((1, output_hbm), (0, value_hbm))
        for q in range(xn)
    ]
    own = [
        pltpu.make_async_copy(tok, own_rows.at[0], sem_own.at[0]),
        pltpu.make_async_copy(cot, own_rows.at[1], sem_own.at[1]),
        pltpu.make_async_copy(
            value_routes_in.at[pl.ds(j * own_heads, own_heads)],
            routes.at[d, pl.ds(0, own_heads)],
            sem_own.at[2],
        ),
        pltpu.make_async_copy(
            output_routes_in.at[pl.ds(j * own_heads, own_heads)],
            routes.at[d, pl.ds(own_heads, own_heads)],
            sem_own.at[3],
        ),
        pltpu.make_async_copy(q_in, heads_raw.at[0], sem_own.at[4]),
        pltpu.make_async_copy(k_in, heads_raw.at[1], sem_own.at[5]),
    ]
    own += [
        pltpu.make_async_copy(
            source.at[:, columns(q * cn + c)], rows.at[block, i, c, q], sem_own.at[6 + i * xn + q]
        )
        for i, source in enumerate((tok, cot))
        for q in range(xn)
    ]
    for copy in own:
        copy.start()

    barrier = pltpu.get_barrier_semaphore()

    def greet(where):
        pl.semaphore_signal(
            barrier, inc=1, device_id=where, device_id_type=pl.DeviceIdType.MESH
        )

    for cc, gg in others:
        greet({"dp": x * cn + near(cc), "head": lax.rem(g + gg, gn), "expert": j})
    for xx, cc in afar:
        greet(across(xx, cc))
    for jj in range(1, jn):
        greet(at(0, 0, jj))
    for copy in own[:2]:
        copy.wait()
    pl.semaphore_wait(barrier, len(others) + len(afar) + jn - 1)

    def on_line(body):
        for k in range(gn):
            pl.when(g == k)(functools.partial(body, k))

    plans = line_plan(gn)

    def place(cc, target):
        return {"dp": x * cn + near(cc), "head": jnp.int32(target), "expert": j}

    def share(i):
        def body(k):
            for target in [k] + plans[i][1][k]:
                for cc in range(cn):
                    for q in range(xn):
                        if cc or target != k:
                            send(
                                ("tok", "cot")[i],
                                own_rows.at[i, :, columns(q * cn + near(cc))],
                                rows.at[block, i, c, q],
                                sem_block.at[g, i],
                                place(cc, target),
                            )

        on_line(body)

    def exchange(i, source):
        for xx in range(1, xn):
            send(
                "cols",
                rows.at[source, i, :, lax.rem(x + xx, xn)],
                far_rows.at[source, i, x],
                sem_cols.at[i],
                across(xx, 0),
            )

    def relay(i, which):
        def body(k):
            for source in plans[i][0][k][which]:
                count = cn - 1 if source == k else cn
                here = rows.at[source * jn + j, i]
                if count:
                    arrived(here.at[pl.ds(0, count)], sem_block.at[source, i])
                onward = plans[i][2][k]
                if source in onward:
                    send("onward", here, here, sem_block.at[source, i], place(0, onward[source]))
                for jj in range(1, jn):
                    send("side", here, here, sem_side.at[source, i], at(0, 0, jj))
                exchange(i, source * jn + j)

        on_line(body)

    share(1)
    for copy in own[2:]:
        copy.wait()
    for dd in range(1, dn):
        send("routes", routes.at[d], routes.at[d], sem_routes.at[0], at(dd, 0, 0))
    for i in range(2):
        turned = jnp.transpose(heads_raw[i].astype(f32), (1, 0, 2)).astype(bf16)
        for jj in range(jn):
            by_heads[i, jj] = turned[jj * own_heads : (jj + 1) * own_heads]
        heads_in[i, j] = by_heads[i, j]
    for jj in range(1, jn):
        peer = lax.rem(j + jj, jn)
        for i in range(2):
            send("heads", by_heads.at[i, peer], heads_in.at[i, j], sem_heads.at[0], at(0, 0, jj))
    for copy in weights_on_way:
        copy.start()
    relay(1, slice(0, 2))
    share(0)
    relay(0, slice(0, 1))
    relay(1, slice(2, gn))

    def flatten(i):
        for b in range(cn):
            for q in range(xn):
                piece = jnp.concatenate(
                    [rows[s, i, b, q].astype(f32) for s in range(sources)], axis=0
                )
                flat[i, q, b * seq_len : (b + 1) * seq_len, :] = piece.astype(bf16)

    def own_span(place_x):
        return pl.ds(pl.multiple_of(place_x * cn * seq_len, cn * seq_len), cn * seq_len)

    def from_side(i, which):
        def body(k):
            for source in plans[i][0][k][which]:
                arrived(rows.at[pl.ds(0, jn - 1), i], sem_side.at[source, i])
                for jj in range(1, jn):
                    exchange(i, source * jn + lax.rem(j + jj, jn))

        on_line(body)

    def gather_columns(i):
        arrived(far_rows.at[:, i, pl.ds(0, xn - 1)], sem_cols.at[i])
        cols[i, own_span(x), :] = flat[i, x]
        for xx in range(1, xn):
            other = lax.rem(x + xx, xn)
            pieces = [
                far_rows[s, i, other, b].astype(f32) for b in range(cn) for s in range(sources)
            ]
            cols[i, own_span(other), :] = jnp.concatenate(pieces, axis=0).astype(bf16)
        flat_t[i] = cols[i].T

    def column(i, h, b):
        c = i * own_heads + h
        return jnp.broadcast_to(route_columns[b, :seq_len, c : c + 1], (seq_len, head_dim))

    def turn_routes(b):
        lines = jnp.concatenate([routes[b, c] for c in range(2 * own_heads)], axis=0)
        spare = route_columns.shape[1] - seq_len
        if spare:
            lines = jnp.concatenate([lines, jnp.zeros((2 * own_heads, spare), jnp.int32)], axis=1)
        route_columns[b] = lines.T

    def project(i):
        for h in range(own_heads):
            picked = [jnp.zeros((seq_len, head_dim), f32) for _ in range(cn)]
            for e in range(0, E, 2):
                p = h * E + e
                every = jnp.zeros((cn * seq_len, 2 * head_dim), f32)
                for q in range(xn):
                    both = jnp.concatenate([weight[i, p, q], weight[i, p + 1, q]], axis=1)
                    every = every + jnp.dot(flat[i, q], both, preferred_element_type=f32)
                for b in range(cn):
                    own_part = every[b * seq_len : (b + 1) * seq_len]
                    route = column(i, h, x * cn + b)
                    picked[b] = jnp.where(route == e, own_part[:, :head_dim], picked[b])
                    picked[b] = jnp.where(route == e + 1, own_part[:, head_dim:], picked[b])
            for b in range(cn):
                part[b, i, h] = picked[b].astype(bf16)
            if (h + 1) % group == 0:
                heads = pl.ds(h + 1 - group, group)
                for cc in range(1, cn):
                    send(
                        "part",
                        part.at[near(cc), i, heads],
                        part_in.at[cc, i, heads],
                        sem_part.at[i],
                        place_near(cc),
                    )

    def place_near(cc):
        return {"dp": x * cn + near(cc), "head": g, "expert": j}

    query_pos = lax.broadcasted_iota(jnp.int32, (seq_len, seq_len), 0)
    key_pos = lax.broadcasted_iota(jnp.int32, (seq_len, seq_len), 1)
    causal = key_pos <= query_pos

    def joined(i, h):
        return jnp.concatenate([heads_in[i, jj, h] for jj in range(jn)], axis=0)

    def total(i, h):
        whole = part[c, i, h].astype(f32)
        for cc in range(1, cn):
            whole = whole + part_in[cc, i, h].astype(f32)
        return whole.astype(bf16)

    def across_rows(a, b):
        return lax.dot_general(a, b, (((1,), (1,)), ((), ())), preferred_element_type=f32)

    def over_rows(a, b):
        return lax.dot_general(a, b, (((0,), (0,)), ((), ())), preferred_element_type=f32)

    def mask(i, groups_x):
        for xx in groups_x:
            for h in range(own_heads):
                for cc in range(cn):
                    b = lax.rem(x + xx, xn) * cn + cc
                    source = factor[b, i, h].astype(f32)
                    route = column(i, h, b)
                    line = pl.ds(pl.multiple_of(b * seq_len, seq_len), seq_len)
                    for e in range(E):
                        p = h * E + e
                        masked[
                            i, p // 2, line, (p % 2) * head_dim : (p % 2 + 1) * head_dim
                        ] = jnp.where(route == e, source, 0.0).astype(bf16)

    def spread(i):
        for cc in range(1, cn):
            send("factor", factor.at[d, i], factor.at[d, i], sem_factor.at[i, 0], place_near(cc))
        for xx in range(1, xn):
            send("factor", factor.at[d, i], factor.at[d, i], sem_factor.at[i, 1], across(xx, 0))

    def near_factor(i):
        arrived(factor.at[pl.ds(0, cn - 1), i], sem_factor.at[i, 0])

    def hand_over(i):
        arrived(factor.at[pl.ds(0, xn - 1), i], sem_factor.at[i, 1])
        for xx in range(1, xn):
            came = factor.at[lax.rem(x + xx, xn) * cn + c, i]
            for cc in range(1, cn):
                send("factor", came, came, sem_factor.at[i, 2], place_near(cc))

    def far_factor(i):
        arrived(factor.at[pl.ds(0, (xn - 1) * (cn - 1)), i], sem_factor.at[i, 2])

    arrived(heads_in.at[:, pl.ds(0, jn - 1)], sem_heads.at[0])
    for h in range(own_heads):
        query, key = joined(0, h), joined(1, h)
        scores = across_rows(query, key) * scale
        top = jnp.max(jnp.where(causal, scores, -jnp.inf), axis=-1, keepdims=True)
        soft = jnp.where(causal, jnp.exp(scores - top), 0.0)
        prob_keep[h] = soft / jnp.sum(soft, axis=-1, keepdims=True)
    arrived(routes.at[pl.ds(0, dn - 1)], sem_routes.at[0])
    for b in range(dn):
        turn_routes(b)
    for copy in weights_on_way[xn:]:
        copy.wait()
    for p in range(own_heads * E):
        for q in range(xn):
            turned_weight[p // 2, q, (p % 2) * head_dim : (p % 2 + 1) * head_dim, :] = weight[
                0, p, q
            ].T
    relay(0, slice(1, 2))
    from_side(1, slice(0, gn))
    flatten(1)
    for copy in weights_on_way[:xn]:
        copy.wait()
    project(1)
    relay(0, slice(2, gn))
    arrived(part_in.at[pl.ds(0, cn - 1), 1], sem_part.at[1])
    for h in range(own_heads):
        upstream_keep[h] = total(1, h)
        factor[d, 0, h] = over_rows(prob_keep[h].astype(bf16), upstream_keep[h]).astype(bf16)
    spread(0)
    near_factor(0)
    mask(0, range(0, 1))
    couples = own_heads * E // 2
    step = min(width, 256)
    for q in range(xn):
        for n in range(0, width, step):
            added = jnp.zeros((cn * seq_len, step), f32)
            for m in range(couples):
                added = added + jnp.dot(
                    masked[0, m, own_span(x), :],
                    turned_weight[m, q, :, n : n + step],
                    preferred_element_type=f32,
                )
            for b in range(cn):
                for r in range(sources):
                    first = b * seq_len + r * tok_rows
                    term[r % jn, r // jn, b, q, :, n : n + step] = added[
                        first : first + tok_rows
                    ].astype(bf16)
    for target in range(gn):
        for jj in range(1, jn):
            send(
                "half",
                term.at[lax.rem(j + jj, jn), target],
                term_side.at[jj, target],
                sem_half.at[target],
                at(0, 0, jj),
            )

    def join_halves(which, k):
        for target in range(gn)[which]:
            arrived(term_side.at[pl.ds(0, jn - 1), target], sem_half.at[target])
            whole = term[j, target].astype(f32)
            for jj in range(1, jn):
                whole = whole + term_side[jj, target].astype(f32)
            term_sum[target] = whole.astype(bf16)
            for cc in range(cn):
                if cc == 0 and target == k:
                    term_in[k * cn + c] = term_sum[k, c]
                else:
                    send(
                        "term",
                        term_sum.at[target, near(cc)],
                        term_in.at[g * cn + c],
                        sem_final.at[0],
                        place(cc, target),
                    )

    from_side(0, slice(0, gn))
    flatten(0)
    project(0)
    arrived(part_in.at[pl.ds(0, cn - 1), 0], sem_part.at[0])
    for h in range(own_heads):
        value, upstream, probs = total(0, h), upstream_keep[h], prob_keep[h]
        output = jnp.dot(probs.astype(bf16), value, preferred_element_type=f32).astype(bf16)
        factor[d, 1, h] = output
        delta = jnp.sum(output.astype(f32) * upstream.astype(f32), axis=-1, keepdims=True)
        score_keep[h] = (probs * (across_rows(upstream, value) - delta)).astype(bf16)
    spread(1)
    on_line(functools.partial(join_halves, slice(0, 1)))
    for h in range(own_heads):
        query, key, score = joined(0, h), joined(1, h), score_keep[h]
        query_grad = (jnp.dot(score, key, preferred_element_type=f32) * scale).astype(bf16)
        key_grad = (over_rows(score, query) * scale).astype(bf16)
        for jj in range(jn):
            back[jj, 0, h] = query_grad[jj * query_rows : (jj + 1) * query_rows]
            back[jj, 1, h] = key_grad[jj * query_rows : (jj + 1) * query_rows]
    for jj in range(1, jn):
        send("back", back.at[lax.rem(j + jj, jn)], back_in.at[j], sem_back.at[0], at(0, 0, jj))

    def gradients(i, out):
        for m in range(couples):
            whole = jnp.dot(flat_t[i], masked[i, m], preferred_element_type=f32)
            out[2 * m] = whole[:, :head_dim].astype(bf16)
            out[2 * m + 1] = whole[:, head_dim:].astype(bf16)


    hand_over(0)
    on_line(functools.partial(join_halves, slice(1, 2)))
    far_factor(0)
    mask(0, range(1, xn))
    on_line(functools.partial(join_halves, slice(2, gn - 1)))
    gather_columns(0)
    hand_over(1)
    gradients(0, vg_out)
    on_line(functools.partial(join_halves, slice(gn - 1, gn)))
    near_factor(1)
    mask(1, range(0, 1))
    gather_columns(1)
    far_factor(1)
    mask(1, range(1, xn))
    gradients(1, og_out)

    back_in[j] = back[j]
    arrived(back_in.at[pl.ds(0, jn - 1)], sem_back.at[0])
    for jj in range(jn):
        qg_out[jj] = back_in[jj, 0]
        kg_out[jj] = back_in[jj, 1]
    all_terms = term_in.at[pl.ds(0, len(others))]
    arrived(all_terms, sem_final.at[0])
    for b in range(cn):
        for q in range(xn):
            total_rows = term_in[b, q].astype(f32)
            for s in range(1, gn):
                total_rows = total_rows + term_in[s * cn + b, q].astype(f32)
            n = (q * cn + b) * width
            tok_out[:, n : n + width] = total_rows.astype(bf16)
    left("term", all_terms)

    def left_line(k):
        for i, kind in enumerate(("tok", "cot")):
            left(kind, term_in.at[pl.ds(0, cn - 1 + cn * len(plans[i][1][k]))])
        count = sum(len(plan[2][k]) for plan in plans)
        if count:
            left("onward", rows.at[pl.ds(0, count), 0])

    on_line(left_line)
    left("routes", routes.at[pl.ds(0, dn - 1)])
    left("side", rows.at[pl.ds(0, gn * (jn - 1))])
    left("heads", heads_in.at[:, pl.ds(0, jn - 1)])
    left("part", part_in.at[pl.ds(0, cn - 1)])
    left("cols", far_rows.at[:, :, pl.ds(0, xn - 1)])
    left("factor", factor.at[pl.ds(0, dn - 1)])
    left("half", term_side.at[pl.ds(0, jn - 1)])
    left("back", back_in.at[pl.ds(0, jn - 1)])


def finish_kernel(
    tok_in, qg_in, kg_in, vg_in, og_in, tok_out, qg_out, kg_out, vg_out, og_out, turned, sems
):
    pieces = E
    size = vg_in.shape[0] // pieces
    whole = [
        pltpu.make_async_copy(source, out, sems.at[i])
        for i, (source, out) in enumerate(((vg_in, vg_out), (og_in, og_out), (tok_in, tok_out)))
    ]
    for i, (source, out) in enumerate(((vg_in, vg_out), (og_in, og_out))):
        for n in range(pieces):
            part = pl.ds(n * size, size)
            pltpu.make_async_copy(source.at[part], out.at[part], sems.at[i]).start()
    whole[2].start()
    for i, (source, out) in enumerate(((qg_in, qg_out), (kg_in, kg_out))):
        turned[i] = jnp.transpose(source[...].astype(jnp.float32), (1, 0, 2)).astype(out.dtype)
        whole.append(pltpu.make_async_copy(turned.at[i], out, sems.at[3 + i]))
        whole[3 + i].start()
    for copy in whole:
        copy.wait()


def fused(
    tokens,
    cotangent,
    queries,
    key_vectors,
    value_routes,
    output_routes,
    value_experts,
    output_experts,
):
    dn, gn, jn = lax.axis_size("dp"), lax.axis_size("head"), lax.axis_size("expert")
    _, tok_rows, model_width = tokens.shape
    width = model_width // dn
    _, query_rows, groups, head_dim = queries.shape
    seq_len = value_routes.shape[2]
    pairs_dev = value_experts.shape[0]
    own_heads = groups // jn
    sources = gn * jn
    xn = dn // NEAR
    bf16 = jnp.bfloat16

    value_lines = value_routes.reshape(groups, 1, seq_len)
    output_lines = output_routes.reshape(groups, 1, seq_len)

    vmem = pl.BlockSpec(memory_space=pltpu.VMEM)
    hbm = pl.BlockSpec(memory_space=pl.ANY)
    dma = pltpu.SemaphoreType.DMA
    head_block = (jn, own_heads, query_rows, head_dim)
    grad_shape = jax.ShapeDtypeStruct((pairs_dev, width, head_dim), bf16)
    tok_grads, query_grads, key_grads, value_grads, output_grads = pl.pallas_call(
        functools.partial(
            fused_kernel, (dn, gn, jn, own_heads, query_rows, tok_rows, width, head_dim)
        ),
        name="fused",
        out_shape=(
            pltpu.VMEM((tok_rows, model_width), bf16),
            pltpu.VMEM(head_block, bf16),
            pltpu.VMEM(head_block, bf16),
            pltpu.VMEM(grad_shape.shape, bf16),
            pltpu.VMEM(grad_shape.shape, bf16),
        ),
        in_specs=[hbm] * 8,
        out_specs=(vmem,) * 5,
        scratch_shapes=[
            pltpu.VMEM((sources, 2, NEAR, xn, tok_rows, width), bf16),
            pltpu.VMEM((sources, 2, xn, NEAR, tok_rows, width), bf16),
            pltpu.VMEM((2, xn, NEAR * seq_len, width), bf16),
            pltpu.VMEM((2, dn * seq_len, width), bf16),
            pltpu.VMEM((2, width, dn * seq_len), bf16),
            pltpu.VMEM((2, query_rows, groups, head_dim), bf16),
            pltpu.VMEM((2, jn, own_heads, query_rows, head_dim), bf16),
            pltpu.VMEM((dn, 2 * own_heads, 1, seq_len), jnp.int32),
            pltpu.VMEM((dn, -(-seq_len // 128) * 128, 2 * own_heads), jnp.int32),
            pltpu.VMEM((2, pairs_dev, xn, width, head_dim), bf16),
            pltpu.VMEM((pairs_dev // 2, xn, 2 * head_dim, width), bf16),
            pltpu.VMEM((2, jn, own_heads, query_rows, head_dim), bf16),
            pltpu.VMEM((NEAR, 2, own_heads, seq_len, head_dim), bf16),
            pltpu.VMEM((NEAR, 2, own_heads, seq_len, head_dim), bf16),
            pltpu.VMEM((dn, 2, own_heads, seq_len, head_dim), bf16),
            pltpu.VMEM((2, pairs_dev // 2, dn * seq_len, 2 * head_dim), bf16),
            pltpu.VMEM((own_heads, seq_len, seq_len), bf16),
            pltpu.VMEM((own_heads, seq_len, seq_len), jnp.float32),
            pltpu.VMEM((own_heads, seq_len, head_dim), bf16),
            pltpu.VMEM((jn, 2, own_heads, query_rows, head_dim), bf16),
            pltpu.VMEM((jn, 2, own_heads, query_rows, head_dim), bf16),
            pltpu.VMEM((jn, gn, NEAR, xn, tok_rows, width), bf16),
            pltpu.VMEM((jn, gn, NEAR, xn, tok_rows, width), bf16),
            pltpu.VMEM((gn, NEAR, xn, tok_rows, width), bf16),
            pltpu.VMEM((gn * NEAR, xn, tok_rows, width), bf16),
            pltpu.VMEM((2, tok_rows, model_width), bf16),
            dma((2, xn)),
            dma((6 + 2 * xn,)),
            dma((len(KINDS),)),
            dma((gn, 2)),
            dma((gn, 2)),
            dma((1,)),
            dma((1,)),
            dma((2,)),
            dma((2, 3)),
            dma((2,)),
            dma((1,)),
            dma((gn,)),
            dma((1,)),
        ],
        compiler_params=pltpu.CompilerParams(
            collective_id=0, has_side_effects=True, vmem_limit_bytes=48 * 1024 * 1024
        ),
    )(
        *(
            pltpu.with_memory_space_constraint(x, pltpu.HBM)
            for x in (
                tokens[0],
                cotangent[0],
                queries[0],
                key_vectors[0],
                value_lines,
                output_lines,
            )
        ),
        value_experts,
        output_experts,
    )

    by_head = (groups, query_rows, head_dim)
    row_shape = jax.ShapeDtypeStruct((query_rows, groups, head_dim), bf16)
    tok_grads, query_grads, key_grads, value_grads, output_grads = pl.pallas_call(
        finish_kernel,
        name="finish",
        out_shape=(
            jax.ShapeDtypeStruct((tok_rows, model_width), bf16),
            row_shape,
            row_shape,
            grad_shape,
            grad_shape,
        ),
        in_specs=[vmem] * 5,
        out_specs=(hbm,) * 5,
        scratch_shapes=[
            pltpu.VMEM((2, query_rows, groups, head_dim), bf16),
            dma((5,)),
        ],
        compiler_params=pltpu.CompilerParams(vmem_limit_bytes=8 * 1024 * 1024),
    )(
        tok_grads,
        query_grads.reshape(by_head),
        key_grads.reshape(by_head),
        value_grads,
        output_grads,
    )
    return tok_grads[None], query_grads[None], key_grads[None], value_grads, output_grads


def chosen(*args):
    groups, pairs_dev = args[2].shape[2], args[6].shape[0]
    dp_count, expert_count = lax.axis_size("dp"), lax.axis_size("expert")
    whole_heads = groups % expert_count == 0 and pairs_dev == groups // expert_count * E
    small = args[4].shape[2] <= 128
    if whole_heads and small and expert_count > 1 and dp_count % NEAR == 0 and dp_count > NEAR and args[0].shape[2] % (dp_count * 256) == 0:
        return fused(*args)
    return local(*args)


def solution(mesh):
    return jax.shard_map(
        chosen,
        mesh=mesh,
        in_specs=(
            P("dp", ("head", "expert"), None),
            P("dp", ("head", "expert"), None),
            P("dp", "expert", "head", None),
            P("dp", "expert", "head", None),
            P("dp", "head", None, None),
            P("dp", "head", None, None),
            P(("head", "expert"), None, None),
            P(("head", "expert"), None, None),
        ),
        out_specs=(
            P("dp", ("head", "expert"), None),
            P("dp", "expert", "head", None),
            P("dp", "expert", "head", None),
            P(("head", "expert"), "dp", None),
            P(("head", "expert"), "dp", None),
        ),
        check_vma=False,
    )
```

```python
import functools

import jax
import jax.numpy as jnp
from jax import lax
from jax.experimental import pallas as pl
from jax.experimental.pallas import tpu as pltpu
from jax.sharding import PartitionSpec as P

E = 4
CAP = 3


def slot_rank(routes):
    places = jnp.arange(routes.shape[-1], dtype=jnp.int32)
    same = routes[..., :, None] == routes[..., None, :]
    return jnp.sum(jnp.logical_and(same, places[None, :] < places[:, None]).astype(jnp.int32), axis=-1)


def slot_table(routes):
    rank_of = slot_rank(routes)
    expert_hit = routes[..., None, None, :] == jnp.arange(E, dtype=jnp.int32)[:, None, None]
    place_hit = rank_of[..., None, None, :] == jnp.arange(CAP, dtype=jnp.int32)[:, None]
    return jnp.logical_and(expert_hit, place_hit).astype(jnp.bfloat16)


def local(
    tokens,
    cotangent,
    queries,
    key_vectors,
    value_routes,
    output_routes,
    value_experts,
    output_experts,
):
    head_count = lax.axis_size("head")
    expert_count = lax.axis_size("expert")
    sources = head_count * expert_count
    expert_index = lax.axis_index("expert")
    tok_rows = tokens.shape[1]
    model_width = tokens.shape[2]
    query_rows = queries.shape[1]
    groups = queries.shape[2]
    head_dim = queries.shape[3]
    seq_len = value_routes.shape[2]
    pairs_dev = value_experts.shape[0]
    slot_count = sources * CAP
    score_scale = head_dim ** (-0.5)
    value_local = value_routes[0, :, :, 0]
    output_local = output_routes[0, :, :, 0]

    def own_block(route_part):
        shaped = route_part.reshape(groups, head_count, expert_count, tok_rows)
        return lax.dynamic_index_in_dim(shaped, expert_index, 2, keepdims=False)

    own_pair = jnp.stack([own_block(value_local), own_block(output_local)])
    own_routes = lax.all_to_all(own_pair, "head", split_axis=2, concat_axis=1, tiled=True).reshape(
        2, groups * head_count, tok_rows
    )
    value_table = slot_table(own_routes[0]).reshape(
        head_count, expert_count, pairs_dev, CAP, tok_rows
    )

    def pair_rows(route_part, gathered):
        slot_map = slot_table(route_part.reshape(groups, sources, tok_rows))
        slot_map = jnp.moveaxis(slot_map, 2, 1).reshape(groups * E, sources, CAP, tok_rows)
        slot_map = lax.dynamic_slice_in_dim(slot_map, expert_index * pairs_dev, pairs_dev, 0)
        picked = jnp.einsum(
            "psmt,stw->psmw",
            slot_map,
            gathered.reshape(sources, tok_rows, model_width),
            preferred_element_type=jnp.float32,
        )
        return picked.astype(jnp.bfloat16).reshape(pairs_dev, slot_count, model_width)

    whole_tokens, whole_cotangent = (
        lax.all_gather(tokens[0], ("head", "expert"), axis=0, tiled=True),
        lax.all_gather(cotangent[0], ("head", "expert"), axis=0, tiled=True),
    )
    token_slots = pair_rows(value_local, whole_tokens)
    cotangent_slots = pair_rows(output_local, whole_cotangent)
    value_slots = jnp.einsum(
        "prw,pwk->prk", token_slots, value_experts, preferred_element_type=jnp.float32
    ).astype(jnp.bfloat16)
    upstream_slots = jnp.einsum(
        "prw,pwk->prk", cotangent_slots, output_experts, preferred_element_type=jnp.float32
    ).astype(jnp.bfloat16)
    query_start = expert_index * query_rows
    group_values, group_upstream, all_keys = (
        lax.all_gather(value_slots, "expert", axis=0, tiled=True),
        lax.all_gather(upstream_slots, "expert", axis=0, tiled=True),
        lax.all_gather(key_vectors[0], "expert", axis=0, tiled=True),
    )
    token_source = jnp.arange(seq_len, dtype=jnp.int32) // tok_rows
    head_base = jnp.arange(groups, dtype=jnp.int32)[:, None] * E
    value_rank = slot_rank(value_local.reshape(groups, sources, tok_rows)).reshape(groups, seq_len)
    value_index = (head_base + value_local) * slot_count + token_source * CAP + value_rank
    value_rows = group_values.reshape(-1, head_dim)[value_index]
    output_rank = slot_rank(output_local.reshape(groups, sources, tok_rows)).reshape(
        groups, seq_len
    )
    block_routes = lax.dynamic_slice_in_dim(output_local, query_start, query_rows, 1)
    block_rank = lax.dynamic_slice_in_dim(output_rank, query_start, query_rows, 1)
    block_source = lax.dynamic_slice_in_dim(token_source, query_start, query_rows, 0)
    upstream_index = (head_base + block_routes) * slot_count + block_source * CAP + block_rank
    upstream_rows = group_upstream.reshape(-1, head_dim)[upstream_index]
    query_own = queries[0]
    scores = (
        jnp.einsum("ihc,jhc->hij", query_own, all_keys, preferred_element_type=jnp.float32)
        * score_scale
    )
    query_pos = query_start + jnp.arange(query_rows, dtype=jnp.int32)
    causal = jnp.arange(seq_len, dtype=jnp.int32)[None, :] <= query_pos[:, None]
    row_top = jnp.max(jnp.where(causal, scores, -jnp.inf), axis=-1, keepdims=True)
    weights = jnp.where(causal, jnp.exp(scores - row_top), 0.0)
    probs_full = weights / jnp.sum(weights, axis=-1, keepdims=True)
    prob_half = probs_full.astype(jnp.bfloat16)
    outputs = jnp.einsum(
        "hij,hjc->hic", prob_half, value_rows, preferred_element_type=jnp.float32
    ).astype(jnp.bfloat16)
    row_delta = jnp.sum(outputs.astype(jnp.float32) * upstream_rows.astype(jnp.float32), axis=-1)
    prob_grads = jnp.einsum(
        "hic,hjc->hij", upstream_rows, value_rows, preferred_element_type=jnp.float32
    )
    score_grads = (probs_full * (prob_grads - row_delta[:, :, None])).astype(jnp.bfloat16)
    query_grads = (
        jnp.einsum("hij,jhc->ihc", score_grads, all_keys, preferred_element_type=jnp.float32)
        * score_scale
    ).astype(jnp.bfloat16)
    key_part = (
        jnp.einsum("hij,ihc->jhc", score_grads, query_own, preferred_element_type=jnp.float32)
        * score_scale
    )
    value_part = jnp.einsum(
        "hij,hic->jhc", prob_half, upstream_rows, preferred_element_type=jnp.float32
    )
    key_sum, value_sum = (
        lax.psum_scatter(key_part, "expert", scatter_dimension=0, tiled=True),
        lax.psum_scatter(value_part, "expert", scatter_dimension=0, tiled=True),
    )
    value_half = value_sum.astype(jnp.bfloat16)
    block_value_routes = lax.dynamic_slice_in_dim(value_local, query_start, query_rows, 1).reshape(
        groups, head_count, tok_rows
    )
    value_place = slot_table(block_value_routes)
    output_place = slot_table(block_routes.reshape(groups, head_count, tok_rows))
    value_send = jnp.einsum(
        "hsemt,sthc->hesmc",
        value_place,
        value_half.reshape(head_count, tok_rows, groups, head_dim),
        preferred_element_type=jnp.float32,
    )
    value_send = value_send.astype(jnp.bfloat16).reshape(groups * E, head_count * CAP, head_dim)
    output_send = jnp.einsum(
        "hsemt,hstc->hesmc",
        output_place,
        outputs.reshape(groups, head_count, tok_rows, head_dim),
        preferred_element_type=jnp.float32,
    )
    output_send = output_send.astype(jnp.bfloat16).reshape(groups * E, head_count * CAP, head_dim)
    output_slots, grad_slots = (
        lax.all_to_all(output_send, "expert", split_axis=0, concat_axis=1, tiled=True),
        lax.all_to_all(value_send, "expert", split_axis=0, concat_axis=1, tiled=True),
    )
    value_term = jnp.einsum(
        "prw,prk->pwk", token_slots, grad_slots, preferred_element_type=jnp.float32
    )
    output_term = jnp.einsum(
        "prw,prk->pwk", cotangent_slots, output_slots, preferred_element_type=jnp.float32
    )
    value_grads, output_grads = (
        lax.psum_scatter(
            value_term.astype(jnp.bfloat16), "dp", scatter_dimension=1, tiled=True
        ).astype(jnp.float32),
        lax.psum_scatter(
            output_term.astype(jnp.bfloat16), "dp", scatter_dimension=1, tiled=True
        ).astype(jnp.float32),
    )
    token_terms = jnp.einsum(
        "prk,pwk->prw", grad_slots, value_experts, preferred_element_type=jnp.float32
    ).astype(jnp.bfloat16)
    returned = lax.all_to_all(
        token_terms.reshape(pairs_dev, sources, CAP, model_width),
        ("head", "expert"),
        split_axis=1,
        concat_axis=0,
        tiled=True,
    )
    returned = returned.reshape(head_count, expert_count, pairs_dev, CAP, model_width)
    token_grads = jnp.einsum(
        "gjpmt,gjpmw->tw", value_table, returned, preferred_element_type=jnp.float32
    )
    return (
        token_grads.astype(jnp.bfloat16)[None],
        query_grads[None],
        key_sum.astype(jnp.bfloat16)[None],
        value_grads.astype(jnp.bfloat16),
        output_grads.astype(jnp.bfloat16),
    )


def line_plan(gn):
    order = [sorted(range(gn), key=lambda t: (abs(t - k), t)) for k in range(gn)]
    plain = (order, [row[1:] for row in order], [{} for _ in range(gn)])
    if gn != 4:
        return plain, plain
    passed = (
        [[0, 1, 3, 2], [1, 2, 0, 3], [2, 1, 3, 0], [3, 2, 0, 1]],
        [[1, 2, 3], [2, 0], [1, 3], [2, 1, 0]],
        [{}, {2: 0}, {1: 3}, {}],
    )
    return plain, passed


KINDS = (
    "tok",
    "cot",
    "onward",
    "routes",
    "side",
    "heads",
    "part",
    "factor",
    "cols",
    "half",
    "term",
    "back",
)
NEAR = 2


def fused_kernel(
    sizes,
    tok,
    cot,
    q_in,
    k_in,
    value_routes_in,
    output_routes_in,
    value_hbm,
    output_hbm,
    tok_out,
    qg_out,
    kg_out,
    vg_out,
    og_out,
    rows,
    far_rows,
    flat,
    cols,
    flat_t,
    heads_raw,
    by_heads,
    routes,
    route_columns,
    weight,
    turned_weight,
    heads_in,
    part,
    part_in,
    factor,
    masked,
    score_keep,
    prob_keep,
    upstream_keep,
    back,
    back_in,
    term,
    term_side,
    term_sum,
    term_in,
    own_rows,
    sem_weight,
    sem_own,
    sem_sent,
    sem_block,
    sem_side,
    sem_routes,
    sem_heads,
    sem_part,
    sem_factor,
    sem_cols,
    sem_back,
    sem_half,
    sem_final,
):
    dn, gn, jn, own_heads, query_rows, tok_rows, width, head_dim = sizes
    sources = gn * jn
    cn, xn = NEAR, dn // NEAR
    seq_len = sources * tok_rows
    scale = head_dim ** (-0.5)
    group = own_heads // 2 if own_heads % 2 == 0 else own_heads
    d, g, j = lax.axis_index("dp"), lax.axis_index("head"), lax.axis_index("expert")
    block = g * jn + j
    x, c = d // cn, lax.rem(d, cn)
    f32, bf16 = jnp.float32, jnp.bfloat16

    def at(dd, gg, jj):
        return {"dp": lax.rem(d + dd, dn), "head": lax.rem(g + gg, gn), "expert": lax.rem(j + jj, jn)}

    def near(cc):
        return lax.rem(c + cc, cn)

    others = [(cc, gg) for gg in range(gn) for cc in range(cn) if (cc, gg) != (0, 0)]
    afar = [(xx, cc) for xx in range(1, xn) for cc in range(cn)]

    def across(xx, cc):
        return {"dp": lax.rem(x + xx, xn) * cn + near(cc), "head": g, "expert": j}

    def remote(kind, src, dst, recv_sem, where):
        return pltpu.make_async_remote_copy(
            src_ref=src,
            dst_ref=dst,
            send_sem=sem_sent.at[KINDS.index(kind)],
            recv_sem=recv_sem,
            device_id=where,
            device_id_type=pl.DeviceIdType.MESH,
        )

    def send(*args):
        remote(*args).start()

    def arrived(region, recv_sem):
        remote("tok", region, region, recv_sem, at(0, 0, 0)).wait_recv()

    def left(kind, region):
        remote(kind, region, region, sem_final.at[0], at(0, 0, 0)).wait_send()

    def columns(index):
        return pl.ds(pl.multiple_of(index * width, 128), width)

    weights_on_way = [
        pltpu.make_async_copy(
            hbm.at[:, columns(q * cn + c), :], weight.at[i, :, q], sem_weight.at[i, q]
        )
        for i, hbm in ((1, output_hbm), (0, value_hbm))
        for q in range(xn)
    ]
    own = [
        pltpu.make_async_copy(tok, own_rows.at[0], sem_own.at[0]),
        pltpu.make_async_copy(cot, own_rows.at[1], sem_own.at[1]),
        pltpu.make_async_copy(
            value_routes_in.at[pl.ds(j * own_heads, own_heads)],
            routes.at[d, pl.ds(0, own_heads)],
            sem_own.at[2],
        ),
        pltpu.make_async_copy(
            output_routes_in.at[pl.ds(j * own_heads, own_heads)],
            routes.at[d, pl.ds(own_heads, own_heads)],
            sem_own.at[3],
        ),
        pltpu.make_async_copy(q_in, heads_raw.at[0], sem_own.at[4]),
        pltpu.make_async_copy(k_in, heads_raw.at[1], sem_own.at[5]),
    ]
    own += [
        pltpu.make_async_copy(
            source.at[:, columns(q * cn + c)], rows.at[block, i, c, q], sem_own.at[6 + i * xn + q]
        )
        for i, source in enumerate((tok, cot))
        for q in range(xn)
    ]
    for copy in own:
        copy.start()

    barrier = pltpu.get_barrier_semaphore()

    def greet(where):
        pl.semaphore_signal(
            barrier, inc=1, device_id=where, device_id_type=pl.DeviceIdType.MESH
        )

    for cc, gg in others:
        greet({"dp": x * cn + near(cc), "head": lax.rem(g + gg, gn), "expert": j})
    for xx, cc in afar:
        greet(across(xx, cc))
    for jj in range(1, jn):
        greet(at(0, 0, jj))
    for copy in own[:2]:
        copy.wait()
    pl.semaphore_wait(barrier, len(others) + len(afar) + jn - 1)

    def on_line(body):
        for k in range(gn):
            pl.when(g == k)(functools.partial(body, k))

    plans = line_plan(gn)

    def place(cc, target):
        return {"dp": x * cn + near(cc), "head": jnp.int32(target), "expert": j}

    def share(i):
        def body(k):
            for target in [k] + plans[i][1][k]:
                for cc in range(cn):
                    for q in range(xn):
                        if cc or target != k:
                            send(
                                ("tok", "cot")[i],
                                own_rows.at[i, :, columns(q * cn + near(cc))],
                                rows.at[block, i, c, q],
                                sem_block.at[g, i],
                                place(cc, target),
                            )

        on_line(body)

    def exchange(i, source):
        for xx in range(1, xn):
            send(
                "cols",
                rows.at[source, i, :, lax.rem(x + xx, xn)],
                far_rows.at[source, i, x],
                sem_cols.at[i],
                across(xx, 0),
            )

    def relay(i, which):
        def body(k):
            for source in plans[i][0][k][which]:
                count = cn - 1 if source == k else cn
                here = rows.at[source * jn + j, i]
                if count:
                    arrived(here.at[pl.ds(0, count)], sem_block.at[source, i])
                onward = plans[i][2][k]
                if source in onward:
                    send("onward", here, here, sem_block.at[source, i], place(0, onward[source]))
                for jj in range(1, jn):
                    send("side", here, here, sem_side.at[source, i], at(0, 0, jj))
                exchange(i, source * jn + j)

        on_line(body)

    share(1)
    for copy in own[2:]:
        copy.wait()
    for dd in range(1, dn):
        send("routes", routes.at[d], routes.at[d], sem_routes.at[0], at(dd, 0, 0))
    for i in range(2):
        turned = jnp.transpose(heads_raw[i].astype(f32), (1, 0, 2)).astype(bf16)
        for jj in range(jn):
            by_heads[i, jj] = turned[jj * own_heads : (jj + 1) * own_heads]
        heads_in[i, j] = by_heads[i, j]
    for jj in range(1, jn):
        peer = lax.rem(j + jj, jn)
        for i in range(2):
            send("heads", by_heads.at[i, peer], heads_in.at[i, j], sem_heads.at[0], at(0, 0, jj))
    for copy in weights_on_way:
        copy.start()
    relay(1, slice(0, 2))
    share(0)
    relay(0, slice(0, 1))
    relay(1, slice(2, gn))

    def flatten(i):
        for b in range(cn):
            for q in range(xn):
                piece = jnp.concatenate(
                    [rows[s, i, b, q].astype(f32) for s in range(sources)], axis=0
                )
                flat[i, q, b * seq_len : (b + 1) * seq_len, :] = piece.astype(bf16)

    def own_span(place_x):
        return pl.ds(pl.multiple_of(place_x * cn * seq_len, cn * seq_len), cn * seq_len)

    def from_side(i, which):
        def body(k):
            for source in plans[i][0][k][which]:
                arrived(rows.at[pl.ds(0, jn - 1), i], sem_side.at[source, i])
                for jj in range(1, jn):
                    exchange(i, source * jn + lax.rem(j + jj, jn))

        on_line(body)

    def gather_columns(i):
        arrived(far_rows.at[:, i, pl.ds(0, xn - 1)], sem_cols.at[i])
        cols[i, own_span(x), :] = flat[i, x]
        for xx in range(1, xn):
            other = lax.rem(x + xx, xn)
            pieces = [
                far_rows[s, i, other, b].astype(f32) for b in range(cn) for s in range(sources)
            ]
            cols[i, own_span(other), :] = jnp.concatenate(pieces, axis=0).astype(bf16)
        flat_t[i] = cols[i].T

    def column(i, h, b):
        c = i * own_heads + h
        return jnp.broadcast_to(route_columns[b, :seq_len, c : c + 1], (seq_len, head_dim))

    def turn_routes(b):
        lines = jnp.concatenate([routes[b, c] for c in range(2 * own_heads)], axis=0)
        spare = route_columns.shape[1] - seq_len
        if spare:
            lines = jnp.concatenate([lines, jnp.zeros((2 * own_heads, spare), jnp.int32)], axis=1)
        route_columns[b] = lines.T

    def project(i):
        for h in range(own_heads):
            picked = [jnp.zeros((seq_len, head_dim), f32) for _ in range(cn)]
            for e in range(0, E, 2):
                p = h * E + e
                every = jnp.zeros((cn * seq_len, 2 * head_dim), f32)
                for q in range(xn):
                    both = jnp.concatenate([weight[i, p, q], weight[i, p + 1, q]], axis=1)
                    every = every + jnp.dot(flat[i, q], both, preferred_element_type=f32)
                for b in range(cn):
                    own_part = every[b * seq_len : (b + 1) * seq_len]
                    route = column(i, h, x * cn + b)
                    picked[b] = jnp.where(route == e, own_part[:, :head_dim], picked[b])
                    picked[b] = jnp.where(route == e + 1, own_part[:, head_dim:], picked[b])
            for b in range(cn):
                part[b, i, h] = picked[b].astype(bf16)
            if (h + 1) % group == 0:
                heads = pl.ds(h + 1 - group, group)
                for cc in range(1, cn):
                    send(
                        "part",
                        part.at[near(cc), i, heads],
                        part_in.at[cc, i, heads],
                        sem_part.at[i],
                        place_near(cc),
                    )

    def place_near(cc):
        return {"dp": x * cn + near(cc), "head": g, "expert": j}

    query_pos = lax.broadcasted_iota(jnp.int32, (seq_len, seq_len), 0)
    key_pos = lax.broadcasted_iota(jnp.int32, (seq_len, seq_len), 1)
    causal = key_pos <= query_pos

    def joined(i, h):
        return jnp.concatenate([heads_in[i, jj, h] for jj in range(jn)], axis=0)

    def total(i, h):
        whole = part[c, i, h].astype(f32)
        for cc in range(1, cn):
            whole = whole + part_in[cc, i, h].astype(f32)
        return whole.astype(bf16)

    def across_rows(a, b):
        return lax.dot_general(a, b, (((1,), (1,)), ((), ())), preferred_element_type=f32)

    def over_rows(a, b):
        return lax.dot_general(a, b, (((0,), (0,)), ((), ())), preferred_element_type=f32)

    def mask(i, groups_x):
        for xx in groups_x:
            for h in range(own_heads):
                for cc in range(cn):
                    b = lax.rem(x + xx, xn) * cn + cc
                    source = factor[b, i, h].astype(f32)
                    route = column(i, h, b)
                    line = pl.ds(pl.multiple_of(b * seq_len, seq_len), seq_len)
                    for e in range(E):
                        p = h * E + e
                        masked[
                            i, p // 2, line, (p % 2) * head_dim : (p % 2 + 1) * head_dim
                        ] = jnp.where(route == e, source, 0.0).astype(bf16)

    def spread(i):
        for cc in range(1, cn):
            send("factor", factor.at[d, i], factor.at[d, i], sem_factor.at[i, 0], place_near(cc))
        for xx in range(1, xn):
            send("factor", factor.at[d, i], factor.at[d, i], sem_factor.at[i, 1], across(xx, 0))

    def near_factor(i):
        arrived(factor.at[pl.ds(0, cn - 1), i], sem_factor.at[i, 0])

    def hand_over(i):
        arrived(factor.at[pl.ds(0, xn - 1), i], sem_factor.at[i, 1])
        for xx in range(1, xn):
            came = factor.at[lax.rem(x + xx, xn) * cn + c, i]
            for cc in range(1, cn):
                send("factor", came, came, sem_factor.at[i, 2], place_near(cc))

    def far_factor(i):
        arrived(factor.at[pl.ds(0, (xn - 1) * (cn - 1)), i], sem_factor.at[i, 2])

    arrived(heads_in.at[:, pl.ds(0, jn - 1)], sem_heads.at[0])
    for h in range(own_heads):
        query, key = joined(0, h), joined(1, h)
        scores = across_rows(query, key) * scale
        top = jnp.max(jnp.where(causal, scores, -jnp.inf), axis=-1, keepdims=True)
        soft = jnp.where(causal, jnp.exp(scores - top), 0.0)
        prob_keep[h] = soft / jnp.sum(soft, axis=-1, keepdims=True)
    arrived(routes.at[pl.ds(0, dn - 1)], sem_routes.at[0])
    for b in range(dn):
        turn_routes(b)
    for copy in weights_on_way[xn:]:
        copy.wait()
    for p in range(own_heads * E):
        for q in range(xn):
            turned_weight[p // 2, q, (p % 2) * head_dim : (p % 2 + 1) * head_dim, :] = weight[
                0, p, q
            ].T
    relay(0, slice(1, 2))
    from_side(1, slice(0, gn))
    flatten(1)
    for copy in weights_on_way[:xn]:
        copy.wait()
    project(1)
    relay(0, slice(2, gn))
    arrived(part_in.at[pl.ds(0, cn - 1), 1], sem_part.at[1])
    for h in range(own_heads):
        upstream_keep[h] = total(1, h)
        factor[d, 0, h] = over_rows(prob_keep[h].astype(bf16), upstream_keep[h]).astype(bf16)
    spread(0)
    near_factor(0)
    mask(0, range(0, 1))
    couples = own_heads * E // 2
    step = min(width, 256)
    for q in range(xn):
        for n in range(0, width, step):
            added = jnp.zeros((cn * seq_len, step), f32)
            for m in range(couples):
                added = added + jnp.dot(
                    masked[0, m, own_span(x), :],
                    turned_weight[m, q, :, n : n + step],
                    preferred_element_type=f32,
                )
            for b in range(cn):
                for r in range(sources):
                    first = b * seq_len + r * tok_rows
                    term[r % jn, r // jn, b, q, :, n : n + step] = added[
                        first : first + tok_rows
                    ].astype(bf16)
    def turns(k):
        return [0] + sorted(range(1, gn), key=lambda t: -abs(t - k))

    def send_halves(k):
        for target in turns(k):
            for jj in range(1, jn):
                send(
                    "half",
                    term.at[lax.rem(j + jj, jn), target],
                    term_side.at[jj, target],
                    sem_half.at[target],
                    at(0, 0, jj),
                )

    on_line(send_halves)

    def join_halves(which, k):
        for target in turns(k)[which]:
            arrived(term_side.at[pl.ds(0, jn - 1), target], sem_half.at[target])
            whole = term[j, target].astype(f32)
            for jj in range(1, jn):
                whole = whole + term_side[jj, target].astype(f32)
            term_sum[target] = whole.astype(bf16)
            for cc in range(cn):
                if cc == 0 and target == k:
                    term_in[k * cn + c] = term_sum[k, c]
                else:
                    send(
                        "term",
                        term_sum.at[target, near(cc)],
                        term_in.at[g * cn + c],
                        sem_final.at[0],
                        place(cc, target),
                    )

    from_side(0, slice(0, gn))
    flatten(0)
    project(0)
    arrived(part_in.at[pl.ds(0, cn - 1), 0], sem_part.at[0])
    for h in range(own_heads):
        value, upstream, probs = total(0, h), upstream_keep[h], prob_keep[h]
        output = jnp.dot(probs.astype(bf16), value, preferred_element_type=f32).astype(bf16)
        factor[d, 1, h] = output
        delta = jnp.sum(output.astype(f32) * upstream.astype(f32), axis=-1, keepdims=True)
        score_keep[h] = (probs * (across_rows(upstream, value) - delta)).astype(bf16)
    spread(1)
    on_line(functools.partial(join_halves, slice(0, 1)))
    for h in range(own_heads):
        query, key, score = joined(0, h), joined(1, h), score_keep[h]
        query_grad = (jnp.dot(score, key, preferred_element_type=f32) * scale).astype(bf16)
        key_grad = (over_rows(score, query) * scale).astype(bf16)
        for jj in range(jn):
            back[jj, 0, h] = query_grad[jj * query_rows : (jj + 1) * query_rows]
            back[jj, 1, h] = key_grad[jj * query_rows : (jj + 1) * query_rows]
    for jj in range(1, jn):
        send("back", back.at[lax.rem(j + jj, jn)], back_in.at[j], sem_back.at[0], at(0, 0, jj))

    def gradients(i, out):
        for m in range(couples):
            whole = jnp.dot(flat_t[i], masked[i, m], preferred_element_type=f32)
            out[2 * m] = whole[:, :head_dim].astype(bf16)
            out[2 * m + 1] = whole[:, head_dim:].astype(bf16)


    gather_columns(1)
    hand_over(0)
    on_line(functools.partial(join_halves, slice(1, 2)))
    far_factor(0)
    mask(0, range(1, xn))
    near_factor(1)
    mask(1, range(0, 1))
    on_line(functools.partial(join_halves, slice(2, gn - 1)))
    gather_columns(0)
    hand_over(1)
    gradients(0, vg_out)
    on_line(functools.partial(join_halves, slice(gn - 1, gn)))
    far_factor(1)
    mask(1, range(1, xn))
    gradients(1, og_out)

    back_in[j] = back[j]
    arrived(back_in.at[pl.ds(0, jn - 1)], sem_back.at[0])
    for jj in range(jn):
        qg_out[jj] = back_in[jj, 0]
        kg_out[jj] = back_in[jj, 1]
    all_terms = term_in.at[pl.ds(0, len(others))]
    arrived(all_terms, sem_final.at[0])
    for b in range(cn):
        for q in range(xn):
            total_rows = term_in[b, q].astype(f32)
            for s in range(1, gn):
                total_rows = total_rows + term_in[s * cn + b, q].astype(f32)
            n = (q * cn + b) * width
            tok_out[:, n : n + width] = total_rows.astype(bf16)
    left("term", all_terms)

    def left_line(k):
        for i, kind in enumerate(("tok", "cot")):
            left(kind, term_in.at[pl.ds(0, cn - 1 + cn * len(plans[i][1][k]))])
        count = sum(len(plan[2][k]) for plan in plans)
        if count:
            left("onward", rows.at[pl.ds(0, count), 0])

    on_line(left_line)
    left("routes", routes.at[pl.ds(0, dn - 1)])
    left("side", rows.at[pl.ds(0, gn * (jn - 1))])
    left("heads", heads_in.at[:, pl.ds(0, jn - 1)])
    left("part", part_in.at[pl.ds(0, cn - 1)])
    left("cols", far_rows.at[:, :, pl.ds(0, xn - 1)])
    left("factor", factor.at[pl.ds(0, dn - 1)])
    left("half", term_side.at[pl.ds(0, jn - 1)])
    left("back", back_in.at[pl.ds(0, jn - 1)])


def finish_kernel(
    tok_in, qg_in, kg_in, vg_in, og_in, tok_out, qg_out, kg_out, vg_out, og_out, turned, sems
):
    pieces = E
    size = vg_in.shape[0] // pieces
    whole = [
        pltpu.make_async_copy(source, out, sems.at[i])
        for i, (source, out) in enumerate(((vg_in, vg_out), (og_in, og_out), (tok_in, tok_out)))
    ]
    for i, (source, out) in enumerate(((vg_in, vg_out), (og_in, og_out))):
        for n in range(pieces):
            part = pl.ds(n * size, size)
            pltpu.make_async_copy(source.at[part], out.at[part], sems.at[i]).start()
    whole[2].start()
    for i, (source, out) in enumerate(((qg_in, qg_out), (kg_in, kg_out))):
        turned[i] = jnp.transpose(source[...].astype(jnp.float32), (1, 0, 2)).astype(out.dtype)
        whole.append(pltpu.make_async_copy(turned.at[i], out, sems.at[3 + i]))
        whole[3 + i].start()
    for copy in whole:
        copy.wait()


def fused(
    tokens,
    cotangent,
    queries,
    key_vectors,
    value_routes,
    output_routes,
    value_experts,
    output_experts,
):
    dn, gn, jn = lax.axis_size("dp"), lax.axis_size("head"), lax.axis_size("expert")
    _, tok_rows, model_width = tokens.shape
    width = model_width // dn
    _, query_rows, groups, head_dim = queries.shape
    seq_len = value_routes.shape[2]
    pairs_dev = value_experts.shape[0]
    own_heads = groups // jn
    sources = gn * jn
    xn = dn // NEAR
    bf16 = jnp.bfloat16

    value_lines = value_routes.reshape(groups, 1, seq_len)
    output_lines = output_routes.reshape(groups, 1, seq_len)

    vmem = pl.BlockSpec(memory_space=pltpu.VMEM)
    hbm = pl.BlockSpec(memory_space=pl.ANY)
    dma = pltpu.SemaphoreType.DMA
    head_block = (jn, own_heads, query_rows, head_dim)
    grad_shape = jax.ShapeDtypeStruct((pairs_dev, width, head_dim), bf16)
    tok_grads, query_grads, key_grads, value_grads, output_grads = pl.pallas_call(
        functools.partial(
            fused_kernel, (dn, gn, jn, own_heads, query_rows, tok_rows, width, head_dim)
        ),
        name="fused",
        out_shape=(
            pltpu.VMEM((tok_rows, model_width), bf16),
            pltpu.VMEM(head_block, bf16),
            pltpu.VMEM(head_block, bf16),
            pltpu.VMEM(grad_shape.shape, bf16),
            pltpu.VMEM(grad_shape.shape, bf16),
        ),
        in_specs=[hbm] * 8,
        out_specs=(vmem,) * 5,
        scratch_shapes=[
            pltpu.VMEM((sources, 2, NEAR, xn, tok_rows, width), bf16),
            pltpu.VMEM((sources, 2, xn, NEAR, tok_rows, width), bf16),
            pltpu.VMEM((2, xn, NEAR * seq_len, width), bf16),
            pltpu.VMEM((2, dn * seq_len, width), bf16),
            pltpu.VMEM((2, width, dn * seq_len), bf16),
            pltpu.VMEM((2, query_rows, groups, head_dim), bf16),
            pltpu.VMEM((2, jn, own_heads, query_rows, head_dim), bf16),
            pltpu.VMEM((dn, 2 * own_heads, 1, seq_len), jnp.int32),
            pltpu.VMEM((dn, -(-seq_len // 128) * 128, 2 * own_heads), jnp.int32),
            pltpu.VMEM((2, pairs_dev, xn, width, head_dim), bf16),
            pltpu.VMEM((pairs_dev // 2, xn, 2 * head_dim, width), bf16),
            pltpu.VMEM((2, jn, own_heads, query_rows, head_dim), bf16),
            pltpu.VMEM((NEAR, 2, own_heads, seq_len, head_dim), bf16),
            pltpu.VMEM((NEAR, 2, own_heads, seq_len, head_dim), bf16),
            pltpu.VMEM((dn, 2, own_heads, seq_len, head_dim), bf16),
            pltpu.VMEM((2, pairs_dev // 2, dn * seq_len, 2 * head_dim), bf16),
            pltpu.VMEM((own_heads, seq_len, seq_len), bf16),
            pltpu.VMEM((own_heads, seq_len, seq_len), jnp.float32),
            pltpu.VMEM((own_heads, seq_len, head_dim), bf16),
            pltpu.VMEM((jn, 2, own_heads, query_rows, head_dim), bf16),
            pltpu.VMEM((jn, 2, own_heads, query_rows, head_dim), bf16),
            pltpu.VMEM((jn, gn, NEAR, xn, tok_rows, width), bf16),
            pltpu.VMEM((jn, gn, NEAR, xn, tok_rows, width), bf16),
            pltpu.VMEM((gn, NEAR, xn, tok_rows, width), bf16),
            pltpu.VMEM((gn * NEAR, xn, tok_rows, width), bf16),
            pltpu.VMEM((2, tok_rows, model_width), bf16),
            dma((2, xn)),
            dma((6 + 2 * xn,)),
            dma((len(KINDS),)),
            dma((gn, 2)),
            dma((gn, 2)),
            dma((1,)),
            dma((1,)),
            dma((2,)),
            dma((2, 3)),
            dma((2,)),
            dma((1,)),
            dma((gn,)),
            dma((1,)),
        ],
        compiler_params=pltpu.CompilerParams(
            collective_id=0, has_side_effects=True, vmem_limit_bytes=48 * 1024 * 1024
        ),
    )(
        *(
            pltpu.with_memory_space_constraint(x, pltpu.HBM)
            for x in (
                tokens[0],
                cotangent[0],
                queries[0],
                key_vectors[0],
                value_lines,
                output_lines,
            )
        ),
        value_experts,
        output_experts,
    )

    by_head = (groups, query_rows, head_dim)
    row_shape = jax.ShapeDtypeStruct((query_rows, groups, head_dim), bf16)
    tok_grads, query_grads, key_grads, value_grads, output_grads = pl.pallas_call(
        finish_kernel,
        name="finish",
        out_shape=(
            jax.ShapeDtypeStruct((tok_rows, model_width), bf16),
            row_shape,
            row_shape,
            grad_shape,
            grad_shape,
        ),
        in_specs=[vmem] * 5,
        out_specs=(hbm,) * 5,
        scratch_shapes=[
            pltpu.VMEM((2, query_rows, groups, head_dim), bf16),
            dma((5,)),
        ],
        compiler_params=pltpu.CompilerParams(vmem_limit_bytes=8 * 1024 * 1024),
    )(
        tok_grads,
        query_grads.reshape(by_head),
        key_grads.reshape(by_head),
        value_grads,
        output_grads,
    )
    return tok_grads[None], query_grads[None], key_grads[None], value_grads, output_grads


def chosen(*args):
    groups, pairs_dev = args[2].shape[2], args[6].shape[0]
    dp_count, expert_count = lax.axis_size("dp"), lax.axis_size("expert")
    whole_heads = groups % expert_count == 0 and pairs_dev == groups // expert_count * E
    small = args[4].shape[2] <= 128
    if whole_heads and small and expert_count > 1 and dp_count % NEAR == 0 and dp_count > NEAR and args[0].shape[2] % (dp_count * 256) == 0:
        return fused(*args)
    return local(*args)


def solution(mesh):
    return jax.shard_map(
        chosen,
        mesh=mesh,
        in_specs=(
            P("dp", ("head", "expert"), None),
            P("dp", ("head", "expert"), None),
            P("dp", "expert", "head", None),
            P("dp", "expert", "head", None),
            P("dp", "head", None, None),
            P("dp", "head", None, None),
            P(("head", "expert"), None, None),
            P(("head", "expert"), None, None),
        ),
        out_specs=(
            P("dp", ("head", "expert"), None),
            P("dp", "expert", "head", None),
            P("dp", "expert", "head", None),
            P(("head", "expert"), "dp", None),
            P(("head", "expert"), "dp", None),
        ),
        check_vma=False,
    )
```

```python
import functools

import jax
import jax.numpy as jnp
from jax import lax
from jax.experimental import pallas as pl
from jax.experimental.pallas import tpu as pltpu
from jax.sharding import PartitionSpec as P

E = 4
CAP = 3


def slot_rank(routes):
    places = jnp.arange(routes.shape[-1], dtype=jnp.int32)
    same = routes[..., :, None] == routes[..., None, :]
    return jnp.sum(jnp.logical_and(same, places[None, :] < places[:, None]).astype(jnp.int32), axis=-1)


def slot_table(routes):
    rank_of = slot_rank(routes)
    expert_hit = routes[..., None, None, :] == jnp.arange(E, dtype=jnp.int32)[:, None, None]
    place_hit = rank_of[..., None, None, :] == jnp.arange(CAP, dtype=jnp.int32)[:, None]
    return jnp.logical_and(expert_hit, place_hit).astype(jnp.bfloat16)


def local(
    tokens,
    cotangent,
    queries,
    key_vectors,
    value_routes,
    output_routes,
    value_experts,
    output_experts,
):
    head_count = lax.axis_size("head")
    expert_count = lax.axis_size("expert")
    sources = head_count * expert_count
    expert_index = lax.axis_index("expert")
    tok_rows = tokens.shape[1]
    model_width = tokens.shape[2]
    query_rows = queries.shape[1]
    groups = queries.shape[2]
    head_dim = queries.shape[3]
    seq_len = value_routes.shape[2]
    pairs_dev = value_experts.shape[0]
    slot_count = sources * CAP
    score_scale = head_dim ** (-0.5)
    value_local = value_routes[0, :, :, 0]
    output_local = output_routes[0, :, :, 0]

    def own_block(route_part):
        shaped = route_part.reshape(groups, head_count, expert_count, tok_rows)
        return lax.dynamic_index_in_dim(shaped, expert_index, 2, keepdims=False)

    own_pair = jnp.stack([own_block(value_local), own_block(output_local)])
    own_routes = lax.all_to_all(own_pair, "head", split_axis=2, concat_axis=1, tiled=True).reshape(
        2, groups * head_count, tok_rows
    )
    value_table = slot_table(own_routes[0]).reshape(
        head_count, expert_count, pairs_dev, CAP, tok_rows
    )

    def pair_rows(route_part, gathered):
        slot_map = slot_table(route_part.reshape(groups, sources, tok_rows))
        slot_map = jnp.moveaxis(slot_map, 2, 1).reshape(groups * E, sources, CAP, tok_rows)
        slot_map = lax.dynamic_slice_in_dim(slot_map, expert_index * pairs_dev, pairs_dev, 0)
        picked = jnp.einsum(
            "psmt,stw->psmw",
            slot_map,
            gathered.reshape(sources, tok_rows, model_width),
            preferred_element_type=jnp.float32,
        )
        return picked.astype(jnp.bfloat16).reshape(pairs_dev, slot_count, model_width)

    whole_tokens, whole_cotangent = (
        lax.all_gather(tokens[0], ("head", "expert"), axis=0, tiled=True),
        lax.all_gather(cotangent[0], ("head", "expert"), axis=0, tiled=True),
    )
    token_slots = pair_rows(value_local, whole_tokens)
    cotangent_slots = pair_rows(output_local, whole_cotangent)
    value_slots = jnp.einsum(
        "prw,pwk->prk", token_slots, value_experts, preferred_element_type=jnp.float32
    ).astype(jnp.bfloat16)
    upstream_slots = jnp.einsum(
        "prw,pwk->prk", cotangent_slots, output_experts, preferred_element_type=jnp.float32
    ).astype(jnp.bfloat16)
    query_start = expert_index * query_rows
    group_values, group_upstream, all_keys = (
        lax.all_gather(value_slots, "expert", axis=0, tiled=True),
        lax.all_gather(upstream_slots, "expert", axis=0, tiled=True),
        lax.all_gather(key_vectors[0], "expert", axis=0, tiled=True),
    )
    token_source = jnp.arange(seq_len, dtype=jnp.int32) // tok_rows
    head_base = jnp.arange(groups, dtype=jnp.int32)[:, None] * E
    value_rank = slot_rank(value_local.reshape(groups, sources, tok_rows)).reshape(groups, seq_len)
    value_index = (head_base + value_local) * slot_count + token_source * CAP + value_rank
    value_rows = group_values.reshape(-1, head_dim)[value_index]
    output_rank = slot_rank(output_local.reshape(groups, sources, tok_rows)).reshape(
        groups, seq_len
    )
    block_routes = lax.dynamic_slice_in_dim(output_local, query_start, query_rows, 1)
    block_rank = lax.dynamic_slice_in_dim(output_rank, query_start, query_rows, 1)
    block_source = lax.dynamic_slice_in_dim(token_source, query_start, query_rows, 0)
    upstream_index = (head_base + block_routes) * slot_count + block_source * CAP + block_rank
    upstream_rows = group_upstream.reshape(-1, head_dim)[upstream_index]
    query_own = queries[0]
    scores = (
        jnp.einsum("ihc,jhc->hij", query_own, all_keys, preferred_element_type=jnp.float32)
        * score_scale
    )
    query_pos = query_start + jnp.arange(query_rows, dtype=jnp.int32)
    causal = jnp.arange(seq_len, dtype=jnp.int32)[None, :] <= query_pos[:, None]
    row_top = jnp.max(jnp.where(causal, scores, -jnp.inf), axis=-1, keepdims=True)
    weights = jnp.where(causal, jnp.exp(scores - row_top), 0.0)
    probs_full = weights / jnp.sum(weights, axis=-1, keepdims=True)
    prob_half = probs_full.astype(jnp.bfloat16)
    outputs = jnp.einsum(
        "hij,hjc->hic", prob_half, value_rows, preferred_element_type=jnp.float32
    ).astype(jnp.bfloat16)
    row_delta = jnp.sum(outputs.astype(jnp.float32) * upstream_rows.astype(jnp.float32), axis=-1)
    prob_grads = jnp.einsum(
        "hic,hjc->hij", upstream_rows, value_rows, preferred_element_type=jnp.float32
    )
    score_grads = (probs_full * (prob_grads - row_delta[:, :, None])).astype(jnp.bfloat16)
    query_grads = (
        jnp.einsum("hij,jhc->ihc", score_grads, all_keys, preferred_element_type=jnp.float32)
        * score_scale
    ).astype(jnp.bfloat16)
    key_part = (
        jnp.einsum("hij,ihc->jhc", score_grads, query_own, preferred_element_type=jnp.float32)
        * score_scale
    )
    value_part = jnp.einsum(
        "hij,hic->jhc", prob_half, upstream_rows, preferred_element_type=jnp.float32
    )
    key_sum, value_sum = (
        lax.psum_scatter(key_part, "expert", scatter_dimension=0, tiled=True),
        lax.psum_scatter(value_part, "expert", scatter_dimension=0, tiled=True),
    )
    value_half = value_sum.astype(jnp.bfloat16)
    block_value_routes = lax.dynamic_slice_in_dim(value_local, query_start, query_rows, 1).reshape(
        groups, head_count, tok_rows
    )
    value_place = slot_table(block_value_routes)
    output_place = slot_table(block_routes.reshape(groups, head_count, tok_rows))
    value_send = jnp.einsum(
        "hsemt,sthc->hesmc",
        value_place,
        value_half.reshape(head_count, tok_rows, groups, head_dim),
        preferred_element_type=jnp.float32,
    )
    value_send = value_send.astype(jnp.bfloat16).reshape(groups * E, head_count * CAP, head_dim)
    output_send = jnp.einsum(
        "hsemt,hstc->hesmc",
        output_place,
        outputs.reshape(groups, head_count, tok_rows, head_dim),
        preferred_element_type=jnp.float32,
    )
    output_send = output_send.astype(jnp.bfloat16).reshape(groups * E, head_count * CAP, head_dim)
    output_slots, grad_slots = (
        lax.all_to_all(output_send, "expert", split_axis=0, concat_axis=1, tiled=True),
        lax.all_to_all(value_send, "expert", split_axis=0, concat_axis=1, tiled=True),
    )
    value_term = jnp.einsum(
        "prw,prk->pwk", token_slots, grad_slots, preferred_element_type=jnp.float32
    )
    output_term = jnp.einsum(
        "prw,prk->pwk", cotangent_slots, output_slots, preferred_element_type=jnp.float32
    )
    value_grads, output_grads = (
        lax.psum_scatter(
            value_term.astype(jnp.bfloat16), "dp", scatter_dimension=1, tiled=True
        ).astype(jnp.float32),
        lax.psum_scatter(
            output_term.astype(jnp.bfloat16), "dp", scatter_dimension=1, tiled=True
        ).astype(jnp.float32),
    )
    token_terms = jnp.einsum(
        "prk,pwk->prw", grad_slots, value_experts, preferred_element_type=jnp.float32
    ).astype(jnp.bfloat16)
    returned = lax.all_to_all(
        token_terms.reshape(pairs_dev, sources, CAP, model_width),
        ("head", "expert"),
        split_axis=1,
        concat_axis=0,
        tiled=True,
    )
    returned = returned.reshape(head_count, expert_count, pairs_dev, CAP, model_width)
    token_grads = jnp.einsum(
        "gjpmt,gjpmw->tw", value_table, returned, preferred_element_type=jnp.float32
    )
    return (
        token_grads.astype(jnp.bfloat16)[None],
        query_grads[None],
        key_sum.astype(jnp.bfloat16)[None],
        value_grads.astype(jnp.bfloat16),
        output_grads.astype(jnp.bfloat16),
    )


def line_plan(gn):
    order = [sorted(range(gn), key=lambda t: (abs(t - k), t)) for k in range(gn)]
    plain = (order, [row[1:] for row in order], [{} for _ in range(gn)])
    if gn != 4:
        return plain, plain
    passed = (
        [[0, 1, 3, 2], [1, 2, 0, 3], [2, 1, 3, 0], [3, 2, 0, 1]],
        [[1, 2, 3], [2, 0], [1, 3], [2, 1, 0]],
        [{}, {2: 0}, {1: 3}, {}],
    )
    return plain, passed


KINDS = (
    "tok",
    "cot",
    "onward",
    "routes",
    "side",
    "heads",
    "part",
    "factor",
    "cols",
    "half",
    "term",
    "back",
)
NEAR = 2


def fused_kernel(
    sizes,
    tok,
    cot,
    q_in,
    k_in,
    value_routes_in,
    output_routes_in,
    value_hbm,
    output_hbm,
    tok_out,
    qg_out,
    kg_out,
    vg_out,
    og_out,
    rows,
    far_rows,
    flat,
    cols,
    flat_t,
    heads_raw,
    by_heads,
    routes,
    route_columns,
    weight,
    turned_weight,
    heads_in,
    part,
    part_in,
    factor,
    masked,
    score_keep,
    prob_keep,
    upstream_keep,
    back,
    back_in,
    term,
    term_side,
    term_sum,
    term_in,
    own_rows,
    sem_weight,
    sem_own,
    sem_sent,
    sem_block,
    sem_side,
    sem_routes,
    sem_heads,
    sem_part,
    sem_factor,
    sem_cols,
    sem_back,
    sem_half,
    sem_final,
):
    dn, gn, jn, own_heads, query_rows, tok_rows, width, head_dim = sizes
    sources = gn * jn
    cn, xn = NEAR, dn // NEAR
    seq_len = sources * tok_rows
    scale = head_dim ** (-0.5)
    group = own_heads // 2 if own_heads % 2 == 0 else own_heads
    d, g, j = lax.axis_index("dp"), lax.axis_index("head"), lax.axis_index("expert")
    block = g * jn + j
    x, c = d // cn, lax.rem(d, cn)
    f32, bf16 = jnp.float32, jnp.bfloat16

    def at(dd, gg, jj):
        return {"dp": lax.rem(d + dd, dn), "head": lax.rem(g + gg, gn), "expert": lax.rem(j + jj, jn)}

    def near(cc):
        return lax.rem(c + cc, cn)

    others = [(cc, gg) for gg in range(gn) for cc in range(cn) if (cc, gg) != (0, 0)]
    afar = [(xx, cc) for xx in range(1, xn) for cc in range(cn)]

    def across(xx, cc):
        return {"dp": lax.rem(x + xx, xn) * cn + near(cc), "head": g, "expert": j}

    def remote(kind, src, dst, recv_sem, where):
        return pltpu.make_async_remote_copy(
            src_ref=src,
            dst_ref=dst,
            send_sem=sem_sent.at[KINDS.index(kind)],
            recv_sem=recv_sem,
            device_id=where,
            device_id_type=pl.DeviceIdType.MESH,
        )

    def send(*args):
        remote(*args).start()

    def arrived(region, recv_sem):
        remote("tok", region, region, recv_sem, at(0, 0, 0)).wait_recv()

    def left(kind, region):
        remote(kind, region, region, sem_final.at[0], at(0, 0, 0)).wait_send()

    def columns(index):
        return pl.ds(pl.multiple_of(index * width, 128), width)

    weights_on_way = [
        pltpu.make_async_copy(
            hbm.at[:, columns(q * cn + c), :], weight.at[i, :, q], sem_weight.at[i, q]
        )
        for i, hbm in ((1, output_hbm), (0, value_hbm))
        for q in range(xn)
    ]
    own = [
        pltpu.make_async_copy(tok, own_rows.at[0], sem_own.at[0]),
        pltpu.make_async_copy(cot, own_rows.at[1], sem_own.at[1]),
        pltpu.make_async_copy(
            value_routes_in.at[pl.ds(j * own_heads, own_heads)],
            routes.at[d, pl.ds(0, own_heads)],
            sem_own.at[2],
        ),
        pltpu.make_async_copy(
            output_routes_in.at[pl.ds(j * own_heads, own_heads)],
            routes.at[d, pl.ds(own_heads, own_heads)],
            sem_own.at[3],
        ),
        pltpu.make_async_copy(q_in, heads_raw.at[0], sem_own.at[4]),
        pltpu.make_async_copy(k_in, heads_raw.at[1], sem_own.at[5]),
    ]
    own += [
        pltpu.make_async_copy(
            source.at[:, columns(q * cn + c)], rows.at[block, i, c, q], sem_own.at[6 + i * xn + q]
        )
        for i, source in enumerate((tok, cot))
        for q in range(xn)
    ]
    for copy in own:
        copy.start()

    barrier = pltpu.get_barrier_semaphore()

    def greet(where):
        pl.semaphore_signal(
            barrier, inc=1, device_id=where, device_id_type=pl.DeviceIdType.MESH
        )

    for cc, gg in others:
        greet({"dp": x * cn + near(cc), "head": lax.rem(g + gg, gn), "expert": j})
    for xx, cc in afar:
        greet(across(xx, cc))
    for jj in range(1, jn):
        greet(at(0, 0, jj))
    for copy in own[:2]:
        copy.wait()
    pl.semaphore_wait(barrier, len(others) + len(afar) + jn - 1)

    def on_line(body):
        for k in range(gn):
            pl.when(g == k)(functools.partial(body, k))

    plans = line_plan(gn)

    def place(cc, target):
        return {"dp": x * cn + near(cc), "head": jnp.int32(target), "expert": j}

    def share(i):
        def body(k):
            for target in [k] + plans[i][1][k]:
                for cc in range(cn):
                    for q in range(xn):
                        if cc or target != k:
                            send(
                                ("tok", "cot")[i],
                                own_rows.at[i, :, columns(q * cn + near(cc))],
                                rows.at[block, i, c, q],
                                sem_block.at[g, i],
                                place(cc, target),
                            )

        on_line(body)

    def exchange(i, source):
        for xx in range(1, xn):
            send(
                "cols",
                rows.at[source, i, :, lax.rem(x + xx, xn)],
                far_rows.at[source, i, x],
                sem_cols.at[i],
                across(xx, 0),
            )

    def relay(i, which):
        def body(k):
            for source in plans[i][0][k][which]:
                count = cn - 1 if source == k else cn
                here = rows.at[source * jn + j, i]
                if count:
                    arrived(here.at[pl.ds(0, count)], sem_block.at[source, i])
                onward = plans[i][2][k]
                if source in onward:
                    send("onward", here, here, sem_block.at[source, i], place(0, onward[source]))
                for jj in range(1, jn):
                    send("side", here, here, sem_side.at[source, i], at(0, 0, jj))
                exchange(i, source * jn + j)

        on_line(body)

    share(1)
    for copy in own[2:]:
        copy.wait()
    for dd in range(1, dn):
        send("routes", routes.at[d], routes.at[d], sem_routes.at[0], at(dd, 0, 0))
    for i in range(2):
        turned = jnp.transpose(heads_raw[i].astype(f32), (1, 0, 2)).astype(bf16)
        for jj in range(jn):
            by_heads[i, jj] = turned[jj * own_heads : (jj + 1) * own_heads]
        heads_in[i, j] = by_heads[i, j]
    for jj in range(1, jn):
        peer = lax.rem(j + jj, jn)
        for i in range(2):
            send("heads", by_heads.at[i, peer], heads_in.at[i, j], sem_heads.at[0], at(0, 0, jj))
    for copy in weights_on_way:
        copy.start()
    relay(1, slice(0, 2))
    share(0)
    relay(0, slice(0, 1))
    relay(1, slice(2, gn))

    def flatten(i):
        for b in range(cn):
            for q in range(xn):
                piece = jnp.concatenate(
                    [rows[s, i, b, q].astype(f32) for s in range(sources)], axis=0
                )
                flat[i, q, b * seq_len : (b + 1) * seq_len, :] = piece.astype(bf16)

    def own_span(place_x):
        return pl.ds(pl.multiple_of(place_x * cn * seq_len, cn * seq_len), cn * seq_len)

    def from_side(i, which):
        def body(k):
            for source in plans[i][0][k][which]:
                arrived(rows.at[pl.ds(0, jn - 1), i], sem_side.at[source, i])
                for jj in range(1, jn):
                    exchange(i, source * jn + lax.rem(j + jj, jn))

        on_line(body)

    def gather_columns(i):
        arrived(far_rows.at[:, i, pl.ds(0, xn - 1)], sem_cols.at[i])
        cols[i, own_span(x), :] = flat[i, x]
        for xx in range(1, xn):
            other = lax.rem(x + xx, xn)
            pieces = [
                far_rows[s, i, other, b].astype(f32) for b in range(cn) for s in range(sources)
            ]
            cols[i, own_span(other), :] = jnp.concatenate(pieces, axis=0).astype(bf16)
        flat_t[i] = cols[i].T

    def column(i, h, b):
        c = i * own_heads + h
        return jnp.broadcast_to(route_columns[b, :seq_len, c : c + 1], (seq_len, head_dim))

    def turn_routes(b):
        lines = jnp.concatenate([routes[b, c] for c in range(2 * own_heads)], axis=0)
        spare = route_columns.shape[1] - seq_len
        if spare:
            lines = jnp.concatenate([lines, jnp.zeros((2 * own_heads, spare), jnp.int32)], axis=1)
        route_columns[b] = lines.T

    def project(i):
        for h in range(own_heads):
            picked = [jnp.zeros((seq_len, head_dim), f32) for _ in range(cn)]
            for e in range(0, E, 2):
                p = h * E + e
                every = jnp.zeros((cn * seq_len, 2 * head_dim), f32)
                for q in range(xn):
                    both = jnp.concatenate([weight[i, p, q], weight[i, p + 1, q]], axis=1)
                    every = every + jnp.dot(flat[i, q], both, preferred_element_type=f32)
                for b in range(cn):
                    own_part = every[b * seq_len : (b + 1) * seq_len]
                    route = column(i, h, x * cn + b)
                    picked[b] = jnp.where(route == e, own_part[:, :head_dim], picked[b])
                    picked[b] = jnp.where(route == e + 1, own_part[:, head_dim:], picked[b])
            for b in range(cn):
                part[b, i, h] = picked[b].astype(bf16)
            if (h + 1) % group == 0:
                heads = pl.ds(h + 1 - group, group)
                for cc in range(1, cn):
                    send(
                        "part",
                        part.at[near(cc), i, heads],
                        part_in.at[cc, i, heads],
                        sem_part.at[i],
                        place_near(cc),
                    )

    def place_near(cc):
        return {"dp": x * cn + near(cc), "head": g, "expert": j}

    query_pos = lax.broadcasted_iota(jnp.int32, (seq_len, seq_len), 0)
    key_pos = lax.broadcasted_iota(jnp.int32, (seq_len, seq_len), 1)
    causal = key_pos <= query_pos

    def joined(i, h):
        return jnp.concatenate([heads_in[i, jj, h] for jj in range(jn)], axis=0)

    def total(i, h):
        whole = part[c, i, h].astype(f32)
        for cc in range(1, cn):
            whole = whole + part_in[cc, i, h].astype(f32)
        return whole.astype(bf16)

    def across_rows(a, b):
        return lax.dot_general(a, b, (((1,), (1,)), ((), ())), preferred_element_type=f32)

    def over_rows(a, b):
        return lax.dot_general(a, b, (((0,), (0,)), ((), ())), preferred_element_type=f32)

    def mask(i, groups_x):
        for xx in groups_x:
            for h in range(own_heads):
                for cc in range(cn):
                    b = lax.rem(x + xx, xn) * cn + cc
                    source = factor[b, i, h].astype(f32)
                    route = column(i, h, b)
                    line = pl.ds(pl.multiple_of(b * seq_len, seq_len), seq_len)
                    for e in range(E):
                        p = h * E + e
                        masked[
                            i, p // 2, line, (p % 2) * head_dim : (p % 2 + 1) * head_dim
                        ] = jnp.where(route == e, source, 0.0).astype(bf16)

    def spread(i):
        for cc in range(1, cn):
            send("factor", factor.at[d, i], factor.at[d, i], sem_factor.at[i, 0], place_near(cc))
        for xx in range(1, xn):
            send("factor", factor.at[d, i], factor.at[d, i], sem_factor.at[i, 1], across(xx, 0))

    def near_factor(i):
        arrived(factor.at[pl.ds(0, cn - 1), i], sem_factor.at[i, 0])

    def hand_over(i):
        arrived(factor.at[pl.ds(0, xn - 1), i], sem_factor.at[i, 1])
        for xx in range(1, xn):
            came = factor.at[lax.rem(x + xx, xn) * cn + c, i]
            for cc in range(1, cn):
                send("factor", came, came, sem_factor.at[i, 2], place_near(cc))

    def far_factor(i):
        arrived(factor.at[pl.ds(0, (xn - 1) * (cn - 1)), i], sem_factor.at[i, 2])

    arrived(heads_in.at[:, pl.ds(0, jn - 1)], sem_heads.at[0])
    for h in range(own_heads):
        query, key = joined(0, h), joined(1, h)
        scores = across_rows(query, key) * scale
        top = jnp.max(jnp.where(causal, scores, -jnp.inf), axis=-1, keepdims=True)
        soft = jnp.where(causal, jnp.exp(scores - top), 0.0)
        prob_keep[h] = soft / jnp.sum(soft, axis=-1, keepdims=True)
    arrived(routes.at[pl.ds(0, dn - 1)], sem_routes.at[0])
    for b in range(dn):
        turn_routes(b)
    for copy in weights_on_way[xn:]:
        copy.wait()
    for p in range(own_heads * E):
        for q in range(xn):
            turned_weight[p // 2, q, (p % 2) * head_dim : (p % 2 + 1) * head_dim, :] = weight[
                0, p, q
            ].T
    relay(0, slice(1, 2))
    from_side(1, slice(0, gn))
    flatten(1)
    for copy in weights_on_way[:xn]:
        copy.wait()
    project(1)
    relay(0, slice(2, gn))
    arrived(part_in.at[pl.ds(0, cn - 1), 1], sem_part.at[1])
    for h in range(own_heads):
        upstream_keep[h] = total(1, h)
        factor[d, 0, h] = over_rows(prob_keep[h].astype(bf16), upstream_keep[h]).astype(bf16)
    spread(0)
    near_factor(0)
    mask(0, range(0, 1))
    couples = own_heads * E // 2
    step = min(width, 256)
    for q in range(xn):
        for n in range(0, width, step):
            added = jnp.zeros((cn * seq_len, step), f32)
            for m in range(couples):
                added = added + jnp.dot(
                    masked[0, m, own_span(x), :],
                    turned_weight[m, q, :, n : n + step],
                    preferred_element_type=f32,
                )
            for b in range(cn):
                for r in range(sources):
                    first = b * seq_len + r * tok_rows
                    term[r % jn, r // jn, b, q, :, n : n + step] = added[
                        first : first + tok_rows
                    ].astype(bf16)
    def turns(k):
        return [0] + sorted(range(1, gn), key=lambda t: -abs(t - k))

    def send_halves(k):
        for target in turns(k):
            for jj in range(1, jn):
                send(
                    "half",
                    term.at[lax.rem(j + jj, jn), target],
                    term_side.at[jj, target],
                    sem_half.at[target],
                    at(0, 0, jj),
                )

    on_line(send_halves)

    def join_halves(which, k):
        for target in turns(k)[which]:
            arrived(term_side.at[pl.ds(0, jn - 1), target], sem_half.at[target])
            whole = term[j, target].astype(f32)
            for jj in range(1, jn):
                whole = whole + term_side[jj, target].astype(f32)
            term_sum[target] = whole.astype(bf16)
            for cc in range(cn):
                if cc == 0 and target == k:
                    term_in[k * cn + c] = term_sum[k, c]
                else:
                    send(
                        "term",
                        term_sum.at[target, near(cc)],
                        term_in.at[g * cn + c],
                        sem_final.at[0],
                        place(cc, target),
                    )

    from_side(0, slice(0, gn))
    flatten(0)
    project(0)
    arrived(part_in.at[pl.ds(0, cn - 1), 0], sem_part.at[0])
    for h in range(own_heads):
        value, upstream, probs = total(0, h), upstream_keep[h], prob_keep[h]
        output = jnp.dot(probs.astype(bf16), value, preferred_element_type=f32).astype(bf16)
        factor[d, 1, h] = output
        delta = jnp.sum(output.astype(f32) * upstream.astype(f32), axis=-1, keepdims=True)
        score_keep[h] = (probs * (across_rows(upstream, value) - delta)).astype(bf16)
    spread(1)
    on_line(functools.partial(join_halves, slice(0, 1)))
    for h in range(own_heads):
        query, key, score = joined(0, h), joined(1, h), score_keep[h]
        query_grad = (jnp.dot(score, key, preferred_element_type=f32) * scale).astype(bf16)
        key_grad = (over_rows(score, query) * scale).astype(bf16)
        for jj in range(jn):
            back[jj, 0, h] = query_grad[jj * query_rows : (jj + 1) * query_rows]
            back[jj, 1, h] = key_grad[jj * query_rows : (jj + 1) * query_rows]
    for jj in range(1, jn):
        send("back", back.at[lax.rem(j + jj, jn)], back_in.at[j], sem_back.at[0], at(0, 0, jj))

    def gradients(i, out, some):
        for m in some:
            whole = jnp.dot(flat_t[i], masked[i, m], preferred_element_type=f32)
            out[2 * m] = whole[:, :head_dim].astype(bf16)
            out[2 * m + 1] = whole[:, head_dim:].astype(bf16)


    gather_columns(1)
    hand_over(0)
    on_line(functools.partial(join_halves, slice(1, 2)))
    far_factor(0)
    mask(0, range(1, xn))
    near_factor(1)
    mask(1, range(0, 1))
    on_line(functools.partial(join_halves, slice(2, gn - 1)))
    gather_columns(0)
    hand_over(1)
    gradients(0, vg_out, range(0, couples * 3 // 4))
    on_line(functools.partial(join_halves, slice(gn - 1, gn)))
    gradients(0, vg_out, range(couples * 3 // 4, couples))
    far_factor(1)
    mask(1, range(1, xn))
    gradients(1, og_out, range(couples))

    back_in[j] = back[j]
    arrived(back_in.at[pl.ds(0, jn - 1)], sem_back.at[0])
    for jj in range(jn):
        qg_out[jj] = back_in[jj, 0]
        kg_out[jj] = back_in[jj, 1]
    all_terms = term_in.at[pl.ds(0, len(others))]
    arrived(all_terms, sem_final.at[0])
    for b in range(cn):
        for q in range(xn):
            total_rows = term_in[b, q].astype(f32)
            for s in range(1, gn):
                total_rows = total_rows + term_in[s * cn + b, q].astype(f32)
            n = (q * cn + b) * width
            tok_out[:, n : n + width] = total_rows.astype(bf16)
    left("term", all_terms)

    def left_line(k):
        for i, kind in enumerate(("tok", "cot")):
            left(kind, term_in.at[pl.ds(0, cn - 1 + cn * len(plans[i][1][k]))])
        count = sum(len(plan[2][k]) for plan in plans)
        if count:
            left("onward", rows.at[pl.ds(0, count), 0])

    on_line(left_line)
    left("routes", routes.at[pl.ds(0, dn - 1)])
    left("side", rows.at[pl.ds(0, gn * (jn - 1))])
    left("heads", heads_in.at[:, pl.ds(0, jn - 1)])
    left("part", part_in.at[pl.ds(0, cn - 1)])
    left("cols", far_rows.at[:, :, pl.ds(0, xn - 1)])
    left("factor", factor.at[pl.ds(0, dn - 1)])
    left("half", term_side.at[pl.ds(0, jn - 1)])
    left("back", back_in.at[pl.ds(0, jn - 1)])


def finish_kernel(
    tok_in, qg_in, kg_in, vg_in, og_in, tok_out, qg_out, kg_out, vg_out, og_out, turned, sems
):
    pieces = vg_in.shape[0]
    size = vg_in.shape[0] // pieces
    whole = [
        pltpu.make_async_copy(source, out, sems.at[i])
        for i, (source, out) in enumerate(((vg_in, vg_out), (og_in, og_out), (tok_in, tok_out)))
    ]
    for i, (source, out) in enumerate(((vg_in, vg_out), (og_in, og_out))):
        for n in range(pieces):
            part = pl.ds(n * size, size)
            pltpu.make_async_copy(source.at[part], out.at[part], sems.at[i]).start()
    whole[2].start()
    for i, (source, out) in enumerate(((qg_in, qg_out), (kg_in, kg_out))):
        turned[i] = jnp.transpose(source[...].astype(jnp.float32), (1, 0, 2)).astype(out.dtype)
        whole.append(pltpu.make_async_copy(turned.at[i], out, sems.at[3 + i]))
        whole[3 + i].start()
    for copy in whole:
        copy.wait()


def fused(
    tokens,
    cotangent,
    queries,
    key_vectors,
    value_routes,
    output_routes,
    value_experts,
    output_experts,
):
    dn, gn, jn = lax.axis_size("dp"), lax.axis_size("head"), lax.axis_size("expert")
    _, tok_rows, model_width = tokens.shape
    width = model_width // dn
    _, query_rows, groups, head_dim = queries.shape
    seq_len = value_routes.shape[2]
    pairs_dev = value_experts.shape[0]
    own_heads = groups // jn
    sources = gn * jn
    xn = dn // NEAR
    bf16 = jnp.bfloat16

    value_lines = value_routes.reshape(groups, 1, seq_len)
    output_lines = output_routes.reshape(groups, 1, seq_len)

    vmem = pl.BlockSpec(memory_space=pltpu.VMEM)
    hbm = pl.BlockSpec(memory_space=pl.ANY)
    dma = pltpu.SemaphoreType.DMA
    head_block = (jn, own_heads, query_rows, head_dim)
    grad_shape = jax.ShapeDtypeStruct((pairs_dev, width, head_dim), bf16)
    tok_grads, query_grads, key_grads, value_grads, output_grads = pl.pallas_call(
        functools.partial(
            fused_kernel, (dn, gn, jn, own_heads, query_rows, tok_rows, width, head_dim)
        ),
        name="fused",
        out_shape=(
            pltpu.VMEM((tok_rows, model_width), bf16),
            pltpu.VMEM(head_block, bf16),
            pltpu.VMEM(head_block, bf16),
            pltpu.VMEM(grad_shape.shape, bf16),
            pltpu.VMEM(grad_shape.shape, bf16),
        ),
        in_specs=[hbm] * 8,
        out_specs=(vmem,) * 5,
        scratch_shapes=[
            pltpu.VMEM((sources, 2, NEAR, xn, tok_rows, width), bf16),
            pltpu.VMEM((sources, 2, xn, NEAR, tok_rows, width), bf16),
            pltpu.VMEM((2, xn, NEAR * seq_len, width), bf16),
            pltpu.VMEM((2, dn * seq_len, width), bf16),
            pltpu.VMEM((2, width, dn * seq_len), bf16),
            pltpu.VMEM((2, query_rows, groups, head_dim), bf16),
            pltpu.VMEM((2, jn, own_heads, query_rows, head_dim), bf16),
            pltpu.VMEM((dn, 2 * own_heads, 1, seq_len), jnp.int32),
            pltpu.VMEM((dn, -(-seq_len // 128) * 128, 2 * own_heads), jnp.int32),
            pltpu.VMEM((2, pairs_dev, xn, width, head_dim), bf16),
            pltpu.VMEM((pairs_dev // 2, xn, 2 * head_dim, width), bf16),
            pltpu.VMEM((2, jn, own_heads, query_rows, head_dim), bf16),
            pltpu.VMEM((NEAR, 2, own_heads, seq_len, head_dim), bf16),
            pltpu.VMEM((NEAR, 2, own_heads, seq_len, head_dim), bf16),
            pltpu.VMEM((dn, 2, own_heads, seq_len, head_dim), bf16),
            pltpu.VMEM((2, pairs_dev // 2, dn * seq_len, 2 * head_dim), bf16),
            pltpu.VMEM((own_heads, seq_len, seq_len), bf16),
            pltpu.VMEM((own_heads, seq_len, seq_len), jnp.float32),
            pltpu.VMEM((own_heads, seq_len, head_dim), bf16),
            pltpu.VMEM((jn, 2, own_heads, query_rows, head_dim), bf16),
            pltpu.VMEM((jn, 2, own_heads, query_rows, head_dim), bf16),
            pltpu.VMEM((jn, gn, NEAR, xn, tok_rows, width), bf16),
            pltpu.VMEM((jn, gn, NEAR, xn, tok_rows, width), bf16),
            pltpu.VMEM((gn, NEAR, xn, tok_rows, width), bf16),
            pltpu.VMEM((gn * NEAR, xn, tok_rows, width), bf16),
            pltpu.VMEM((2, tok_rows, model_width), bf16),
            dma((2, xn)),
            dma((6 + 2 * xn,)),
            dma((len(KINDS),)),
            dma((gn, 2)),
            dma((gn, 2)),
            dma((1,)),
            dma((1,)),
            dma((2,)),
            dma((2, 3)),
            dma((2,)),
            dma((1,)),
            dma((gn,)),
            dma((1,)),
        ],
        compiler_params=pltpu.CompilerParams(
            collective_id=0, has_side_effects=True, vmem_limit_bytes=48 * 1024 * 1024
        ),
    )(
        *(
            pltpu.with_memory_space_constraint(x, pltpu.HBM)
            for x in (
                tokens[0],
                cotangent[0],
                queries[0],
                key_vectors[0],
                value_lines,
                output_lines,
            )
        ),
        value_experts,
        output_experts,
    )

    by_head = (groups, query_rows, head_dim)
    row_shape = jax.ShapeDtypeStruct((query_rows, groups, head_dim), bf16)
    tok_grads, query_grads, key_grads, value_grads, output_grads = pl.pallas_call(
        finish_kernel,
        name="finish",
        out_shape=(
            jax.ShapeDtypeStruct((tok_rows, model_width), bf16),
            row_shape,
            row_shape,
            grad_shape,
            grad_shape,
        ),
        in_specs=[vmem] * 5,
        out_specs=(hbm,) * 5,
        scratch_shapes=[
            pltpu.VMEM((2, query_rows, groups, head_dim), bf16),
            dma((5,)),
        ],
        compiler_params=pltpu.CompilerParams(vmem_limit_bytes=8 * 1024 * 1024),
    )(
        tok_grads,
        query_grads.reshape(by_head),
        key_grads.reshape(by_head),
        value_grads,
        output_grads,
    )
    return tok_grads[None], query_grads[None], key_grads[None], value_grads, output_grads


def chosen(*args):
    groups, pairs_dev = args[2].shape[2], args[6].shape[0]
    dp_count, expert_count = lax.axis_size("dp"), lax.axis_size("expert")
    whole_heads = groups % expert_count == 0 and pairs_dev == groups // expert_count * E
    small = args[4].shape[2] <= 128
    if whole_heads and small and expert_count > 1 and dp_count % NEAR == 0 and dp_count > NEAR and args[0].shape[2] % (dp_count * 256) == 0:
        return fused(*args)
    return local(*args)


def solution(mesh):
    return jax.shard_map(
        chosen,
        mesh=mesh,
        in_specs=(
            P("dp", ("head", "expert"), None),
            P("dp", ("head", "expert"), None),
            P("dp", "expert", "head", None),
            P("dp", "expert", "head", None),
            P("dp", "head", None, None),
            P("dp", "head", None, None),
            P(("head", "expert"), None, None),
            P(("head", "expert"), None, None),
        ),
        out_specs=(
            P("dp", ("head", "expert"), None),
            P("dp", "expert", "head", None),
            P("dp", "expert", "head", None),
            P(("head", "expert"), "dp", None),
            P(("head", "expert"), "dp", None),
        ),
        check_vma=False,
    )
```
